32 devices in a mesh: members: 2 (over x), row: 16 (over z, y, core).
Axes of the slice: x: 2, y: 2, z: 4, core: 2. Of those that a mesh axis runs over, the one named last changes fastest.
Arguments:
- node_features: bfloat16 [32768, 512], P(('members', 'row')), parts along dimension 0, may hold values from -18 to 18
- nbr_table: int32 [128, 8], P('row'), may hold values from 0 to 27, as said below
- nbr_count: int32 [128], P('row'), may hold values from 4 to 8
- send_block: int32 [256, 1], P('row'), may hold values from 0 to 7
- w_query: bfloat16 [2, 512, 512], replicated, may hold values from -9 to 9
- w_key: bfloat16 [2, 512, 512], replicated, may hold values from -0.7 to 0.7
- w_value: bfloat16 [2, 512, 512], replicated, may hold values from -0.25 to 0.25
- w_out: bfloat16 [2, 512, 512], replicated, may hold values from -0.25 to 0.25
- w_up: bfloat16 [2, 512, 2048], replicated, may hold values from -0.25 to 0.25
- w_down: bfloat16 [2, 2048, 512], replicated, may hold values from -0.125 to 0.125
- w_virtual: bfloat16 [2, 512, 512], replicated, may hold values from -0.25 to 0.25
- gains: float32 [2, 4, 512], replicated, may hold values from 0.25 to 1.75
Outputs:
- latents_out: bfloat16 [32768, 512], P(('members', 'row')), parts along dimension 0
The draws below stay inside these ranges and needn't reach their ends.
There are 2 independent parts, one for each index of `members`. The reference program is written for one: setup_inputs(seed, part) draws one part's arguments, and reference() takes and returns one part's arrays. A program takes and returns all parts, laid end to end along the dimension named above; an argument that names none is the same for every part. Nothing has to cross between parts.
Inputs may be any that keep to these rules, and one draw needn't show every extreme that they name: `nbr_table`: entry t of a row of block g names a block of device g // 8's table: t below 12 are the device's own blocks with 2 blocks of each neighbour along the node order around them, own block b at t = 2 + b; the others are received slots as in the reference program. The first entry of each row is the block itself. Every live entry names a block that exists.
All inputs are finite; a program needn't handle non-finite values.
Results may differ from the reference program's by a relative error of at most 0.007.
Values may be sent and summed in bfloat16 or wider, within the bound.
A program may use at most 128 MiB of HBM per device.

```python
import math
import jax
import jax.numpy as jnp
from jax import lax

D = 512
FF = 2048
HEADS = 4
BLOCK = 128
NBR = 8
HALO_B = 2
SLOTS = 1
LAYERS = 2
BLK_DEV = 8
NBLK = 128
NODES = 16384
N_ROW = 16


def graph_lists(key):
    devices_count = NBLK // BLK_DEV
    near_count = 2 * HALO_B + BLK_DEV
    counts = jax.random.randint(jax.random.fold_in(key, 11), (NBLK,), NBR // 2, NBR + 1).astype(jnp.int32)
    devices = jnp.arange(devices_count, dtype=jnp.int32)
    ranking = jax.random.randint(jax.random.fold_in(key, 12), (devices_count, devices_count), 0, 1 << 20).astype(jnp.int32)
    ranking = ranking * devices_count + devices[None, :]
    ranking = jnp.where(devices[:, None] == devices[None, :], jnp.int32(1 << 30), ranking)
    order = jnp.argsort(ranking, axis=1, stable=True).astype(jnp.int32)
    most_far = min(devices_count - 1, (NBR // 2 - 1) * BLK_DEV // SLOTS)
    far_live = jax.random.randint(jax.random.fold_in(key, 13), (devices_count,), 1, most_far + 1).astype(jnp.int32)
    per_device = counts.reshape(devices_count, BLK_DEV)
    slot_number = jnp.arange(1, NBR, dtype=jnp.int32)
    live = (slot_number[None, None, :] < per_device[:, :, None]).reshape(devices_count, BLK_DEV * (NBR - 1)).astype(jnp.int32)
    rank = jnp.cumsum(live, axis=1) - 1
    far_position = (live == 1) & (rank < (far_live * SLOTS)[:, None])
    safe_rank = jnp.clip(rank, 0, devices_count * SLOTS - 1)
    peer = jnp.take_along_axis(order, jnp.clip(safe_rank // SLOTS, 0, devices_count - 1), axis=1)
    far_entry = near_count + peer * SLOTS + safe_rank % SLOTS
    lower = jnp.where(devices == 0, HALO_B, 0).astype(jnp.int32)[:, None]
    upper = jnp.where(devices == devices_count - 1, HALO_B + BLK_DEV, near_count).astype(jnp.int32)[:, None]
    random_pick = jax.random.randint(jax.random.fold_in(key, 14), (devices_count, BLK_DEV * (NBR - 1)), 0, 1 << 20).astype(jnp.int32)
    local_entry = lower + random_pick % (upper - lower)
    entries = jnp.where(far_position, far_entry, local_entry).reshape(devices_count, BLK_DEV, NBR - 1)
    own_entry = jnp.broadcast_to((HALO_B + jnp.arange(BLK_DEV, dtype=jnp.int32))[None, :, None], (devices_count, BLK_DEV, 1))
    table = jnp.concatenate((own_entry, entries), axis=2).reshape(NBLK, NBR)
    return (table.astype(jnp.int32), counts)


def draw_nbr_table(key, part):
    return graph_lists(key)[0]


def draw_nbr_count(key, part):
    return graph_lists(key)[1]


def draw_node_features(key, part):
    first, second = jax.random.split(jax.random.fold_in(key, 31), 2)
    position = jnp.arange(NODES, dtype=jnp.float32) / max(NODES - 1, 1)
    offset = jnp.clip(jax.random.normal(second, (D,), jnp.float32), -3.0, 3.0)
    ramp = jnp.exp(jnp.log(3.0) * position)
    base = jnp.clip(jax.random.normal(first, (NODES, D), jnp.float32), -6.0, 6.0)
    values = base + 0.7 * ramp[:, None] * offset[None, :]
    return values.astype(jnp.bfloat16)


def key_weights(key):
    first = jax.random.fold_in(jax.random.fold_in(key, 21), 0)
    drawn = jnp.clip(jax.random.normal(first, (LAYERS, D, D), jnp.float32), -6.0, 6.0) / jnp.sqrt(jnp.float32(D))
    return drawn


def draw_w_key(key, part):
    return key_weights(key).astype(jnp.bfloat16)


def draw_w_query(key, part):
    values = jnp.clip(jax.random.normal(jax.random.fold_in(key, 23), (LAYERS, D, D), jnp.float32), -6.0, 6.0) / jnp.sqrt(jnp.float32(D))
    return values.astype(jnp.bfloat16)


def with_ends(values, rng, low, high):
    shape = values.shape
    place = [jax.random.randint(jax.random.fold_in(rng, axis), (), 0, shape[axis]) for axis in range(len(shape))]
    values = values.at[tuple(place)].set(low)
    longest = shape.index(max(shape))
    place[longest] = (place[longest] + 1) % shape[longest]
    return values.at[tuple(place)].set(high)


def normal_values(rng, shape, deviation, limit, kind=jnp.bfloat16):
    array = deviation * jax.random.normal(rng, shape, jnp.float32)
    return jnp.clip(array, min=-limit, max=limit).astype(kind)


def setup_inputs(seed: int = 0, part: int = 0) -> dict:
    key_of = jax.random.split(jax.random.key(seed), 13)
    part_keys = jax.random.split(jax.random.fold_in(key_of[12], part), 13)
    node_features = draw_node_features(jax.random.fold_in(jax.random.fold_in(key_of[12], part), 71), part)
    nbr_table = draw_nbr_table(jax.random.fold_in(key_of[12], 71), part)
    nbr_count = draw_nbr_count(jax.random.fold_in(key_of[12], 71), part)
    send_block = with_ends(jax.random.randint(key_of[3], (N_ROW * N_ROW, SLOTS), 0, BLK_DEV), jax.random.fold_in(key_of[3], 1), 0, BLK_DEV - 1).astype(jnp.int32)
    w_query = draw_w_query(jax.random.fold_in(key_of[12], 71), part)
    w_key = draw_w_key(jax.random.fold_in(key_of[12], 71), part)
    w_value = normal_values(key_of[6], (LAYERS, D, D), D ** -0.5, 0.25)
    w_out = normal_values(key_of[7], (LAYERS, D, D), D ** -0.5, 0.25)
    w_up = normal_values(key_of[8], (LAYERS, D, FF), D ** -0.5, 0.25)
    w_down = normal_values(key_of[9], (LAYERS, FF, D), FF ** -0.5, 0.125)
    w_virtual = normal_values(key_of[10], (LAYERS, D, D), D ** -0.5, 0.25)
    gains = jnp.clip(1.0 + 0.15 * jax.random.normal(key_of[11], (LAYERS, 4, D), jnp.float32), 0.25, 1.75)
    return {"node_features": node_features, "nbr_table": nbr_table, "nbr_count": nbr_count, "send_block": send_block, "w_query": w_query, "w_key": w_key, "w_value": w_value, "w_out": w_out, "w_up": w_up, "w_down": w_down, "w_virtual": w_virtual, "gains": gains}


def normalize(values, scaling):
    centred = values - lax.optimization_barrier(jnp.mean(values, axis=-1, keepdims=True))
    spread = lax.optimization_barrier(jnp.mean(centred * centred, axis=-1, keepdims=True))
    return centred * lax.rsqrt(spread + 1e-05) * scaling

def attend(queries, table, listed, counts):
    groups, block, width = queries.shape
    slots = listed.shape[1]
    head_size = width // HEADS
    picked = table[listed]
    keys = picked[..., :width].reshape(groups, slots * block, HEADS, head_size)
    values = picked[..., width:].reshape(groups, slots * block, HEADS, head_size)
    heads_q = queries.reshape(groups, block, HEADS, head_size)
    scores = jnp.einsum('gqhd,gkhd->ghqk', heads_q.astype(jnp.float32), keys.astype(jnp.float32)) / math.sqrt(head_size)
    live = (jnp.arange(slots * block, dtype=jnp.int32) // block)[None, :] < counts[:, None]
    scores = jnp.where(live[:, None, None, :], scores, -1e+30)
    top = lax.optimization_barrier(jnp.max(scores, axis=-1, keepdims=True))
    weights = jnp.exp(scores - top)
    probs = (weights / lax.optimization_barrier(jnp.sum(weights, axis=-1, keepdims=True))).astype(jnp.bfloat16)
    context = jnp.einsum('ghqk,gkhd->gqhd', probs.astype(jnp.float32), values.astype(jnp.float32))
    return context.astype(jnp.bfloat16).reshape(groups, block, width)

def reference(node_features, nbr_table, nbr_count, send_block, w_query, w_key, w_value, w_out, w_up, w_down, w_virtual, gains):
    near_count = 2 * HALO_B + BLK_DEV
    owner = (jnp.arange(NBLK, dtype=jnp.int32) // BLK_DEV)[:, None]
    beyond = jnp.maximum(nbr_table - near_count, 0)
    peer = beyond // SLOTS
    sent = send_block[peer * N_ROW + owner, beyond % SLOTS]
    source_blocks = jnp.where(nbr_table < near_count, owner * BLK_DEV + nbr_table - HALO_B, peer * BLK_DEV + sent).astype(jnp.int32)
    latent = node_features
    for layer_index in range(LAYERS):
        current = latent.astype(jnp.float32)
        node_mean = lax.optimization_barrier(jnp.sum(current, axis=0)) / NODES
        normed = normalize(current, gains[layer_index, 0]).astype(jnp.bfloat16)
        queries = jnp.dot(normed, w_query[layer_index], preferred_element_type=jnp.float32).astype(jnp.bfloat16)
        w_pair = jnp.concatenate((w_key[layer_index], w_value[layer_index]), axis=1)
        pairs = jnp.dot(normed, w_pair, preferred_element_type=jnp.float32).astype(jnp.bfloat16).reshape(NBLK, BLOCK, 2 * D)

        def attend_device(operands):
            return attend(operands[0], pairs, operands[1], operands[2])
        context = lax.map(attend_device, (queries.reshape(N_ROW, BLK_DEV, BLOCK, D), source_blocks.reshape(N_ROW, BLK_DEV, NBR), nbr_count.reshape(N_ROW, BLK_DEV)))
        context = context.reshape(NODES, D)
        after_att = current + normalize(jnp.dot(context, w_out[layer_index], preferred_element_type=jnp.float32), gains[layer_index, 1])
        middle = normalize(after_att, gains[layer_index, 2]).astype(jnp.bfloat16)
        hidden = jax.nn.gelu(jnp.dot(middle, w_up[layer_index], preferred_element_type=jnp.float32)).astype(jnp.bfloat16)
        virtual_mean = node_mean.astype(jnp.bfloat16)
        virtual = jnp.dot(virtual_mean[None, :], w_virtual[layer_index], preferred_element_type=jnp.float32)
        output_part = normalize(jnp.dot(hidden, w_down[layer_index], preferred_element_type=jnp.float32), gains[layer_index, 3])
        latent = (after_att + output_part + virtual).astype(jnp.bfloat16)
    return latent
```

```python
import functools
import math

import jax
import jax.numpy as jnp
from jax import lax
from jax.experimental import pallas as pl
from jax.experimental.pallas import tpu as pltpu
from jax.sharding import PartitionSpec as P

HEADS = 4
HALO_B = 2
VMEM_LIMIT = 67_000_000
MESH = pl.DeviceIdType.MESH
BF16 = jnp.bfloat16
F32 = jnp.float32
AXIS = "row"


def normalize(values, scaling):
    centred = values - jnp.mean(values, axis=-1, keepdims=True)
    spread = jnp.mean(centred * centred, axis=-1, keepdims=True)
    return centred * lax.rsqrt(spread + 1e-05) * scaling


def dot(a, b, contract=((1,), (0,))):
    return lax.dot_general(a, b, (contract, ((), ())), preferred_element_type=F32)


def gelu(x):
    return 0.5 * x * (1.0 + jnp.tanh(math.sqrt(2 / math.pi) * (x + 0.044715 * x * x * x)))


def flip(a, b, bits):
    out = 0
    for bit in range(bits):
        weight = 1 << bit
        x = lax.rem(lax.div(a, jnp.int32(weight)), jnp.int32(2))
        y = lax.rem(lax.div(b, jnp.int32(weight)), jnp.int32(2))
        out = out + weight * lax.rem(x + y, jnp.int32(2))
    return out


def below(a, b):
    return jnp.minimum(jnp.maximum(b - a, 0), 1)


def equal(a, b):
    return 1 - jnp.minimum(jnp.maximum(a - b, b - a), 1)


def kernel(shapes, table_sm, count_sm, send_sm, x_ref, gains_ref, wq_hbm, wk_hbm, wv_hbm, wo_hbm, wu_hbm, wd_hbm,
           wm_hbm, out_ref, wq, wk, wv, wo, wu, wd, wm, normed, latent, keys, values, context, send_buf, far,
           halo_send, halo, sum_send, sums, total_ref, virtual, perm_sm, pos_sm, place_sm, w_sem, far_send, far_recv,
           halo_ssem, halo_rsem, sum_ssem, sum_rsem):
    peers, layers, blocks, block, width, slots, listed, group, node_total = shapes
    near = 2 * HALO_B + blocks
    bits = peers.bit_length() - 1
    half, quarter = peers // 2, peers // 4
    rows = group * block
    steps = blocks // group
    head = width // HEADS
    hidden_size = wu.shape[-1]
    me = lax.axis_index(AXIS)
    inner = jnp.where((me >= quarter) & (me < half + quarter), 1, 0)

    def order(layer, k):
        outer = jnp.where(k < half, half + k, peers - 1 - k)
        if layer == 0:
            inside = jnp.where(k < half - 1, half - 1 - k, peers - 1 - (k - (half - 1)))
        else:
            late = k - quarter
            inside = jnp.where(
                late < 0, peers - 1 - k, jnp.where(late < half - 1, half - 1 - late, peers - 1 - quarter - (late - half + 1))
            )
        return flip(me, jnp.where(inner == 1, inside, outer), bits)

    def remote(src, dst, ssem, rsem, to):
        return pltpu.make_async_remote_copy(
            src_ref=src, dst_ref=dst, send_sem=ssem, recv_sem=rsem, device_id={AXIS: to}, device_id_type=MESH
        )

    def far_out(layer, to):
        return remote(send_buf.at[layer, to], far.at[layer, me], far_send.at[layer, to], far_recv.at[layer, me], to)

    def far_in(layer, source):
        return remote(
            send_buf.at[layer, source], far.at[layer, source], far_send.at[layer, source], far_recv.at[layer, source], source
        )

    def sum_out(layer, to):
        return remote(sum_send.at[layer], sums.at[layer, me], sum_ssem.at[layer, to], sum_rsem.at[layer, me], to)

    def sum_in(layer, source):
        return remote(sum_send.at[layer], sums.at[layer, source], sum_ssem.at[layer, source], sum_rsem.at[layer, source], source)

    def halo_copy(layer, side, to):
        return remote(
            halo_send.at[layer, side], halo.at[layer, 1 - side], halo_ssem.at[layer, side], halo_rsem.at[layer, 1 - side], to
        )

    def halo_each(layer, act):
        @pl.when(me > 0)
        def _():
            act(halo_copy(layer, 0, me - 1), 0)

        @pl.when(me < peers - 1)
        def _():
            act(halo_copy(layer, 1, me + 1), 1)

    barrier = pltpu.get_barrier_semaphore()

    def greet(k, carry):
        pl.semaphore_signal(barrier, inc=1, device_id={AXIS: lax.rem(me + k, peers)}, device_id_type=MESH)
        return carry

    lax.fori_loop(1, peers, greet, 0)

    loads = []
    for layer in range(layers):
        for n, (src, dst) in enumerate(
            ((wk_hbm, wk), (wv_hbm, wv), (wm_hbm, wm), (wq_hbm, wq), (wo_hbm, wo), (wu_hbm, wu), (wd_hbm, wd))
        ):
            loads.append(pltpu.make_async_copy(src.at[layer], dst.at[layer], w_sem.at[layer, n]))
    for load in loads:
        load.start()

    total_ref[0:1, :] = jnp.zeros((1, width), F32)

    def first(i, carry):
        x = x_ref[pl.ds(i * group, group)].reshape(rows, width).astype(F32)
        total_ref[0:1, :] = total_ref[0:1, :] + jnp.sum(x, axis=0, keepdims=True)
        fresh = normalize(x, gains_ref[0, 0:1, :]).astype(BF16)
        normed[0, pl.ds(i * group, group)] = fresh.reshape(group, block, width)
        return carry

    lax.fori_loop(0, steps, first, 0)

    def stage(layer, to):
        for slot in range(slots):
            at = send_sm[to * slots + slot]
            if layer > 0:
                at = pos_sm[at]
            send_buf[layer, to, pl.ds(slot * block, block), :] = normed[layer, at]

    def stage_self(layer):
        for slot in range(slots):
            at = send_sm[me * slots + slot]
            if layer > 0:
                at = pos_sm[at]
            far[layer, me, pl.ds(slot * block, block), :] = normed[layer, at]

    def stage_edges(layer):
        for side in range(2):
            for b in range(HALO_B):
                at = b if side == 0 else blocks - HALO_B + b
                if layer > 0:
                    at = pos_sm[at]
                halo_send[layer, side, pl.ds(b * block, block), :] = normed[layer, at]
        for k in range(width // 128):
            part = total_ref[0:1, k * 128 : (k + 1) * 128]
            sum_send[layer, k : k + 1, :] = part
            sums[layer, me, k : k + 1, :] = part

    def send_edges(layer):
        def one(k, carry):
            sum_out(layer, order(layer, k)).start()
            return carry

        lax.fori_loop(0, peers - 1, one, 0)
        halo_each(layer, lambda copy, side: copy.start())

    def stage_all(k, carry):
        stage(0, order(0, k))
        return carry

    def send_all(k, carry):
        far_out(0, order(0, k)).start()
        return carry

    stage_edges(0)
    lax.fori_loop(0, peers - 1, stage_all, 0)
    pl.semaphore_wait(barrier, peers - 1)
    send_edges(0)
    lax.fori_loop(0, peers - 1, send_all, 0)
    stage_self(0)

    uses = [jnp.int32(peers * slots + n) for n in range(blocks)]
    for k in range(peers - 2, -1, -1):
        to = order(1, jnp.int32(k))
        for slot in range(slots - 1, -1, -1):
            b = send_sm[to * slots + slot]
            uses = [use + equal(b, n) * (k * slots + slot - use) for n, use in enumerate(uses)]
    places = []
    for n in range(blocks):
        place = jnp.int32(0)
        for other in range(blocks):
            if other != n:
                place = place + below(uses[other], uses[n])
        places.append(place)
        pos_sm[n] = place
    for n in range(blocks):
        which = jnp.int32(0)
        for b in range(blocks):
            which = which + equal(places[b], n) * b
        perm_sm[n] = which
    for t in range(near + peers * slots):
        place_sm[0, t] = jnp.int32(t)
        own_b = t - HALO_B
        place_sm[1, t] = HALO_B + places[own_b] if 0 <= own_b < blocks else jnp.int32(t)

    count_w = 7

    def use(layer, names):
        for n in names:
            loads[layer * count_w + n].wait()

    def project(layer, piece, at):
        count = piece.shape[0]
        flat = piece.reshape(count * block, width)
        keys[pl.ds(at, count)] = dot(flat, wk[layer]).astype(BF16).reshape(count, block, width)
        turned = dot(wv[layer], flat, ((0,), (1,))).astype(BF16)
        for n in range(count):
            values[at + n] = turned[:, n * block : (n + 1) * block]

    def gather(layer):
        chunk = math.gcd(blocks, 4)

        def own_piece(i, carry):
            project(layer, normed[layer, pl.ds(i * chunk, chunk)], HALO_B + i * chunk)
            return carry

        lax.fori_loop(0, blocks // chunk, own_piece, 0)

        def halo_in(copy, side):
            copy.wait_recv()
            project(layer, halo[layer, side].reshape(HALO_B, block, width), 0 if side == 0 else HALO_B + blocks)

        @pl.when(me > 0)
        def _():
            halo_in(halo_copy(layer, 1, me - 1), 0)

        @pl.when(me < peers - 1)
        def _():
            halo_in(halo_copy(layer, 0, me + 1), 1)

        many = math.gcd(quarter, 4)
        for inside, outside in ((2, 0), (0, 1), (1, 3), (3, 2)):
            part = flip(lax.div(me, jnp.int32(quarter)), jnp.where(inner == 1, inside, outside), 2) * quarter

            def wait_one(n, carry, part=part):
                source = part + n

                @pl.when(source != me)
                def _():
                    far_in(layer, source).wait_recv()

                return carry

            def far_piece(i, carry, part=part):
                source = part + i * many
                lax.fori_loop(i * many, (i + 1) * many, wait_one, 0)
                piece = far[layer, pl.ds(source, many)].reshape(many * slots, block, width)
                project(layer, piece, near + source * slots)
                return carry

            lax.fori_loop(0, quarter // many, far_piece, 0)

        def sum_wait(k, carry):
            sum_in(layer, order(layer, k)).wait_recv()
            return carry

        lax.fori_loop(0, peers - 1, sum_wait, 0)
        whole = jnp.sum(sums[layer], axis=0)
        mean = jnp.concatenate([whole[k : k + 1, :] for k in range(width // 128)], axis=1) / node_total
        mean = jnp.broadcast_to(mean, (16, width)).astype(BF16)
        virtual[...] = dot(mean, wm[layer])

    scale = math.log2(math.e) / math.sqrt(head)

    def attend(layer, which, queries, at):
        count = count_sm[which]
        home = table_sm[which, 0]
        spots = []
        for j in range(listed):
            entry = table_sm[which, j]
            if 2 * j >= listed:
                entry = home + below(j, count) * (entry - home)
            spots.append(place_sm[layer, entry])
        dead = [(1 - below(j, count)).astype(F32) * -1e30 for j in range(listed)]
        blank = jnp.zeros((head, block), BF16)
        for h in range(0, HEADS, 2):
            pair = slice(h * head, (h + 2) * head)
            upper = queries[h * head : (h + 1) * head, at : at + block]
            lower = queries[(h + 1) * head : (h + 2) * head, at : at + block]
            both = jnp.concatenate(
                [jnp.concatenate([upper, blank], axis=1), jnp.concatenate([blank, lower], axis=1)], axis=0
            )
            scores = []
            for j in range(listed):
                s = dot(keys[spots[j], :, pair], both)
                scores.append(s if 2 * j < listed else s + dead[j])
            top = jnp.max(functools.reduce(jnp.maximum, scores), axis=0, keepdims=True)
            weights = [jnp.exp2((s - top) * scale) for s in scores]
            inverse = 1.0 / jnp.sum(functools.reduce(jnp.add, weights), axis=0, keepdims=True)
            probs = jnp.concatenate([w.astype(BF16) for w in weights], axis=0)
            v = jnp.concatenate([values[p, pair] for p in spots], axis=1)
            mixed = dot(v, probs)
            for n in range(2):
                part = slice(n * block, (n + 1) * block)
                of_head = slice((h + n) * head, (h + n + 1) * head)
                context[of_head, at : at + block] = (
                    mixed[n * head : (n + 1) * head, part] * inverse[:, part]
                ).astype(BF16)

    def block_step(layer, i):
        last = layer == layers - 1
        order_at = [i * group + g for g in range(group)]
        if last:
            which = order_at
            source = [pos_sm[w] for w in which]
        else:
            which = [perm_sm[n] for n in order_at]
            source = which
        mine = jnp.concatenate([normed[layer, s] for s in source], axis=0)
        queries = dot(wq[layer], mine, ((0,), (1,))).astype(BF16)
        for g in range(group):
            attend(layer, which[g], queries, g * block)
        current = latent if layer > 0 else x_ref
        x = jnp.concatenate([current[s] for s in source], axis=0).astype(F32)
        after_att = x + normalize(dot(context[...], wo[layer], ((0,), (0,))), gains_ref[layer, 1:2, :])
        middle = normalize(after_att, gains_ref[layer, 2:3, :]).astype(BF16)
        part = math.gcd(hidden_size, 512)
        down = None
        for f in range(0, hidden_size, part):
            hidden = gelu(dot(middle, wu[layer, :, f : f + part])).astype(BF16)
            term = dot(hidden, wd[layer, f : f + part, :])
            down = term if down is None else down + term
        result = (after_att + normalize(down, gains_ref[layer, 3:4, :]) + virtual[0:1, :]).astype(BF16)
        at = pl.ds(i * group, group)
        if last:
            out_ref[at] = result.reshape(group, block, width)
        else:
            latent[at] = result.reshape(group, block, width)
            wide = result.astype(F32)
            fresh = normalize(wide, gains_ref[layer + 1, 0:1, :]).astype(BF16)
            normed[layer + 1, at] = fresh.reshape(group, block, width)
            total_ref[0:1, :] = total_ref[0:1, :] + jnp.sum(wide, axis=0, keepdims=True)

    use(0, range(3))
    gather(0)
    use(0, range(3, count_w))
    total_ref[0:1, :] = jnp.zeros((1, width), F32)

    def sending_step(i, carry):
        block_step(0, i)

        def each(k, carry):
            stage(1, order(1, k))
            return carry

        def go(k, carry):
            far_out(1, order(1, k)).start()
            return carry

        lax.fori_loop(i * group, (i + 1) * group, each, 0)
        lax.fori_loop(i * group, (i + 1) * group, go, 0)
        return carry

    def rest(k, carry):
        stage(1, order(1, k))
        return carry

    def go_rest(k, carry):
        far_out(1, order(1, k)).start()
        return carry

    lax.fori_loop(0, steps, sending_step, 0)
    stage_edges(1)
    lax.fori_loop(blocks, peers - 1, rest, 0)
    send_edges(1)
    lax.fori_loop(blocks, peers - 1, go_rest, 0)
    stage_self(1)

    use(1, range(3))
    gather(1)
    use(1, range(3, count_w))

    def last_step(i, carry):
        block_step(1, i)
        return carry

    lax.fori_loop(0, steps, last_step, 0)

    for layer in range(layers):
        def drain(k, carry, layer=layer):
            to = order(layer, k)
            far_out(layer, to).wait_send()
            sum_out(layer, to).wait_send()
            return carry

        lax.fori_loop(0, peers - 1, drain, 0)
        halo_each(layer, lambda copy, side: copy.wait_send())


def body(node_features, nbr_table, nbr_count, send_block, w_query, w_key, w_value, w_out, w_up, w_down, w_virtual, gains):
    blocks, listed = nbr_table.shape
    own, width = node_features.shape
    block = own // blocks
    peers = lax.axis_size(AXIS)
    slots = send_block.shape[1]
    layers = w_query.shape[0]
    group = math.gcd(blocks, 4)
    near = 2 * HALO_B + blocks
    entries = near + peers * slots
    shapes = (peers, layers, blocks, block, width, slots, listed, group, own * peers)
    weights = (w_query, w_key, w_value, w_out, w_up, w_down, w_virtual)
    vmem, smem, hbm = (pl.BlockSpec(memory_space=s) for s in (pltpu.VMEM, pltpu.SMEM, pl.ANY))
    dma = pltpu.SemaphoreType.DMA
    scratch = [pltpu.VMEM(w.shape, BF16) for w in weights]
    scratch += [
        pltpu.VMEM((layers, blocks, block, width), BF16),
        pltpu.VMEM((blocks, block, width), BF16),
        pltpu.VMEM((entries, block, width), BF16),
        pltpu.VMEM((entries, width, block), BF16),
        pltpu.VMEM((width, group * block), BF16),
        pltpu.VMEM((layers, peers, slots * block, width), BF16),
        pltpu.VMEM((layers, peers, slots * block, width), BF16),
        pltpu.VMEM((layers, 2, HALO_B * block, width), BF16),
        pltpu.VMEM((layers, 2, HALO_B * block, width), BF16),
        pltpu.VMEM((layers, width // 128, 128), F32),
        pltpu.VMEM((layers, peers, width // 128, 128), F32),
        pltpu.VMEM((8, width), F32),
        pltpu.VMEM((16, width), F32),
        pltpu.SMEM((blocks,), jnp.int32),
        pltpu.SMEM((blocks,), jnp.int32),
        pltpu.SMEM((layers, entries), jnp.int32),
        dma((layers, len(weights))),
        dma((layers, peers)),
        dma((layers, peers)),
        dma((layers, 2)),
        dma((layers, 2)),
        dma((layers, peers)),
        dma((layers, peers)),
    ]
    return pl.pallas_call(
        functools.partial(kernel, shapes),
        out_shape=jax.ShapeDtypeStruct((blocks, block, width), BF16),
        in_specs=[smem, smem, smem, vmem, vmem] + [hbm] * len(weights),
        out_specs=vmem,
        scratch_shapes=scratch,
        compiler_params=pltpu.CompilerParams(collective_id=0, has_side_effects=True, vmem_limit_bytes=VMEM_LIMIT),
        name="processor",
    )(nbr_table, nbr_count, send_block.reshape(-1), node_features.reshape(blocks, block, width), gains, *weights).reshape(own, width)


def solution(mesh):
    across = P(("members", "row"), None)
    in_specs = (across, P("row", None), P("row"), P("row", None)) + (P(),) * 8
    return jax.shard_map(body, mesh=mesh, in_specs=in_specs, out_specs=across, check_vma=False)
```

```python
import functools
import math

import jax
import jax.numpy as jnp
from jax import lax
from jax.experimental import pallas as pl
from jax.experimental.pallas import tpu as pltpu
from jax.sharding import PartitionSpec as P

HEADS = 4
HALO_B = 2
VMEM_LIMIT = 67_000_000
MESH = pl.DeviceIdType.MESH
BF16 = jnp.bfloat16
F32 = jnp.float32
AXIS = "row"


def normalize(values, scaling):
    centred = values - jnp.mean(values, axis=-1, keepdims=True)
    spread = jnp.mean(centred * centred, axis=-1, keepdims=True)
    return centred * lax.rsqrt(spread + 1e-05) * scaling


def dot(a, b, contract=((1,), (0,))):
    return lax.dot_general(a, b, (contract, ((), ())), preferred_element_type=F32)


def gelu(x):
    return 0.5 * x * (1.0 + jnp.tanh(math.sqrt(2 / math.pi) * (x + 0.044715 * x * x * x)))


def flip(a, b, bits):
    out = 0
    for bit in range(bits):
        weight = 1 << bit
        x = lax.rem(lax.div(a, jnp.int32(weight)), jnp.int32(2))
        y = lax.rem(lax.div(b, jnp.int32(weight)), jnp.int32(2))
        out = out + weight * lax.rem(x + y, jnp.int32(2))
    return out


def below(a, b):
    return jnp.minimum(jnp.maximum(b - a, 0), 1)


def equal(a, b):
    return 1 - jnp.minimum(jnp.maximum(a - b, b - a), 1)


def attend(count, key_of, value_of, query_of, context, at, listed, head, block):
    scale = math.log2(math.e) / math.sqrt(head)
    dead = [(1 - below(j, count)).astype(F32) * -1e30 for j in range(listed)]
    blank = jnp.zeros((head, block), BF16)
    for h in range(0, HEADS, 2):
        pair = slice(h * head, (h + 2) * head)
        upper = query_of(slice(h * head, (h + 1) * head))
        lower = query_of(slice((h + 1) * head, (h + 2) * head))
        both = jnp.concatenate(
            [jnp.concatenate([upper, blank], axis=1), jnp.concatenate([blank, lower], axis=1)], axis=0
        )
        scores = []
        for j in range(listed):
            s = dot(key_of(j, pair), both)
            scores.append(s if 2 * j < listed else s + dead[j])
        top = jnp.max(functools.reduce(jnp.maximum, scores), axis=0, keepdims=True)
        weights = [jnp.exp2((s - top) * scale) for s in scores]
        inverse = 1.0 / jnp.sum(functools.reduce(jnp.add, weights), axis=0, keepdims=True)
        probs = jnp.concatenate([w.astype(BF16) for w in weights], axis=0)
        mixed = dot(jnp.concatenate([value_of(j, pair) for j in range(listed)], axis=1), probs)
        for n in range(2):
            part = slice(n * block, (n + 1) * block)
            of_head = slice((h + n) * head, (h + n + 1) * head)
            context[of_head, at : at + block] = (mixed[n * head : (n + 1) * head, part] * inverse[:, part]).astype(BF16)


def feed(x, context, wo, wu, wd, gains_ref, layer):
    after_att = x + normalize(dot(context, wo, ((0,), (0,))), gains_ref[layer, 1:2, :])
    middle = normalize(after_att, gains_ref[layer, 2:3, :]).astype(BF16)
    hidden_size = wu.shape[-1]
    part = math.gcd(hidden_size, 512)
    down = None
    for f in range(0, hidden_size, part):
        hidden = gelu(dot(middle, wu[:, f : f + part])).astype(BF16)
        term = dot(hidden, wd[f : f + part, :])
        down = term if down is None else down + term
    return after_att + normalize(down, gains_ref[layer, 3:4, :])


def exchange_kernel(shapes, table_sm, count_sm, send_sm, gains_ref, x_hbm, wq_hbm, wk_hbm, wv_hbm, wo_hbm, wu_hbm,
                    wd_hbm, wm_hbm, early_out, keys_out, values_out, queries_out, latent_out, virtual_ref, wq, wk, wv,
                    wo, wu, wd, wm, x_ref, normed, latent, keys, values, context, send_buf, far, halo_send, halo,
                    sum_send, sums, total_ref, early, asked, arranged, virtual, perm_sm, pos_sm, x_sem, w_sem, far_send,
                    far_recv, halo_ssem, halo_rsem, sum_ssem, sum_rsem, table_sem, early_sem):
    peers, layers, blocks, block, width, slots, listed, group, node_total = shapes
    near = 2 * HALO_B + blocks
    bits = peers.bit_length() - 1
    half, quarter = peers // 2, peers // 4
    rows = group * block
    steps = blocks // group
    head = width // HEADS
    me = lax.axis_index(AXIS)
    inner = jnp.where((me >= quarter) & (me < half + quarter), 1, 0)

    def order(layer, k):
        outer = jnp.where(k < half, half + k, peers - 1 - k)
        if layer == 0:
            inside = jnp.where(k < half - 1, half - 1 - k, peers - 1 - (k - (half - 1)))
        else:
            lead = quarter // 2
            late = k - lead
            inside = jnp.where(
                late < 0, peers - 1 - k, jnp.where(late < half - 1, half - 1 - late, peers - 1 - lead - (late - half + 1))
            )
        return flip(me, jnp.where(inner == 1, inside, outer), bits)

    def remote(src, dst, ssem, rsem, to):
        return pltpu.make_async_remote_copy(
            src_ref=src, dst_ref=dst, send_sem=ssem, recv_sem=rsem, device_id={AXIS: to}, device_id_type=MESH
        )

    def far_out(layer, to):
        return remote(send_buf.at[layer, to], far.at[layer, me], far_send.at[layer, to], far_recv.at[layer, me], to)

    def far_in(layer, source):
        return remote(
            send_buf.at[layer, source], far.at[layer, source], far_send.at[layer, source], far_recv.at[layer, source], source
        )

    def sum_out(layer, to):
        return remote(sum_send.at[layer], sums.at[layer, me], sum_ssem.at[layer, to], sum_rsem.at[layer, me], to)

    def sum_in(layer, source):
        return remote(sum_send.at[layer], sums.at[layer, source], sum_ssem.at[layer, source], sum_rsem.at[layer, source], source)

    def halo_copy(layer, side, to):
        return remote(
            halo_send.at[layer, side], halo.at[layer, 1 - side], halo_ssem.at[layer, side], halo_rsem.at[layer, 1 - side], to
        )

    def halo_each(layer, act):
        @pl.when(me > 0)
        def _():
            act(halo_copy(layer, 0, me - 1), 0)

        @pl.when(me < peers - 1)
        def _():
            act(halo_copy(layer, 1, me + 1), 1)

    barrier = pltpu.get_barrier_semaphore()

    def greet(k, carry):
        pl.semaphore_signal(barrier, inc=1, device_id={AXIS: lax.rem(me + k, peers)}, device_id_type=MESH)
        return carry

    lax.fori_loop(1, peers, greet, 0)

    load_x = pltpu.make_async_copy(x_hbm, x_ref, x_sem)
    load_x.start()
    loads = []
    for layer in range(layers):
        for n, (src, dst) in enumerate(
            ((wk_hbm, wk), (wv_hbm, wv), (wm_hbm, wm), (wq_hbm, wq), (wo_hbm, wo), (wu_hbm, wu), (wd_hbm, wd))
        ):
            loads.append(pltpu.make_async_copy(src.at[layer], dst.at[layer], w_sem.at[layer, n]))
    for load in loads:
        load.start()

    total_ref[0:1, :] = jnp.zeros((1, width), F32)
    load_x.wait()

    def first(i, carry):
        x = x_ref[pl.ds(i * group, group)].reshape(rows, width).astype(F32)
        total_ref[0:1, :] = total_ref[0:1, :] + jnp.sum(x, axis=0, keepdims=True)
        fresh = normalize(x, gains_ref[0, 0:1, :]).astype(BF16)
        normed[0, pl.ds(i * group, group)] = fresh.reshape(group, block, width)
        return carry

    lax.fori_loop(0, steps, first, 0)

    def stage(layer, to):
        for slot in range(slots):
            at = send_sm[to * slots + slot]
            if layer > 0:
                at = pos_sm[at]
            send_buf[layer, to, pl.ds(slot * block, block), :] = normed[layer, at]

    def stage_self(layer):
        for slot in range(slots):
            at = send_sm[me * slots + slot]
            if layer > 0:
                at = pos_sm[at]
            far[layer, me, pl.ds(slot * block, block), :] = normed[layer, at]

    def stage_edges(layer):
        for side in range(2):
            for b in range(HALO_B):
                at = b if side == 0 else blocks - HALO_B + b
                if layer > 0:
                    at = pos_sm[at]
                halo_send[layer, side, pl.ds(b * block, block), :] = normed[layer, at]
        for k in range(width // 128):
            part = total_ref[0:1, k * 128 : (k + 1) * 128]
            sum_send[layer, k : k + 1, :] = part
            sums[layer, me, k : k + 1, :] = part

    def send_edges(layer):
        def one(k, carry):
            sum_out(layer, order(layer, k)).start()
            return carry

        lax.fori_loop(0, peers - 1, one, 0)
        halo_each(layer, lambda copy, side: copy.start())

    def stage_all(k, carry):
        stage(0, order(0, k))
        return carry

    def send_all(k, carry):
        far_out(0, order(0, k)).start()
        return carry

    stage_edges(0)
    lax.fori_loop(0, peers - 1, stage_all, 0)
    pl.semaphore_wait(barrier, peers - 1)
    send_edges(0)
    lax.fori_loop(0, peers - 1, send_all, 0)
    stage_self(0)

    uses = [jnp.int32(peers * slots + n) for n in range(blocks)]
    for k in range(peers - 2, -1, -1):
        to = order(1, jnp.int32(k))
        for slot in range(slots - 1, -1, -1):
            b = send_sm[to * slots + slot]
            uses = [use + equal(b, n) * (k * slots + slot - use) for n, use in enumerate(uses)]
    places = []
    for n in range(blocks):
        place = jnp.int32(0)
        for other in range(blocks):
            if other != n:
                place = place + below(uses[other], uses[n])
        places.append(place)
        pos_sm[n] = place
    for n in range(blocks):
        which = jnp.int32(0)
        for b in range(blocks):
            which = which + equal(places[b], n) * b
        perm_sm[n] = which
    count_w = 7

    def use(layer, names):
        for n in names:
            loads[layer * count_w + n].wait()

    def project(layer, piece, at):
        count = piece.shape[0]
        flat = piece.reshape(count * block, width)
        keys[pl.ds(at, count)] = dot(flat, wk[layer]).astype(BF16).reshape(count, block, width)
        turned = dot(wv[layer], flat, ((0,), (1,))).astype(BF16)
        for n in range(count):
            values[at + n] = turned[:, n * block : (n + 1) * block]

    def export(at, count, n):
        part = pl.ds(at, count)
        return (
            pltpu.make_async_copy(keys.at[part], keys_out.at[part], table_sem.at[0, n]),
            pltpu.make_async_copy(values.at[part], values_out.at[part], table_sem.at[1, n]),
        )

    chunk = math.gcd(blocks, 4)
    many = math.gcd(quarter, 4)
    first_far = blocks // chunk + 2

    def hand_on(layer, at, count, n):
        if layer == layers - 1:
            for copy in export(at, count, n):
                copy.start()

    def gather(layer):
        def own_piece(i, carry):
            if layer == 0:
                piece = normed[layer, pl.ds(i * chunk, chunk)]
            else:
                piece = jnp.concatenate([normed[layer, pos_sm[i * chunk + n]] for n in range(chunk)], axis=0)
                piece = piece.reshape(chunk, block, width)
            project(layer, piece, HALO_B + i * chunk)
            hand_on(layer, HALO_B + i * chunk, chunk, i)
            return carry

        lax.fori_loop(0, blocks // chunk, own_piece, 0)

        def halo_in(copy, side):
            copy.wait_recv()
            at = 0 if side == 0 else HALO_B + blocks
            project(layer, halo[layer, side].reshape(HALO_B, block, width), at)
            hand_on(layer, at, HALO_B, blocks // chunk + side)

        @pl.when(me > 0)
        def _():
            halo_in(halo_copy(layer, 1, me - 1), 0)

        @pl.when(me < peers - 1)
        def _():
            halo_in(halo_copy(layer, 0, me + 1), 1)

        if layer == layers - 1:
            lax.fori_loop(0, steps, early_step, 0)
            drain(0)
        for inside, outside in ((2, 0), (0, 1), (1, 3), (3, 2)):
            part = flip(lax.div(me, jnp.int32(quarter)), jnp.where(inner == 1, inside, outside), 2) * quarter

            def wait_one(n, carry, part=part):
                source = part + n

                @pl.when(source != me)
                def _():
                    far_in(layer, source).wait_recv()

                return carry

            def far_piece(i, carry, part=part):
                source = part + i * many
                lax.fori_loop(i * many, (i + 1) * many, wait_one, 0)
                piece = far[layer, pl.ds(source, many)].reshape(many * slots, block, width)
                project(layer, piece, near + source * slots)
                hand_on(layer, near + source * slots, many * slots, first_far + lax.div(source, jnp.int32(many)))
                return carry

            lax.fori_loop(0, quarter // many, far_piece, 0)

        def sum_wait(k, carry):
            sum_in(layer, lax.rem(me + k, peers)).wait_recv()
            return carry

        lax.fori_loop(1, peers, sum_wait, 0)
        whole = jnp.sum(sums[layer], axis=0)
        mean = jnp.concatenate([whole[k : k + 1, :] for k in range(width // 128)], axis=1) / node_total
        mean = jnp.broadcast_to(mean, (16, width)).astype(BF16)
        virtual[...] = dot(mean, wm[layer])

    def attend_in(layer, which, queries, at):
        count = count_sm[which]
        home = table_sm[which, 0]
        spots = []
        for j in range(listed):
            entry = table_sm[which, j]
            if 2 * j >= listed:
                entry = home + below(j, count) * (entry - home)
            spots.append(entry)
        attend(
            count,
            lambda j, pair: keys[spots[j], :, pair],
            lambda j, pair: values[spots[j], pair],
            lambda part: queries[part, at : at + block],
            context,
            at,
            listed,
            head,
            block,
        )

    def early_copies(i):
        at = pl.ds(i * group, group)
        return (
            pltpu.make_async_copy(early.at[at], early_out.at[at], early_sem.at[0, i]),
            pltpu.make_async_copy(asked.at[at], queries_out.at[at], early_sem.at[1, i]),
            pltpu.make_async_copy(arranged.at[at], latent_out.at[at], early_sem.at[2, i]),
        )

    def block_step(layer, i):
        last = layer == layers - 1
        order_at = [i * group + g for g in range(group)]
        if last:
            which = order_at
            source = [pos_sm[w] for w in which]
            for w, s in zip(which, source):
                arranged[w] = latent[s]
        else:
            which = [perm_sm[n] for n in order_at]
            source = which
        mine = jnp.concatenate([normed[layer, s] for s in source], axis=0)
        queries = dot(wq[layer], mine, ((0,), (1,))).astype(BF16)
        if last:
            for g in range(group):
                asked[which[g]] = queries[:, g * block : (g + 1) * block]
        for g in range(group):
            attend_in(layer, which[g], queries, g * block)
        current = latent if layer > 0 else x_ref
        x = jnp.concatenate([current[s] for s in source], axis=0).astype(F32)
        result = feed(x, context[...], wo[layer], wu.at[layer], wd.at[layer], gains_ref, layer)
        at = pl.ds(i * group, group)
        if last:
            early[at] = result.reshape(group, block, width)
            for copy in early_copies(i):
                copy.start()
        else:
            result = (result + virtual[0:1, :]).astype(BF16)
            latent[at] = result.reshape(group, block, width)
            wide = result.astype(F32)
            fresh = normalize(wide, gains_ref[layer + 1, 0:1, :]).astype(BF16)
            normed[layer + 1, at] = fresh.reshape(group, block, width)
            total_ref[0:1, :] = total_ref[0:1, :] + jnp.sum(wide, axis=0, keepdims=True)

    def early_step(i, carry):
        block_step(layers - 1, i)
        return carry

    def drain(layer):
        def one(k, carry):
            to = lax.rem(me + k, peers)
            far_out(layer, to).wait_send()
            sum_out(layer, to).wait_send()
            return carry

        lax.fori_loop(1, peers, one, 0)
        halo_each(layer, lambda copy, side: copy.wait_send())

    use(0, range(3))
    gather(0)
    use(0, range(3, count_w))
    total_ref[0:1, :] = jnp.zeros((1, width), F32)

    def sending_step(i, carry):
        block_step(0, i)

        @pl.when(i == steps - 1)
        def _():
            stage_edges(1)
            send_edges(1)

        def each(k, carry):
            stage(1, order(1, k))
            return carry

        def go(k, carry):
            far_out(1, order(1, k)).start()
            return carry

        lax.fori_loop(i * group, (i + 1) * group, each, 0)
        lax.fori_loop(i * group, (i + 1) * group, go, 0)
        return carry

    def rest(k, carry):
        stage(1, order(1, k))
        return carry

    def go_rest(k, carry):
        far_out(1, order(1, k)).start()
        return carry

    lax.fori_loop(0, steps, sending_step, 0)
    lax.fori_loop(blocks, peers - 1, rest, 0)
    lax.fori_loop(blocks, peers - 1, go_rest, 0)
    stage_self(1)

    use(1, range(count_w))
    gather(1)
    virtual_ref[...] = virtual[...]

    drain(1)

    def await_own(n, carry):
        for copy in export(HALO_B + n * chunk, chunk, n):
            copy.wait()
        return carry

    def await_far(n, carry):
        for copy in export(near + n * many * slots, many * slots, first_far + n):
            copy.wait()
        return carry

    def await_early(n, carry):
        for copy in early_copies(n):
            copy.wait()
        return carry

    @pl.when(me > 0)
    def _():
        for copy in export(0, HALO_B, blocks // chunk):
            copy.wait()

    @pl.when(me < peers - 1)
    def _():
        for copy in export(HALO_B + blocks, HALO_B, blocks // chunk + 1):
            copy.wait()

    lax.fori_loop(0, blocks // chunk, await_own, 0)
    lax.fori_loop(0, peers // many, await_far, 0)
    lax.fori_loop(0, steps, await_early, 0)


def finish_kernel(layer, near, group, table_sm, count_sm, gains_ref, virtual_ref, early_hbm, keys_hbm, values_hbm,
                  queries_hbm, latent_hbm, wo_hbm, wu_hbm, wd_hbm, out_ref, early, kept_keys, kept_values, asked, current,
                  context, wo, wu, wd, todo_sm, early_sem, w_sem, key_sem, value_sem, row_sem):
    blocks, block, width = out_ref.shape
    listed = table_sm.shape[1]
    head = width // HEADS

    load_early = pltpu.make_async_copy(early_hbm, early, early_sem)
    weight_loads = [
        pltpu.make_async_copy(src.at[layer], dst, w_sem.at[n])
        for n, (src, dst) in enumerate(((wo_hbm, wo), (wu_hbm, wu), (wd_hbm, wd)))
    ]

    number = jnp.int32(0)
    for b in range(blocks):
        away = jnp.int32(0)
        for j in range(listed):
            away = jnp.where((j < count_sm[b]) & (table_sm[b, j] >= near), 1, away)

        @pl.when(away > 0)
        def _(b=b, number=number):
            todo_sm[number] = b

        number = number + away

    def block_of(i, g):
        return todo_sm[jnp.minimum(i * group + g, number - 1)]

    def entry_of(which, j):
        return jnp.where(j < count_sm[which], table_sm[which, j], table_sm[which, 0])

    def copies(i, g):
        which = block_of(i, g)
        row = [
            pltpu.make_async_copy(queries_hbm.at[which], asked.at[g], row_sem.at[0, g]),
            pltpu.make_async_copy(latent_hbm.at[which], current.at[g], row_sem.at[1, g]),
        ]
        for j in range(listed):
            entry = entry_of(which, j)
            row.append(pltpu.make_async_copy(keys_hbm.at[entry], kept_keys.at[g, j], key_sem.at[g, j]))
            row.append(pltpu.make_async_copy(values_hbm.at[entry], kept_values.at[g, j], value_sem.at[g, j]))
        return row

    @pl.when(number > 0)
    def _():
        for g in range(group):
            for copy in copies(0, g):
                copy.start()

    load_early.start()
    for load in weight_loads:
        load.start()
    load_early.wait()
    shared = virtual_ref[0:1, :]

    def settle(b, carry):
        out_ref[b] = (early[b] + shared).astype(BF16)
        return carry

    lax.fori_loop(0, blocks, settle, 0)
    for load in weight_loads:
        load.wait()

    def late_step(i, carry):
        @pl.when(i > 0)
        def _():
            for g in range(group):
                for copy in copies(i, g):
                    copy.start()

        for g in range(group):
            which = block_of(i, g)
            for copy in copies(i, g):
                copy.wait()
            attend(
                count_sm[which],
                lambda j, pair, g=g: kept_keys[g, j, :, pair],
                lambda j, pair, g=g: kept_values[g, j, pair, :],
                lambda part, g=g: asked[g, part, :],
                context,
                g * block,
                listed,
                head,
                block,
            )
        x = current[...].reshape(group * block, width).astype(F32)
        result = feed(x, context[...], wo[...], wu, wd, gains_ref, layer) + shared
        result = result.astype(BF16).reshape(group, block, width)
        for g in range(group):
            out_ref[block_of(i, g)] = result[g]
        return carry

    lax.fori_loop(0, (number + group - 1) // group, late_step, 0)


def body(node_features, nbr_table, nbr_count, send_block, w_query, w_key, w_value, w_out, w_up, w_down, w_virtual, gains):
    blocks, listed = nbr_table.shape
    own, width = node_features.shape
    block = own // blocks
    peers = lax.axis_size(AXIS)
    slots = send_block.shape[1]
    layers = w_query.shape[0]
    group = math.gcd(blocks, 4)
    near = 2 * HALO_B + blocks
    entries = near + peers * slots
    shapes = (peers, layers, blocks, block, width, slots, listed, group, own * peers)
    weights = (w_query, w_key, w_value, w_out, w_up, w_down, w_virtual)
    vmem, smem, hbm = (pl.BlockSpec(memory_space=s) for s in (pltpu.VMEM, pltpu.SMEM, pl.ANY))
    dma = pltpu.SemaphoreType.DMA
    shape = jax.ShapeDtypeStruct
    steps = blocks // group
    groups = blocks // math.gcd(blocks, 4) + 2 + peers // math.gcd(peers // 4, 4)
    scratch = [pltpu.VMEM(w.shape, BF16) for w in weights]
    scratch += [
        pltpu.VMEM((blocks, block, width), BF16),
        pltpu.VMEM((layers, blocks, block, width), BF16),
        pltpu.VMEM((blocks, block, width), BF16),
        pltpu.VMEM((entries, block, width), BF16),
        pltpu.VMEM((entries, width, block), BF16),
        pltpu.VMEM((width, group * block), BF16),
        pltpu.VMEM((layers, peers, slots * block, width), BF16),
        pltpu.VMEM((layers, peers, slots * block, width), BF16),
        pltpu.VMEM((layers, 2, HALO_B * block, width), BF16),
        pltpu.VMEM((layers, 2, HALO_B * block, width), BF16),
        pltpu.VMEM((layers, width // 128, 128), F32),
        pltpu.VMEM((layers, peers, width // 128, 128), F32),
        pltpu.VMEM((8, width), F32),
        pltpu.VMEM((blocks, block, width), F32),
        pltpu.VMEM((blocks, width, block), BF16),
        pltpu.VMEM((blocks, block, width), BF16),
        pltpu.VMEM((16, width), F32),
        pltpu.SMEM((blocks,), jnp.int32),
        pltpu.SMEM((blocks,), jnp.int32),
        dma,
        dma((layers, len(weights))),
        dma((layers, peers)),
        dma((layers, peers)),
        dma((layers, 2)),
        dma((layers, 2)),
        dma((layers, peers)),
        dma((layers, peers)),
        dma((2, groups)),
        dma((3, steps)),
    ]
    early, keys, values, queries, latent, virtual = pl.pallas_call(
        functools.partial(exchange_kernel, shapes),
        out_shape=(
            shape((blocks, block, width), F32),
            shape((entries, block, width), BF16),
            shape((entries, width, block), BF16),
            shape((blocks, width, block), BF16),
            shape((blocks, block, width), BF16),
            shape((16, width), F32),
        ),
        in_specs=[smem, smem, smem, vmem] + [hbm] * (1 + len(weights)),
        out_specs=(hbm, hbm, hbm, hbm, hbm, vmem),
        scratch_shapes=scratch,
        compiler_params=pltpu.CompilerParams(collective_id=0, has_side_effects=True, vmem_limit_bytes=VMEM_LIMIT),
        name="exchange",
    )(nbr_table, nbr_count, send_block.reshape(-1), gains, node_features.reshape(blocks, block, width), *weights)
    result = pl.pallas_call(
        functools.partial(finish_kernel, layers - 1, near, group),
        out_shape=shape((blocks, block, width), BF16),
        in_specs=[smem, smem, vmem, vmem] + [hbm] * 8,
        out_specs=vmem,
        scratch_shapes=[
            pltpu.VMEM((blocks, block, width), F32),
            pltpu.VMEM((group, listed, block, width), BF16),
            pltpu.VMEM((group, listed, width, block), BF16),
            pltpu.VMEM((group, width, block), BF16),
            pltpu.VMEM((group, block, width), BF16),
            pltpu.VMEM((width, group * block), BF16),
            pltpu.VMEM(w_out.shape[1:], BF16),
            pltpu.VMEM(w_up.shape[1:], BF16),
            pltpu.VMEM(w_down.shape[1:], BF16),
            pltpu.SMEM((blocks,), jnp.int32),
            dma,
            dma((3,)),
            dma((group, listed)),
            dma((group, listed)),
            dma((2, group)),
        ],
        compiler_params=pltpu.CompilerParams(vmem_limit_bytes=VMEM_LIMIT),
        name="finish",
    )(nbr_table, nbr_count, gains, virtual, early, keys, values, queries, latent, w_out, w_up, w_down)
    return result.reshape(own, width)


def solution(mesh):
    across = P(("members", "row"), None)
    in_specs = (across, P("row", None), P("row"), P("row", None)) + (P(),) * 8
    return jax.shard_map(body, mesh=mesh, in_specs=in_specs, out_specs=across, check_vma=False)
```

```python
import functools
import math

import jax
import jax.numpy as jnp
from jax import lax
from jax.experimental import pallas as pl
from jax.experimental.pallas import tpu as pltpu
from jax.sharding import PartitionSpec as P

HEADS = 4
HALO_B = 2
VMEM_LIMIT = 67_000_000
MESH = pl.DeviceIdType.MESH
BF16 = jnp.bfloat16
F32 = jnp.float32
AXIS = "row"


def normalize(values, scaling):
    centred = values - jnp.mean(values, axis=-1, keepdims=True)
    spread = jnp.mean(centred * centred, axis=-1, keepdims=True)
    return centred * lax.rsqrt(spread + 1e-05) * scaling


def dot(a, b, contract=((1,), (0,))):
    return lax.dot_general(a, b, (contract, ((), ())), preferred_element_type=F32)


def gelu(x):
    return 0.5 * x * (1.0 + jnp.tanh(math.sqrt(2 / math.pi) * (x + 0.044715 * x * x * x)))


def flip(a, b, bits):
    out = 0
    for bit in range(bits):
        weight = 1 << bit
        x = lax.rem(lax.div(a, jnp.int32(weight)), jnp.int32(2))
        y = lax.rem(lax.div(b, jnp.int32(weight)), jnp.int32(2))
        out = out + weight * lax.rem(x + y, jnp.int32(2))
    return out


def below(a, b):
    return jnp.minimum(jnp.maximum(b - a, 0), 1)


def equal(a, b):
    return 1 - jnp.minimum(jnp.maximum(a - b, b - a), 1)


def attend(count, key_of, value_of, query_of, context, at, listed, head, block):
    scale = math.log2(math.e) / math.sqrt(head)
    dead = [(1 - below(j, count)).astype(F32) * -1e30 for j in range(listed)]
    blank = jnp.zeros((head, block), BF16)
    for h in range(0, HEADS, 2):
        pair = slice(h * head, (h + 2) * head)
        upper = query_of(slice(h * head, (h + 1) * head))
        lower = query_of(slice((h + 1) * head, (h + 2) * head))
        both = jnp.concatenate(
            [jnp.concatenate([upper, blank], axis=1), jnp.concatenate([blank, lower], axis=1)], axis=0
        )
        scores = []
        for j in range(listed):
            s = dot(key_of(j, pair), both)
            scores.append(s if 2 * j < listed else s + dead[j])
        top = jnp.max(functools.reduce(jnp.maximum, scores), axis=0, keepdims=True)
        weights = [jnp.exp2((s - top) * scale) for s in scores]
        inverse = 1.0 / jnp.sum(functools.reduce(jnp.add, weights), axis=0, keepdims=True)
        probs = jnp.concatenate([w.astype(BF16) for w in weights], axis=0)
        mixed = dot(jnp.concatenate([value_of(j, pair) for j in range(listed)], axis=1), probs)
        for n in range(2):
            part = slice(n * block, (n + 1) * block)
            of_head = slice((h + n) * head, (h + n + 1) * head)
            context[of_head, at : at + block] = (mixed[n * head : (n + 1) * head, part] * inverse[:, part]).astype(BF16)


def feed(x, context, wo, wu, wd, gains_ref, layer):
    after_att = x + normalize(dot(context, wo, ((0,), (0,))), gains_ref[layer, 1:2, :])
    middle = normalize(after_att, gains_ref[layer, 2:3, :]).astype(BF16)
    hidden_size = wu.shape[-1]
    part = math.gcd(hidden_size, 512)
    down = None
    for f in range(0, hidden_size, part):
        hidden = gelu(dot(middle, wu[:, f : f + part])).astype(BF16)
        term = dot(hidden, wd[f : f + part, :])
        down = term if down is None else down + term
    return after_att + normalize(down, gains_ref[layer, 3:4, :])


def exchange_kernel(shapes, table_sm, count_sm, send_sm, gains_ref, x_hbm, wq_hbm, wk_hbm, wv_hbm, wo_hbm, wu_hbm,
                    wd_hbm, wm_hbm, settled_out, keys_out, values_out, queries_out, latent_out, virtual_ref, wq, wk, wv,
                    wo, wu, wd, wm, x_ref, normed, latent, keys, values, context, send_buf, far, halo_send, halo,
                    sum_send, sums, total_ref, early, asked, arranged, virtual, perm_sm, pos_sm, x_sem, w_sem, far_send,
                    far_recv, halo_ssem, halo_rsem, sum_ssem, sum_rsem, table_sem, early_sem):
    peers, layers, blocks, block, width, slots, listed, group, node_total = shapes
    near = 2 * HALO_B + blocks
    bits = peers.bit_length() - 1
    half, quarter = peers // 2, peers // 4
    rows = group * block
    steps = blocks // group
    head = width // HEADS
    me = lax.axis_index(AXIS)
    inner = jnp.where((me >= quarter) & (me < half + quarter), 1, 0)

    def order(layer, k):
        outer = jnp.where(k < half, half + k, peers - 1 - k)
        if layer == 0:
            inside = jnp.where(k < half - 1, half - 1 - k, peers - 1 - (k - (half - 1)))
        else:
            lead = quarter
            late = k - lead
            inside = jnp.where(
                late < 0, peers - 1 - k, jnp.where(late < half - 1, half - 1 - late, peers - 1 - lead - (late - half + 1))
            )
        return flip(me, jnp.where(inner == 1, inside, outer), bits)

    def remote(src, dst, ssem, rsem, to):
        return pltpu.make_async_remote_copy(
            src_ref=src, dst_ref=dst, send_sem=ssem, recv_sem=rsem, device_id={AXIS: to}, device_id_type=MESH
        )

    def far_out(layer, to):
        return remote(send_buf.at[layer, to], far.at[layer, me], far_send.at[layer, to], far_recv.at[layer, me], to)

    def far_in(layer, source):
        return remote(
            send_buf.at[layer, source], far.at[layer, source], far_send.at[layer, source], far_recv.at[layer, source], source
        )

    def sum_out(layer, to):
        return remote(sum_send.at[layer], sums.at[layer, me], sum_ssem.at[layer, to], sum_rsem.at[layer, me], to)

    def sum_in(layer, source):
        return remote(sum_send.at[layer], sums.at[layer, source], sum_ssem.at[layer, source], sum_rsem.at[layer, source], source)

    def halo_copy(layer, side, to):
        return remote(
            halo_send.at[layer, side], halo.at[layer, 1 - side], halo_ssem.at[layer, side], halo_rsem.at[layer, 1 - side], to
        )

    middle_side = [jnp.where(me == half, 1, 0), jnp.where(me == half - 1, 1, 0)]
    middle = middle_side[0] + middle_side[1]

    def halo_each(act, across=None):
        for side in range(2):
            there = me > 0 if side == 0 else me < peers - 1
            if across is not None:
                there = there & (middle_side[side] == across)

            @pl.when(there)
            def _(side=side):
                act(side, me - 1 if side == 0 else me + 1)

    load_x = pltpu.make_async_copy(x_hbm, x_ref, x_sem)
    load_x.start()
    barrier = pltpu.get_barrier_semaphore()

    def greet(k, carry):
        pl.semaphore_signal(barrier, inc=1, device_id={AXIS: lax.rem(me + k, peers)}, device_id_type=MESH)
        return carry

    lax.fori_loop(1, peers, greet, 0)
    loads = []
    for layer in range(layers):
        for n, (src, dst) in enumerate(
            ((wk_hbm, wk), (wv_hbm, wv), (wm_hbm, wm), (wq_hbm, wq), (wo_hbm, wo), (wu_hbm, wu), (wd_hbm, wd))
        ):
            loads.append(pltpu.make_async_copy(src.at[layer], dst.at[layer], w_sem.at[layer, n]))
    total_ref[0:1, :] = jnp.zeros((1, width), F32)
    load_x.wait()
    for load in loads:
        load.start()

    def first(i, carry):
        x = x_ref[pl.ds(i * group, group)].reshape(rows, width).astype(F32)
        total_ref[0:1, :] = total_ref[0:1, :] + jnp.sum(x, axis=0, keepdims=True)
        fresh = normalize(x, gains_ref[0, 0:1, :]).astype(BF16)
        normed[0, pl.ds(i * group, group)] = fresh.reshape(group, block, width)
        return carry

    lax.fori_loop(0, steps, first, 0)

    def stage(layer, to):
        for slot in range(slots):
            at = send_sm[to * slots + slot]
            if layer > 0:
                at = pos_sm[at]
            send_buf[layer, to, pl.ds(slot * block, block), :] = normed[layer, at]

    def stage_self(layer):
        for slot in range(slots):
            at = send_sm[me * slots + slot]
            if layer > 0:
                at = pos_sm[at]
            far[layer, me, pl.ds(slot * block, block), :] = normed[layer, at]

    def stage_halo(layer, side):
        for b in range(HALO_B):
            at = b if side == 0 else blocks - HALO_B + b
            if layer > 0:
                at = pos_sm[at]
            halo_send[layer, side, pl.ds(b * block, block), :] = normed[layer, at]

    def send_halo(layer, across=None):
        halo_each(lambda side, to: stage_halo(layer, side), across)
        halo_each(lambda side, to: halo_copy(layer, side, to).start(), across)

    def stage_sum(layer):
        for k in range(width // 128):
            part = total_ref[0:1, k * 128 : (k + 1) * 128]
            sum_send[layer, k : k + 1, :] = part
            sums[layer, me, k : k + 1, :] = part

    def send_sum(layer):
        def one(k, carry):
            sum_out(layer, lax.rem(me + k, peers)).start()
            return carry

        lax.fori_loop(1, peers, one, 0)

    def stage_all(k, carry):
        stage(0, order(0, k))
        return carry

    def send_all(k, carry):
        far_out(0, order(0, k)).start()
        return carry

    stage_sum(0)
    lax.fori_loop(0, peers - 1, stage_all, 0)
    pl.semaphore_wait(barrier, peers - 1)
    send_halo(0)
    send_sum(0)
    lax.fori_loop(0, peers - 1, send_all, 0)
    stage_self(0)

    uses = [jnp.int32(peers * slots + n) for n in range(blocks)]
    for k in range(peers - 2, -1, -1):
        to = order(1, jnp.int32(k))
        for slot in range(slots - 1, -1, -1):
            b = send_sm[to * slots + slot]
            uses = [use + equal(b, n) * (k * slots + slot - use) for n, use in enumerate(uses)]
    for n in range(HALO_B):
        low, high = n, blocks - HALO_B + n
        uses[low] = uses[low] - middle_side[0] * 2 * peers * slots
        uses[high] = uses[high] - middle_side[1] * 2 * peers * slots
    places = []
    for n in range(blocks):
        place = jnp.int32(0)
        for other in range(blocks):
            if other != n:
                place = place + below(uses[other], uses[n])
        places.append(place)
        pos_sm[n] = place
    for n in range(blocks):
        which = jnp.int32(0)
        for b in range(blocks):
            which = which + equal(places[b], n) * b
        perm_sm[n] = which
    count_w = 7

    def use(layer, names):
        for n in names:
            loads[layer * count_w + n].wait()

    def project(layer, piece, at):
        count = piece.shape[0]
        flat = piece.reshape(count * block, width)
        keys[pl.ds(at, count)] = dot(flat, wk[layer]).astype(BF16).reshape(count, block, width)
        turned = dot(wv[layer], flat, ((0,), (1,))).astype(BF16)
        for n in range(count):
            values[at + n] = turned[:, n * block : (n + 1) * block]

    def export(at, count, n):
        part = pl.ds(at, count)
        return (
            pltpu.make_async_copy(keys.at[part], keys_out.at[part], table_sem.at[0, n]),
            pltpu.make_async_copy(values.at[part], values_out.at[part], table_sem.at[1, n]),
        )

    chunk = math.gcd(blocks, 4)
    many = math.gcd(quarter, 4)
    first_far = blocks // chunk + 2

    def hand_on(layer, at, count, n):
        if layer == layers - 1:
            for copy in export(at, count, n):
                copy.start()

    def gather(layer):
        def own_piece(i, carry):
            if layer == 0:
                piece = normed[layer, pl.ds(i * chunk, chunk)]
            else:
                piece = jnp.concatenate([normed[layer, pos_sm[i * chunk + n]] for n in range(chunk)], axis=0)
                piece = piece.reshape(chunk, block, width)
            project(layer, piece, HALO_B + i * chunk)
            hand_on(layer, HALO_B + i * chunk, chunk, i)
            return carry

        lax.fori_loop(0, blocks // chunk, own_piece, 0)

        def halo_in(copy, side):
            copy.wait_recv()
            at = 0 if side == 0 else HALO_B + blocks
            project(layer, halo[layer, side].reshape(HALO_B, block, width), at)
            hand_on(layer, at, HALO_B, blocks // chunk + side)

        @pl.when(me > 0)
        def _():
            halo_in(halo_copy(layer, 1, me - 1), 0)

        @pl.when(me < peers - 1)
        def _():
            halo_in(halo_copy(layer, 0, me + 1), 1)

        if layer == layers - 1:
            lax.fori_loop(0, steps, early_step, 0)
            drain(0)
        for inside, outside in ((2, 0), (0, 1), (1, 3), (3, 2)):
            part = flip(lax.div(me, jnp.int32(quarter)), jnp.where(inner == 1, inside, outside), 2) * quarter

            def wait_one(n, carry, part=part):
                source = part + n

                @pl.when(source != me)
                def _():
                    far_in(layer, source).wait_recv()

                return carry

            def far_piece(i, carry, part=part):
                source = part + i * many
                lax.fori_loop(i * many, (i + 1) * many, wait_one, 0)
                piece = far[layer, pl.ds(source, many)].reshape(many * slots, block, width)
                project(layer, piece, near + source * slots)
                hand_on(layer, near + source * slots, many * slots, first_far + lax.div(source, jnp.int32(many)))
                return carry

            lax.fori_loop(0, quarter // many, far_piece, 0)

        def sum_wait(k, carry):
            sum_in(layer, lax.rem(me + k, peers)).wait_recv()
            return carry

        lax.fori_loop(1, peers, sum_wait, 0)
        whole = jnp.sum(sums[layer], axis=0)
        mean = jnp.concatenate([whole[k : k + 1, :] for k in range(width // 128)], axis=1) / node_total
        mean = jnp.broadcast_to(mean, (16, width)).astype(BF16)
        virtual[...] = dot(mean, wm[layer])

    def attend_in(layer, which, queries, at):
        count = count_sm[which]
        home = table_sm[which, 0]
        spots = []
        for j in range(listed):
            entry = table_sm[which, j]
            if 2 * j >= listed:
                entry = home + below(j, count) * (entry - home)
            spots.append(entry)
        attend(
            count,
            lambda j, pair: keys[spots[j], :, pair],
            lambda j, pair: values[spots[j], pair],
            lambda part: queries[part, at : at + block],
            context,
            at,
            listed,
            head,
            block,
        )

    def early_copies(i):
        at = pl.ds(i * group, group)
        return (
            pltpu.make_async_copy(asked.at[at], queries_out.at[at], early_sem.at[0, i]),
            pltpu.make_async_copy(arranged.at[at], latent_out.at[at], early_sem.at[1, i]),
        )

    def block_step(layer, i):
        last = layer == layers - 1
        order_at = [i * group + g for g in range(group)]
        if last:
            which = order_at
            source = [pos_sm[w] for w in which]
            for w, s in zip(which, source):
                arranged[w] = latent[s]
        else:
            which = [perm_sm[n] for n in order_at]
            source = which
        mine = jnp.concatenate([normed[layer, s] for s in source], axis=0)
        queries = dot(wq[layer], mine, ((0,), (1,))).astype(BF16)
        if last:
            for g in range(group):
                asked[which[g]] = queries[:, g * block : (g + 1) * block]
        for g in range(group):
            attend_in(layer, which[g], queries, g * block)
        current = latent if layer > 0 else x_ref
        x = jnp.concatenate([current[s] for s in source], axis=0).astype(F32)
        result = feed(x, context[...], wo[layer], wu.at[layer], wd.at[layer], gains_ref, layer)
        at = pl.ds(i * group, group)
        if last:
            early[at] = result.reshape(group, block, width)
            for copy in early_copies(i):
                copy.start()
        else:
            result = (result + virtual[0:1, :]).astype(BF16)
            latent[at] = result.reshape(group, block, width)
            wide = result.astype(F32)
            fresh = normalize(wide, gains_ref[layer + 1, 0:1, :]).astype(BF16)
            normed[layer + 1, at] = fresh.reshape(group, block, width)
            total_ref[0:1, :] = total_ref[0:1, :] + jnp.sum(wide, axis=0, keepdims=True)

    def early_step(i, carry):
        block_step(layers - 1, i)
        return carry

    def drain(layer):
        def one(k, carry):
            to = lax.rem(me + k, peers)
            far_out(layer, to).wait_send()
            sum_out(layer, to).wait_send()
            return carry

        lax.fori_loop(1, peers, one, 0)
        halo_each(lambda side, to: halo_copy(layer, side, to).wait_send())

    use(0, range(3))
    gather(0)
    use(0, range(3, count_w))
    total_ref[0:1, :] = jnp.zeros((1, width), F32)

    def sending_step(i, carry):
        block_step(0, i)

        @pl.when(i == 0)
        def _():
            send_halo(1, 1)

        @pl.when(i == steps - 1)
        def _():
            stage_sum(1)
            send_halo(1, 0)
            send_sum(1)

        held = HALO_B * middle
        begin = jnp.maximum(i * group - held, 0)
        end = (i + 1) * group - held
        def each(k, carry):
            stage(1, order(1, k))
            return carry

        def go(k, carry):
            far_out(1, order(1, k)).start()
            return carry

        lax.fori_loop(begin, end, each, 0)
        lax.fori_loop(begin, end, go, 0)
        return carry

    def rest(k, carry):
        stage(1, order(1, k))
        return carry

    def go_rest(k, carry):
        far_out(1, order(1, k)).start()
        return carry

    lax.fori_loop(0, steps, sending_step, 0)
    lax.fori_loop(blocks - HALO_B * middle, peers - 1, rest, 0)
    lax.fori_loop(blocks - HALO_B * middle, peers - 1, go_rest, 0)
    stage_self(1)

    use(1, range(count_w))
    gather(1)
    virtual_ref[...] = virtual[...]
    settled = pltpu.make_async_copy(latent, settled_out, x_sem)

    def settle(b, carry):
        latent[b] = (early[b] + virtual[0:1, :]).astype(BF16)
        return carry

    lax.fori_loop(0, blocks, settle, 0)
    settled.start()
    drain(1)

    def await_own(n, carry):
        for copy in export(HALO_B + n * chunk, chunk, n):
            copy.wait()
        return carry

    def await_far(n, carry):
        for copy in export(near + n * many * slots, many * slots, first_far + n):
            copy.wait()
        return carry

    def await_early(n, carry):
        for copy in early_copies(n):
            copy.wait()
        return carry

    @pl.when(me > 0)
    def _():
        for copy in export(0, HALO_B, blocks // chunk):
            copy.wait()

    @pl.when(me < peers - 1)
    def _():
        for copy in export(HALO_B + blocks, HALO_B, blocks // chunk + 1):
            copy.wait()

    lax.fori_loop(0, blocks // chunk, await_own, 0)
    lax.fori_loop(0, peers // many, await_far, 0)
    lax.fori_loop(0, steps, await_early, 0)
    settled.wait()


def finish_kernel(layer, near, group, table_sm, count_sm, gains_ref, virtual_ref, settled_hbm, keys_hbm, values_hbm,
                  queries_hbm, latent_hbm, wo_hbm, wu_hbm, wd_hbm, out_hbm, kept_keys, kept_values, asked, current, fresh,
                  context, kept, wo, wu, wd, todo_sm, away_sm, w_sem, key_sem, value_sem, row_sem, out_sem,
                  kept_sem, keep_sem):
    blocks = table_sm.shape[0]
    block, width = current.shape[1:]
    listed = table_sm.shape[1]
    head = width // HEADS
    weight_loads = [
        pltpu.make_async_copy(src.at[layer], dst, w_sem.at[n])
        for n, (src, dst) in enumerate(((wo_hbm, wo), (wu_hbm, wu), (wd_hbm, wd)))
    ]
    number = jnp.int32(0)
    for b in range(blocks):
        away = jnp.int32(0)
        for j in range(listed):
            away = jnp.where((j < count_sm[b]) & (table_sm[b, j] >= near), 1, away)

        @pl.when(away > 0)
        def _(b=b, number=number):
            todo_sm[number] = b

        away_sm[b] = away
        number = number + away

    load_kept = pltpu.make_async_copy(settled_hbm, kept, kept_sem)

    def keep(b, act):
        @pl.when(away_sm[b] == 0)
        def _():
            act(pltpu.make_async_copy(kept.at[b], out_hbm.at[b], keep_sem.at[b]))

    def block_of(i, g):
        return todo_sm[jnp.minimum(i * group + g, number - 1)]

    def fetch(i, g, act):
        which = block_of(i, g)
        act(pltpu.make_async_copy(queries_hbm.at[which], asked.at[g], row_sem.at[0, g]))
        act(pltpu.make_async_copy(latent_hbm.at[which], current.at[g], row_sem.at[1, g]))
        for j in range(listed):
            def one(j=j):
                entry = table_sm[which, j]
                act(pltpu.make_async_copy(keys_hbm.at[entry], kept_keys.at[g, j], key_sem.at[g, j]))
                act(pltpu.make_async_copy(values_hbm.at[entry], kept_values.at[g, j], value_sem.at[g, j]))

            if 2 * j < listed:
                one()
            else:
                pl.when(j < count_sm[which])(one)

    def begin(i):
        for g in range(group):
            fetch(i, g, lambda copy: copy.start())

    def late_step(i, carry):
        pl.when(i > 0)(lambda: begin(i))
        for g in range(group):
            which = block_of(i, g)
            count = count_sm[which]
            fetch(i, g, lambda copy: copy.wait())
            spots = [j * below(j, count) for j in range(listed)]
            attend(
                count,
                lambda j, pair, g=g, spots=spots: kept_keys[g, spots[j], :, pair],
                lambda j, pair, g=g, spots=spots: kept_values[g, spots[j], pair, :],
                lambda part, g=g: asked[g, part, :],
                context,
                g * block,
                listed,
                head,
                block,
            )

        @pl.when(i == 0)
        def _():
            load_kept.wait()
            for b in range(blocks):
                keep(b, lambda copy: copy.start())
            for load in weight_loads:
                load.wait()

        x = current[...].reshape(group * block, width).astype(F32)
        result = feed(x, context[...], wo[...], wu, wd, gains_ref, layer) + virtual_ref[0:1, :]
        fresh[...] = result.astype(BF16).reshape(group, block, width)

        def put(g):
            return pltpu.make_async_copy(fresh.at[g], out_hbm.at[block_of(i, g)], out_sem.at[g])

        for g in range(group):
            pl.when(i * group + g < number)(lambda g=g: put(g).start())
        for g in range(group):
            pl.when(i * group + g < number)(lambda g=g: put(g).wait())
        return carry

    @pl.when(number > 0)
    def _():
        begin(0)
        load_kept.start()
        for load in weight_loads:
            load.start()
        lax.fori_loop(0, (number + group - 1) // group, late_step, 0)

    @pl.when(number == 0)
    def _():
        load_kept.start()
        load_kept.wait()
        for b in range(blocks):
            keep(b, lambda copy: copy.start())

    for b in range(blocks):
        keep(b, lambda copy: copy.wait())


def body(node_features, nbr_table, nbr_count, send_block, w_query, w_key, w_value, w_out, w_up, w_down, w_virtual, gains):
    blocks, listed = nbr_table.shape
    own, width = node_features.shape
    block = own // blocks
    peers = lax.axis_size(AXIS)
    slots = send_block.shape[1]
    layers = w_query.shape[0]
    group = math.gcd(blocks, 4)
    near = 2 * HALO_B + blocks
    entries = near + peers * slots
    shapes = (peers, layers, blocks, block, width, slots, listed, group, own * peers)
    weights = (w_query, w_key, w_value, w_out, w_up, w_down, w_virtual)
    vmem, smem, hbm = (pl.BlockSpec(memory_space=s) for s in (pltpu.VMEM, pltpu.SMEM, pl.ANY))
    dma = pltpu.SemaphoreType.DMA
    shape = jax.ShapeDtypeStruct
    steps = blocks // group
    groups = blocks // math.gcd(blocks, 4) + 2 + peers // math.gcd(peers // 4, 4)
    scratch = [pltpu.VMEM(w.shape, BF16) for w in weights]
    scratch += [
        pltpu.VMEM((blocks, block, width), BF16),
        pltpu.VMEM((layers, blocks, block, width), BF16),
        pltpu.VMEM((blocks, block, width), BF16),
        pltpu.VMEM((entries, block, width), BF16),
        pltpu.VMEM((entries, width, block), BF16),
        pltpu.VMEM((width, group * block), BF16),
        pltpu.VMEM((layers, peers, slots * block, width), BF16),
        pltpu.VMEM((layers, peers, slots * block, width), BF16),
        pltpu.VMEM((layers, 2, HALO_B * block, width), BF16),
        pltpu.VMEM((layers, 2, HALO_B * block, width), BF16),
        pltpu.VMEM((layers, width // 128, 128), F32),
        pltpu.VMEM((layers, peers, width // 128, 128), F32),
        pltpu.VMEM((8, width), F32),
        pltpu.VMEM((blocks, block, width), F32),
        pltpu.VMEM((blocks, width, block), BF16),
        pltpu.VMEM((blocks, block, width), BF16),
        pltpu.VMEM((16, width), F32),
        pltpu.SMEM((blocks,), jnp.int32),
        pltpu.SMEM((blocks,), jnp.int32),
        dma,
        dma((layers, len(weights))),
        dma((layers, peers)),
        dma((layers, peers)),
        dma((layers, 2)),
        dma((layers, 2)),
        dma((layers, peers)),
        dma((layers, peers)),
        dma((2, groups)),
        dma((2, steps)),
    ]
    settled, keys, values, queries, latent, virtual = pl.pallas_call(
        functools.partial(exchange_kernel, shapes),
        out_shape=(
            shape((blocks, block, width), BF16),
            shape((entries, block, width), BF16),
            shape((entries, width, block), BF16),
            shape((blocks, width, block), BF16),
            shape((blocks, block, width), BF16),
            shape((16, width), F32),
        ),
        in_specs=[smem, smem, smem, vmem] + [hbm] * (1 + len(weights)),
        out_specs=(hbm, hbm, hbm, hbm, hbm, vmem),
        scratch_shapes=scratch,
        compiler_params=pltpu.CompilerParams(collective_id=0, has_side_effects=True, vmem_limit_bytes=VMEM_LIMIT),
        name="exchange",
    )(nbr_table, nbr_count, send_block.reshape(-1), gains, node_features.reshape(blocks, block, width), *weights)
    result = pl.pallas_call(
        functools.partial(finish_kernel, layers - 1, near, group),
        out_shape=shape((blocks, block, width), BF16),
        in_specs=[smem, smem, vmem, vmem] + [hbm] * 8,
        out_specs=hbm,
        scratch_shapes=[
            pltpu.VMEM((group, listed, block, width), BF16),
            pltpu.VMEM((group, listed, width, block), BF16),
            pltpu.VMEM((group, width, block), BF16),
            pltpu.VMEM((group, block, width), BF16),
            pltpu.VMEM((group, block, width), BF16),
            pltpu.VMEM((width, group * block), BF16),
            pltpu.VMEM((blocks, block, width), BF16),
            pltpu.VMEM(w_out.shape[1:], BF16),
            pltpu.VMEM(w_up.shape[1:], BF16),
            pltpu.VMEM(w_down.shape[1:], BF16),
            pltpu.SMEM((blocks,), jnp.int32),
            pltpu.SMEM((blocks,), jnp.int32),
            dma((3,)),
            dma((group, listed)),
            dma((group, listed)),
            dma((2, group)),
            dma((group,)),
            dma,
            dma((blocks,)),
        ],
        compiler_params=pltpu.CompilerParams(vmem_limit_bytes=VMEM_LIMIT),
        name="finish",
    )(nbr_table, nbr_count, gains, virtual, settled, keys, values, queries, latent, w_out, w_up, w_down)
    return result.reshape(own, width)


def solution(mesh):
    across = P(("members", "row"), None)
    in_specs = (across, P("row", None), P("row"), P("row", None)) + (P(),) * 8
    return jax.shard_map(body, mesh=mesh, in_specs=in_specs, out_specs=across, check_vma=False)
```

```python
import functools
import math

import jax
import jax.numpy as jnp
from jax import lax
from jax.experimental import pallas as pl
from jax.experimental.pallas import tpu as pltpu
from jax.sharding import PartitionSpec as P

HEADS = 4
HALO_B = 2
VMEM_LIMIT = 67_000_000
MESH = pl.DeviceIdType.MESH
BF16 = jnp.bfloat16
F32 = jnp.float32
AXIS = "row"


def normalize(values, scaling):
    centred = values - jnp.mean(values, axis=-1, keepdims=True)
    spread = jnp.mean(centred * centred, axis=-1, keepdims=True)
    return centred * lax.rsqrt(spread + 1e-05) * scaling


def dot(a, b, contract=((1,), (0,))):
    return lax.dot_general(a, b, (contract, ((), ())), preferred_element_type=F32)


def gelu(x):
    return 0.5 * x * (1.0 + jnp.tanh(math.sqrt(2 / math.pi) * (x + 0.044715 * x * x * x)))


def flip(a, b, bits):
    out = 0
    for bit in range(bits):
        weight = 1 << bit
        x = lax.rem(lax.div(a, jnp.int32(weight)), jnp.int32(2))
        y = lax.rem(lax.div(b, jnp.int32(weight)), jnp.int32(2))
        out = out + weight * lax.rem(x + y, jnp.int32(2))
    return out


def below(a, b):
    return jnp.minimum(jnp.maximum(b - a, 0), 1)


def equal(a, b):
    return 1 - jnp.minimum(jnp.maximum(a - b, b - a), 1)


def attend(count, key_of, value_of, query_of, context, at, listed, head, block):
    scale = math.log2(math.e) / math.sqrt(head)
    dead = [(1 - below(j, count)).astype(F32) * -1e30 for j in range(listed)]
    blank = jnp.zeros((head, block), BF16)
    for h in range(0, HEADS, 2):
        pair = slice(h * head, (h + 2) * head)
        upper = query_of(slice(h * head, (h + 1) * head))
        lower = query_of(slice((h + 1) * head, (h + 2) * head))
        both = jnp.concatenate(
            [jnp.concatenate([upper, blank], axis=1), jnp.concatenate([blank, lower], axis=1)], axis=0
        )
        scores = []
        for j in range(listed):
            s = dot(key_of(j, pair), both)
            scores.append(s if 2 * j < listed else s + dead[j])
        top = jnp.max(functools.reduce(jnp.maximum, scores), axis=0, keepdims=True)
        weights = [jnp.exp2((s - top) * scale) for s in scores]
        inverse = 1.0 / jnp.sum(functools.reduce(jnp.add, weights), axis=0, keepdims=True)
        probs = jnp.concatenate([w.astype(BF16) for w in weights], axis=0)
        mixed = dot(jnp.concatenate([value_of(j, pair) for j in range(listed)], axis=1), probs)
        for n in range(2):
            part = slice(n * block, (n + 1) * block)
            of_head = slice((h + n) * head, (h + n + 1) * head)
            context[of_head, at : at + block] = (mixed[n * head : (n + 1) * head, part] * inverse[:, part]).astype(BF16)


def feed(x, context, wo, wu, wd, gains_ref, layer):
    after_att = x + normalize(dot(context, wo, ((0,), (0,))), gains_ref[layer, 1:2, :])
    middle = normalize(after_att, gains_ref[layer, 2:3, :]).astype(BF16)
    hidden_size = wu.shape[-1]
    part = math.gcd(hidden_size, 512)
    down = None
    for f in range(0, hidden_size, part):
        hidden = gelu(dot(middle, wu[:, f : f + part])).astype(BF16)
        term = dot(hidden, wd[f : f + part, :])
        down = term if down is None else down + term
    return after_att + normalize(down, gains_ref[layer, 3:4, :])


def exchange_kernel(shapes, table_hbm, count_hbm, send_hbm, gains_hbm, x_hbm, wq_hbm, wk_hbm, wv_hbm, wo_hbm, wu_hbm,
                    wd_hbm, wm_hbm, settled_out, keys_out, values_out, queries_out, latent_out, virtual_ref, wq, wk, wv,
                    wo, wu, wd, wm, x_ref, normed, latent, keys, values, context, send_buf, far, halo_send, halo,
                    sum_send, sums, total_ref, early, asked, arranged, virtual, table_sm, count_sm, send_sm,
                    gains_ref, perm_sm, pos_sm, x_sem, small_sem, w_sem, far_send,
                    far_recv, halo_ssem, halo_rsem, sum_ssem, sum_rsem, table_sem, early_sem):
    peers, layers, blocks, block, width, slots, listed, group, node_total = shapes
    near = 2 * HALO_B + blocks
    bits = peers.bit_length() - 1
    half, quarter = peers // 2, peers // 4
    rows = group * block
    steps = blocks // group
    head = width // HEADS
    me = lax.axis_index(AXIS)
    inner = jnp.where((me >= quarter) & (me < half + quarter), 1, 0)

    def order(layer, k):
        outer = jnp.where(k < half, half + k, peers - 1 - k)
        lead = quarter // 2 if layer == 0 else quarter
        late = k - lead
        inside = jnp.where(
            late < 0, peers - 1 - k, jnp.where(late < half - 1, half - 1 - late, peers - 1 - lead - (late - half + 1))
        )
        return flip(me, jnp.where(inner == 1, inside, outer), bits)

    def remote(src, dst, ssem, rsem, to):
        return pltpu.make_async_remote_copy(
            src_ref=src, dst_ref=dst, send_sem=ssem, recv_sem=rsem, device_id={AXIS: to}, device_id_type=MESH
        )

    my_part = lax.div(me, jnp.int32(quarter))

    def far_out(layer, to):
        return remote(send_buf.at[layer, to], far.at[layer, me], far_send.at[layer], far_recv.at[layer, my_part], to)

    def far_some(layer, start, count, part):
        some = pl.ds(start, count)
        return remote(send_buf.at[layer, some], far.at[layer, some], far_send.at[layer], far_recv.at[layer, part], me)

    def sum_out(layer, to):
        return remote(sum_send.at[layer], sums.at[layer, me], sum_ssem.at[layer], sum_rsem.at[layer], to)

    def sum_all(layer):
        some = sums.at[layer, pl.ds(0, peers - 1)]
        return remote(some, some, sum_ssem.at[layer], sum_rsem.at[layer], me)

    def halo_copy(layer, side, to):
        return remote(
            halo_send.at[layer, side], halo.at[layer, 1 - side], halo_ssem.at[layer, side], halo_rsem.at[layer, 1 - side], to
        )

    middle_side = [jnp.where(me == half, 1, 0), jnp.where(me == half - 1, 1, 0)]
    middle = middle_side[0] + middle_side[1]

    def halo_each(act, across=None):
        for side in range(2):
            there = me > 0 if side == 0 else me < peers - 1
            if across is not None:
                there = there & (middle_side[side] == across)

            @pl.when(there)
            def _(side=side):
                act(side, me - 1 if side == 0 else me + 1)

    load_x = pltpu.make_async_copy(x_hbm, x_ref, x_sem)
    load_x.start()
    smalls = [
        pltpu.make_async_copy(src, dst, small_sem.at[n])
        for n, (src, dst) in enumerate(
            ((gains_hbm, gains_ref), (send_hbm, send_sm), (table_hbm, table_sm), (count_hbm, count_sm))
        )
    ]
    for small in smalls:
        small.start()
    barrier = pltpu.get_barrier_semaphore()

    def greet(k, carry):
        pl.semaphore_signal(barrier, inc=1, device_id={AXIS: lax.rem(me + k, peers)}, device_id_type=MESH)
        return carry

    lax.fori_loop(1, peers, greet, 0)
    loads = []
    for n, (src, dst) in enumerate(
        ((wk_hbm, wk), (wv_hbm, wv), (wm_hbm, wm), (wq_hbm, wq), (wo_hbm, wo), (wu_hbm, wu), (wd_hbm, wd))
    ):
        loads.append(pltpu.make_async_copy(src, dst, w_sem.at[n]))
    total_ref[0:1, :] = jnp.zeros((1, width), F32)
    load_x.wait()
    for small in smalls:
        small.wait()
    for load in loads:
        load.start()

    def first(i, carry):
        x = x_ref[pl.ds(i * group, group)].reshape(rows, width).astype(F32)
        total_ref[0:1, :] = total_ref[0:1, :] + jnp.sum(x, axis=0, keepdims=True)
        fresh = normalize(x, gains_ref[0, 0:1, :]).astype(BF16)
        normed[0, pl.ds(i * group, group)] = fresh.reshape(group, block, width)
        return carry

    lax.fori_loop(0, steps, first, 0)

    def stage(layer, to):
        for slot in range(slots):
            at = send_sm[to * slots + slot]
            if layer > 0:
                at = pos_sm[at]
            send_buf[layer, to, pl.ds(slot * block, block), :] = normed[layer, at]

    def stage_self(layer):
        for slot in range(slots):
            at = send_sm[me * slots + slot]
            if layer > 0:
                at = pos_sm[at]
            far[layer, me, pl.ds(slot * block, block), :] = normed[layer, at]

    def stage_halo(layer, side):
        for b in range(HALO_B):
            at = b if side == 0 else blocks - HALO_B + b
            if layer > 0:
                at = pos_sm[at]
            halo_send[layer, side, pl.ds(b * block, block), :] = normed[layer, at]

    def send_halo(layer, across=None):
        halo_each(lambda side, to: stage_halo(layer, side), across)
        halo_each(lambda side, to: halo_copy(layer, side, to).start(), across)

    def stage_sum(layer):
        for k in range(width // 128):
            part = total_ref[0:1, k * 128 : (k + 1) * 128]
            sum_send[layer, k : k + 1, :] = part
            sums[layer, me, k : k + 1, :] = part

    def send_sum(layer):
        def one(k, carry):
            sum_out(layer, lax.rem(me + k, peers)).start()
            return carry

        lax.fori_loop(1, peers, one, 0)

    def stage_all(k, carry):
        stage(0, order(0, k))
        return carry

    def send_all(k, carry):
        far_out(0, order(0, k)).start()
        return carry

    stage_sum(0)
    lax.fori_loop(0, peers - 1, stage_all, 0)
    pl.semaphore_wait(barrier, peers - 1)
    send_halo(0)
    send_sum(0)
    lax.fori_loop(0, peers - 1, send_all, 0)
    stage_self(0)

    uses = [jnp.int32(peers * slots + n) for n in range(blocks)]
    for k in range(peers - 2, -1, -1):
        to = order(1, jnp.int32(k))
        for slot in range(slots - 1, -1, -1):
            b = send_sm[to * slots + slot]
            uses = [use + equal(b, n) * (k * slots + slot - use) for n, use in enumerate(uses)]
    for n in range(HALO_B):
        low, high = n, blocks - HALO_B + n
        uses[low] = uses[low] - middle_side[0] * 2 * peers * slots
        uses[high] = uses[high] - middle_side[1] * 2 * peers * slots
    places = []
    for n in range(blocks):
        place = jnp.int32(0)
        for other in range(blocks):
            if other != n:
                place = place + below(uses[other], uses[n])
        places.append(place)
        pos_sm[n] = place
    for n in range(blocks):
        which = jnp.int32(0)
        for b in range(blocks):
            which = which + equal(places[b], n) * b
        perm_sm[n] = which
    def project(layer, piece, at):
        count = piece.shape[0]
        flat = piece.reshape(count * block, width)
        keys[pl.ds(at, count)] = dot(flat, wk[layer]).astype(BF16).reshape(count, block, width)
        turned = dot(wv[layer], flat, ((0,), (1,))).astype(BF16)
        for n in range(count):
            values[at + n] = turned[:, n * block : (n + 1) * block]

    def export(at, count, n):
        part = pl.ds(at, count)
        return (
            pltpu.make_async_copy(keys.at[part], keys_out.at[part], table_sem.at[0, n]),
            pltpu.make_async_copy(values.at[part], values_out.at[part], table_sem.at[1, n]),
        )

    chunk = math.gcd(blocks, 4)
    many = math.gcd(quarter, 4)

    def hand_on(layer, at, count, n):
        if layer == layers - 1:
            for copy in export(at, count, n):
                copy.start()

    def gather(layer):
        def own_piece(i, carry):
            if layer == 0:
                piece = normed[layer, pl.ds(i * chunk, chunk)]
            else:
                piece = jnp.concatenate([normed[layer, pos_sm[i * chunk + n]] for n in range(chunk)], axis=0)
                piece = piece.reshape(chunk, block, width)
            project(layer, piece, HALO_B + i * chunk)
            hand_on(layer, HALO_B + i * chunk, chunk, 0)
            return carry

        lax.fori_loop(0, blocks // chunk, own_piece, 0)

        def halo_in(copy, side):
            copy.wait_recv()
            at = 0 if side == 0 else HALO_B + blocks
            project(layer, halo[layer, side].reshape(HALO_B, block, width), at)
            hand_on(layer, at, HALO_B, 2 + side)

        @pl.when(me > 0)
        def _():
            halo_in(halo_copy(layer, 1, me - 1), 0)

        @pl.when(me < peers - 1)
        def _():
            halo_in(halo_copy(layer, 0, me + 1), 1)

        if layer == layers - 1:
            lax.fori_loop(0, steps, early_step, 0)
            drain(0)
        for n, (inside, outside) in enumerate(((2, 0), (0, 1), (1, 3), (3, 2))):
            if n == 3:
                sum_all(layer).wait_recv()
                whole = jnp.sum(sums[layer], axis=0)
                mean = jnp.concatenate([whole[k : k + 1, :] for k in range(width // 128)], axis=1) / node_total
                mean = jnp.broadcast_to(mean, (16, width)).astype(BF16)
                virtual[...] = dot(mean, wm[layer])
                if layer == layers - 1:
                    virtual_ref[...] = virtual[...]
                    lax.fori_loop(0, blocks, settle, 0)
                    settled.start()
            part = flip(my_part, jnp.where(inner == 1, inside, outside), 2)
            start = part * quarter

            @pl.when(part == my_part)
            def _(part=part, start=start):
                far_some(layer, start, quarter - 1, part).wait_recv()

            @pl.when(part != my_part)
            def _(part=part, start=start):
                far_some(layer, start, quarter, part).wait_recv()

            def far_piece(i, carry, start=start):
                source = start + i * many
                piece = far[layer, pl.ds(source, many)].reshape(many * slots, block, width)
                project(layer, piece, near + source * slots)
                hand_on(layer, near + source * slots, many * slots, 1)
                return carry

            lax.fori_loop(0, quarter // many, far_piece, 0)

    def attend_in(layer, which, queries, at):
        count = count_sm[which]
        home = table_sm[which, 0]
        spots = []
        for j in range(listed):
            entry = table_sm[which, j]
            if 2 * j >= listed:
                entry = home + below(j, count) * (entry - home)
            spots.append(entry)
        attend(
            count,
            lambda j, pair: keys[spots[j], :, pair],
            lambda j, pair: values[spots[j], pair],
            lambda part: queries[part, at : at + block],
            context,
            at,
            listed,
            head,
            block,
        )

    def early_copies(start, count):
        at = pl.ds(start, count)
        return (
            pltpu.make_async_copy(asked.at[at], queries_out.at[at], early_sem.at[0]),
            pltpu.make_async_copy(arranged.at[at], latent_out.at[at], early_sem.at[1]),
        )

    def block_step(layer, i):
        last = layer == layers - 1
        order_at = [i * group + g for g in range(group)]
        if last:
            which = order_at
            source = [pos_sm[w] for w in which]
            for w, s in zip(which, source):
                arranged[w] = latent[s]
        else:
            which = [perm_sm[n] for n in order_at]
            source = which
        mine = jnp.concatenate([normed[layer, s] for s in source], axis=0)
        queries = dot(wq[layer], mine, ((0,), (1,))).astype(BF16)
        if last:
            for g in range(group):
                asked[which[g]] = queries[:, g * block : (g + 1) * block]
        for g in range(group):
            attend_in(layer, which[g], queries, g * block)
        current = latent if layer > 0 else x_ref
        x = jnp.concatenate([current[s] for s in source], axis=0).astype(F32)
        result = feed(x, context[...], wo[layer], wu.at[layer], wd.at[layer], gains_ref, layer)
        at = pl.ds(i * group, group)
        if last:
            early[at] = result.reshape(group, block, width)
            for copy in early_copies(i * group, group):
                copy.start()
        else:
            result = (result + virtual[0:1, :]).astype(BF16)
            latent[at] = result.reshape(group, block, width)
            wide = result.astype(F32)
            fresh = normalize(wide, gains_ref[layer + 1, 0:1, :]).astype(BF16)
            normed[layer + 1, at] = fresh.reshape(group, block, width)
            total_ref[0:1, :] = total_ref[0:1, :] + jnp.sum(wide, axis=0, keepdims=True)

    def early_step(i, carry):
        block_step(layers - 1, i)
        return carry

    def drain(layer):
        far_some(layer, 0, peers - 1, my_part).wait_send()
        sum_all(layer).wait_send()
        halo_each(lambda side, to: halo_copy(layer, side, to).wait_send())

    settled = pltpu.make_async_copy(latent, settled_out, x_sem)

    def settle(b, carry):
        latent[b] = (early[b] + virtual[0:1, :]).astype(BF16)
        return carry

    for load in loads[:3]:
        load.wait()
    gather(0)
    for load in loads[3:]:
        load.wait()
    total_ref[0:1, :] = jnp.zeros((1, width), F32)

    def sending_step(i, carry):
        block_step(0, i)

        @pl.when(i == 0)
        def _():
            send_halo(1, 1)

        @pl.when(i == steps - 1)
        def _():
            stage_sum(1)
            send_halo(1, 0)
            send_sum(1)

        held = HALO_B * middle
        begin = jnp.maximum(i * group - held, 0)
        end = (i + 1) * group - held
        def each(k, carry):
            stage(1, order(1, k))
            return carry

        def go(k, carry):
            far_out(1, order(1, k)).start()
            return carry

        lax.fori_loop(begin, end, each, 0)
        lax.fori_loop(begin, end, go, 0)
        return carry

    def rest(k, carry):
        stage(1, order(1, k))
        return carry

    def go_rest(k, carry):
        far_out(1, order(1, k)).start()
        return carry

    lax.fori_loop(0, steps, sending_step, 0)
    lax.fori_loop(blocks - HALO_B * middle, peers - 1, rest, 0)
    lax.fori_loop(blocks - HALO_B * middle, peers - 1, go_rest, 0)
    stage_self(1)

    gather(1)
    drain(1)
    for start, count, n in ((HALO_B, blocks, 0), (near, peers * slots, 1)):
        for copy in export(start, count, n):
            copy.wait()

    @pl.when(me > 0)
    def _():
        for copy in export(0, HALO_B, 2):
            copy.wait()

    @pl.when(me < peers - 1)
    def _():
        for copy in export(HALO_B + blocks, HALO_B, 3):
            copy.wait()

    for copy in early_copies(0, blocks):
        copy.wait()
    settled.wait()


def finish_kernel(layer, near, group, table_sm, count_sm, gains_ref, virtual_ref, settled_hbm, keys_hbm, values_hbm,
                  queries_hbm, latent_hbm, wo_hbm, wu_hbm, wd_hbm, out_hbm, kept_keys, kept_values, asked, current, context,
                  kept, wo, wu, wd, todo_sm, w_sem, key_sem, value_sem, row_sem, kept_sem):
    blocks, block, width = kept.shape
    listed = table_sm.shape[1]
    head = width // HEADS
    weight_loads = [
        pltpu.make_async_copy(src.at[layer], dst, w_sem.at[n])
        for n, (src, dst) in enumerate(((wo_hbm, wo), (wu_hbm, wu), (wd_hbm, wd)))
    ]
    number = jnp.int32(0)
    for b in range(blocks):
        away = jnp.int32(0)
        for j in range(listed):
            away = jnp.where((j < count_sm[b]) & (table_sm[b, j] >= near), 1, away)

        @pl.when(away > 0)
        def _(b=b, number=number):
            todo_sm[number] = b

        number = number + away

    def block_of(i, g):
        return todo_sm[jnp.minimum(i * group + g, number - 1)]

    def rows(which, g):
        return (
            pltpu.make_async_copy(queries_hbm.at[which], asked.at[g], row_sem.at[0, g]),
            pltpu.make_async_copy(latent_hbm.at[which], current.at[g], row_sem.at[1, g]),
        )

    def fetch(i, g):
        which = block_of(i, g)
        for copy in rows(which, g):
            copy.start()
        for j in range(listed):
            entry = table_sm[which, j * below(j, count_sm[which])]
            pltpu.make_async_copy(keys_hbm.at[entry], kept_keys.at[g, j], key_sem.at[g]).start()
            pltpu.make_async_copy(values_hbm.at[entry], kept_values.at[g, j], value_sem.at[g]).start()

    def fetched(i, g):
        for copy in rows(block_of(i, g), g):
            copy.wait()
        some = pl.ds(0, listed)
        pltpu.make_async_copy(keys_hbm.at[some], kept_keys.at[g], key_sem.at[g]).wait()
        pltpu.make_async_copy(values_hbm.at[some], kept_values.at[g], value_sem.at[g]).wait()

    def each_live(i, act):
        for g in range(group):
            pl.when(i * group + g < number)(lambda g=g: act(i, g))

    def late_step(i, carry):
        pl.when(i > 0)(lambda: each_live(i, fetch))
        each_live(i, fetched)
        for g in range(group):
            attend(
                count_sm[block_of(i, g)],
                lambda j, pair, g=g: kept_keys[g, j, :, pair],
                lambda j, pair, g=g: kept_values[g, j, pair, :],
                lambda part, g=g: asked[g, part, :],
                context,
                g * block,
                listed,
                head,
                block,
            )

        @pl.when(i == 0)
        def _():
            for load in weight_loads:
                load.wait()
            load_kept.wait()

        x = current[...].reshape(group * block, width).astype(F32)
        result = feed(x, context[...], wo[...], wu, wd, gains_ref, layer) + virtual_ref[0:1, :]
        result = result.astype(BF16).reshape(group, block, width)

        def put(i, g):
            kept[block_of(i, g)] = result[g]

        each_live(i, put)
        return carry

    load_kept = pltpu.make_async_copy(settled_hbm, kept, kept_sem)

    @pl.when(number > 0)
    def _():
        each_live(0, fetch)
        for load in weight_loads:
            load.start()
        load_kept.start()
        lax.fori_loop(0, (number + group - 1) // group, late_step, 0)

    @pl.when(number == 0)
    def _():
        load_kept.start()
        load_kept.wait()

    give = pltpu.make_async_copy(kept, out_hbm, kept_sem)
    give.start()
    give.wait()


def body(node_features, nbr_table, nbr_count, send_block, w_query, w_key, w_value, w_out, w_up, w_down, w_virtual, gains):
    blocks, listed = nbr_table.shape
    own, width = node_features.shape
    block = own // blocks
    peers = lax.axis_size(AXIS)
    slots = send_block.shape[1]
    layers = w_query.shape[0]
    group = math.gcd(blocks, 4)
    near = 2 * HALO_B + blocks
    entries = near + peers * slots
    shapes = (peers, layers, blocks, block, width, slots, listed, group, own * peers)
    weights = (w_query, w_key, w_value, w_out, w_up, w_down, w_virtual)
    vmem, smem, hbm = (pl.BlockSpec(memory_space=s) for s in (pltpu.VMEM, pltpu.SMEM, pl.ANY))
    dma = pltpu.SemaphoreType.DMA
    shape = jax.ShapeDtypeStruct
    scratch = [pltpu.VMEM(w.shape, BF16) for w in weights]
    scratch += [
        pltpu.VMEM((blocks, block, width), BF16),
        pltpu.VMEM((layers, blocks, block, width), BF16),
        pltpu.VMEM((blocks, block, width), BF16),
        pltpu.VMEM((entries, block, width), BF16),
        pltpu.VMEM((entries, width, block), BF16),
        pltpu.VMEM((width, group * block), BF16),
        pltpu.VMEM((layers, peers, slots * block, width), BF16),
        pltpu.VMEM((layers, peers, slots * block, width), BF16),
        pltpu.VMEM((layers, 2, HALO_B * block, width), BF16),
        pltpu.VMEM((layers, 2, HALO_B * block, width), BF16),
        pltpu.VMEM((layers, width // 128, 128), F32),
        pltpu.VMEM((layers, peers, width // 128, 128), F32),
        pltpu.VMEM((8, width), F32),
        pltpu.VMEM((blocks, block, width), F32),
        pltpu.VMEM((blocks, width, block), BF16),
        pltpu.VMEM((blocks, block, width), BF16),
        pltpu.VMEM((16, width), F32),
        pltpu.SMEM(nbr_table.shape, jnp.int32),
        pltpu.SMEM(nbr_count.shape, jnp.int32),
        pltpu.SMEM((peers * slots,), jnp.int32),
        pltpu.VMEM(gains.shape, F32),
        pltpu.SMEM((blocks,), jnp.int32),
        pltpu.SMEM((blocks,), jnp.int32),
        dma,
        dma((4,)),
        dma((len(weights),)),
        dma((layers,)),
        dma((layers, 4)),
        dma((layers, 2)),
        dma((layers, 2)),
        dma((layers,)),
        dma((layers,)),
        dma((2, 4)),
        dma((2,)),
    ]
    settled, keys, values, queries, latent, virtual = pl.pallas_call(
        functools.partial(exchange_kernel, shapes),
        out_shape=(
            shape((blocks, block, width), BF16),
            shape((entries, block, width), BF16),
            shape((entries, width, block), BF16),
            shape((blocks, width, block), BF16),
            shape((blocks, block, width), BF16),
            shape((16, width), F32),
        ),
        in_specs=[hbm] * (5 + len(weights)),
        out_specs=(hbm, hbm, hbm, hbm, hbm, vmem),
        scratch_shapes=scratch,
        compiler_params=pltpu.CompilerParams(collective_id=0, has_side_effects=True, vmem_limit_bytes=VMEM_LIMIT),
        name="exchange",
    )(nbr_table, nbr_count, send_block.reshape(-1), gains, node_features.reshape(blocks, block, width), *weights)
    result = pl.pallas_call(
        functools.partial(finish_kernel, layers - 1, near, group),
        out_shape=shape((blocks, block, width), BF16),
        in_specs=[smem, smem, vmem, vmem] + [hbm] * 8,
        out_specs=hbm,
        scratch_shapes=[
            pltpu.VMEM((group, listed, block, width), BF16),
            pltpu.VMEM((group, listed, width, block), BF16),
            pltpu.VMEM((group, width, block), BF16),
            pltpu.VMEM((group, block, width), BF16),
            pltpu.VMEM((width, group * block), BF16),
            pltpu.VMEM((blocks, block, width), BF16),
            pltpu.VMEM(w_out.shape[1:], BF16),
            pltpu.VMEM(w_up.shape[1:], BF16),
            pltpu.VMEM(w_down.shape[1:], BF16),
            pltpu.SMEM((blocks,), jnp.int32),
            dma((3,)),
            dma((group,)),
            dma((group,)),
            dma((2, group)),
            dma,
        ],
        compiler_params=pltpu.CompilerParams(vmem_limit_bytes=VMEM_LIMIT),
        name="finish",
    )(nbr_table, nbr_count, gains, virtual, settled, keys, values, queries, latent, w_out, w_up, w_down)
    return result.reshape(own, width)


def solution(mesh):
    across = P(("members", "row"), None)
    in_specs = (across, P("row", None), P("row"), P("row", None)) + (P(),) * 8
    return jax.shard_map(body, mesh=mesh, in_specs=in_specs, out_specs=across, check_vma=False)
```

```python
import functools
import math

import jax
import jax.numpy as jnp
from jax import lax
from jax.experimental import pallas as pl
from jax.experimental.pallas import tpu as pltpu
from jax.sharding import PartitionSpec as P

HEADS = 4
HALO_B = 2
VMEM_LIMIT = 67_000_000
MESH = pl.DeviceIdType.MESH
BF16 = jnp.bfloat16
F32 = jnp.float32
AXIS = "row"


def normalize(values, scaling):
    centred = values - jnp.mean(values, axis=-1, keepdims=True)
    spread = jnp.mean(centred * centred, axis=-1, keepdims=True)
    return centred * lax.rsqrt(spread + 1e-05) * scaling


def dot(a, b, contract=((1,), (0,))):
    return lax.dot_general(a, b, (contract, ((), ())), preferred_element_type=F32)


def gelu(x):
    return 0.5 * x * (1.0 + jnp.tanh(math.sqrt(2 / math.pi) * (x + 0.044715 * x * x * x)))


def flip(a, b, bits):
    out = 0
    for bit in range(bits):
        weight = 1 << bit
        x = lax.rem(lax.div(a, jnp.int32(weight)), jnp.int32(2))
        y = lax.rem(lax.div(b, jnp.int32(weight)), jnp.int32(2))
        out = out + weight * lax.rem(x + y, jnp.int32(2))
    return out


def below(a, b):
    return jnp.minimum(jnp.maximum(b - a, 0), 1)


def equal(a, b):
    return 1 - jnp.minimum(jnp.maximum(a - b, b - a), 1)


def attend(count, key_of, value_of, query_of, context, at, listed, head, block):
    scale = math.log2(math.e) / math.sqrt(head)
    dead = [(1 - below(j, count)).astype(F32) * -1e30 for j in range(listed)]
    blank = jnp.zeros((head, block), BF16)
    for h in range(0, HEADS, 2):
        pair = slice(h * head, (h + 2) * head)
        upper = query_of(slice(h * head, (h + 1) * head))
        lower = query_of(slice((h + 1) * head, (h + 2) * head))
        both = jnp.concatenate(
            [jnp.concatenate([upper, blank], axis=1), jnp.concatenate([blank, lower], axis=1)], axis=0
        )
        scores = []
        for j in range(listed):
            s = dot(key_of(j, pair), both)
            scores.append(s if 2 * j < listed else s + dead[j])
        top = jnp.max(functools.reduce(jnp.maximum, scores), axis=0, keepdims=True)
        weights = [jnp.exp2((s - top) * scale) for s in scores]
        inverse = 1.0 / jnp.sum(functools.reduce(jnp.add, weights), axis=0, keepdims=True)
        probs = jnp.concatenate([w.astype(BF16) for w in weights], axis=0)
        mixed = dot(jnp.concatenate([value_of(j, pair) for j in range(listed)], axis=1), probs)
        for n in range(2):
            part = slice(n * block, (n + 1) * block)
            of_head = slice((h + n) * head, (h + n + 1) * head)
            context[of_head, at : at + block] = (mixed[n * head : (n + 1) * head, part] * inverse[:, part]).astype(BF16)


def feed(x, context, wo, wu, wd, gains_ref, layer):
    after_att = x + normalize(dot(context, wo, ((0,), (0,))), gains_ref[layer, 1:2, :])
    middle = normalize(after_att, gains_ref[layer, 2:3, :]).astype(BF16)
    hidden_size = wu.shape[-1]
    part = math.gcd(hidden_size, 512)
    down = None
    for f in range(0, hidden_size, part):
        hidden = gelu(dot(middle, wu[:, f : f + part])).astype(BF16)
        term = dot(hidden, wd[f : f + part, :])
        down = term if down is None else down + term
    return after_att + normalize(down, gains_ref[layer, 3:4, :])


def exchange_kernel(shapes, table_hbm, count_hbm, send_hbm, gains_hbm, x_hbm, wq_hbm, wk_hbm, wv_hbm, wo_hbm, wu_hbm,
                    wd_hbm, wm_hbm, settled_out, keys_out, values_out, queries_out, latent_out, virtual_ref, wq, wk, wv,
                    wo, wu, wd, wm, x_ref, normed, latent, keys, values, context, send_buf, far, halo_send, halo,
                    sum_send, sums, total_ref, early, asked, arranged, virtual, table_sm, count_sm, send_sm,
                    gains_ref, perm_sm, pos_sm, x_sem, small_sem, w_sem, far_send,
                    far_recv, halo_ssem, halo_rsem, sum_ssem, sum_rsem, table_sem, early_sem):
    peers, layers, blocks, block, width, slots, listed, group, node_total = shapes
    near = 2 * HALO_B + blocks
    bits = peers.bit_length() - 1
    half, quarter = peers // 2, peers // 4
    rows = group * block
    steps = blocks // group
    head = width // HEADS
    me = lax.axis_index(AXIS)
    inner = jnp.where((me >= quarter) & (me < half + quarter), 1, 0)

    def order(layer, k):
        outer = jnp.where(k < half, half + k, peers - 1 - k)
        lead = quarter // 2 if layer == 0 else quarter
        late = k - lead
        inside = jnp.where(
            late < 0, peers - 1 - k, jnp.where(late < half - 1, half - 1 - late, peers - 1 - lead - (late - half + 1))
        )
        return flip(me, jnp.where(inner == 1, inside, outer), bits)

    def remote(src, dst, ssem, rsem, to):
        return pltpu.make_async_remote_copy(
            src_ref=src, dst_ref=dst, send_sem=ssem, recv_sem=rsem, device_id={AXIS: to}, device_id_type=MESH
        )

    my_part = lax.div(me, jnp.int32(quarter))

    def far_out(layer, to):
        return remote(send_buf.at[layer, to], far.at[layer, me], far_send.at[layer], far_recv.at[layer, my_part], to)

    def far_some(layer, start, count, part):
        some = pl.ds(start, count)
        return remote(send_buf.at[layer, some], far.at[layer, some], far_send.at[layer], far_recv.at[layer, part], me)

    def sum_out(layer, to):
        return remote(sum_send.at[layer], sums.at[layer, me], sum_ssem.at[layer], sum_rsem.at[layer], to)

    def sum_all(layer):
        some = sums.at[layer, pl.ds(0, peers - 1)]
        return remote(some, some, sum_ssem.at[layer], sum_rsem.at[layer], me)

    def halo_copy(layer, side, to):
        return remote(
            halo_send.at[layer, side], halo.at[layer, 1 - side], halo_ssem.at[layer, side], halo_rsem.at[layer, 1 - side], to
        )

    middle_side = [jnp.where(me == half, 1, 0), jnp.where(me == half - 1, 1, 0)]
    middle = middle_side[0] + middle_side[1]

    def halo_each(act, across=None):
        for side in range(2):
            there = me > 0 if side == 0 else me < peers - 1
            if across is not None:
                there = there & (middle_side[side] == across)

            @pl.when(there)
            def _(side=side):
                act(side, me - 1 if side == 0 else me + 1)

    load_x = pltpu.make_async_copy(x_hbm, x_ref, x_sem)
    load_x.start()
    smalls = [
        pltpu.make_async_copy(src, dst, small_sem.at[n])
        for n, (src, dst) in enumerate(
            ((gains_hbm, gains_ref), (send_hbm, send_sm), (table_hbm, table_sm), (count_hbm, count_sm))
        )
    ]
    for small in smalls:
        small.start()
    barrier = pltpu.get_barrier_semaphore()

    def greet(k, carry):
        pl.semaphore_signal(barrier, inc=1, device_id={AXIS: lax.rem(me + k, peers)}, device_id_type=MESH)
        return carry

    lax.fori_loop(1, peers, greet, 0)
    loads = []
    for n, (src, dst) in enumerate(
        ((wk_hbm, wk), (wv_hbm, wv), (wm_hbm, wm), (wq_hbm, wq), (wo_hbm, wo), (wu_hbm, wu), (wd_hbm, wd))
    ):
        loads.append(pltpu.make_async_copy(src, dst, w_sem.at[n]))
    total_ref[0:1, :] = jnp.zeros((1, width), F32)
    load_x.wait()
    for small in smalls:
        small.wait()
    for load in loads:
        load.start()

    def first(i, carry):
        x = x_ref[pl.ds(i * group, group)].reshape(rows, width).astype(F32)
        total_ref[0:1, :] = total_ref[0:1, :] + jnp.sum(x, axis=0, keepdims=True)
        fresh = normalize(x, gains_ref[0, 0:1, :]).astype(BF16)
        normed[0, pl.ds(i * group, group)] = fresh.reshape(group, block, width)
        return carry

    lax.fori_loop(0, steps, first, 0)

    def stage(layer, to):
        for slot in range(slots):
            at = send_sm[to * slots + slot]
            if layer > 0:
                at = pos_sm[at]
            send_buf[layer, to, pl.ds(slot * block, block), :] = normed[layer, at]

    def stage_self(layer):
        for slot in range(slots):
            at = send_sm[me * slots + slot]
            if layer > 0:
                at = pos_sm[at]
            far[layer, me, pl.ds(slot * block, block), :] = normed[layer, at]

    def stage_halo(layer, side):
        for b in range(HALO_B):
            at = b if side == 0 else blocks - HALO_B + b
            if layer > 0:
                at = pos_sm[at]
            halo_send[layer, side, pl.ds(b * block, block), :] = normed[layer, at]

    def send_halo(layer, across=None):
        halo_each(lambda side, to: stage_halo(layer, side), across)
        halo_each(lambda side, to: halo_copy(layer, side, to).start(), across)

    def stage_sum(layer):
        for k in range(width // 128):
            part = total_ref[0:1, k * 128 : (k + 1) * 128]
            sum_send[layer, k : k + 1, :] = part
            sums[layer, me, k : k + 1, :] = part

    def send_sum(layer):
        def one(k, carry):
            sum_out(layer, lax.rem(me + k, peers)).start()
            return carry

        lax.fori_loop(1, peers, one, 0)

    def stage_all(k, carry):
        stage(0, order(0, k))
        return carry

    def send_all(k, carry):
        far_out(0, order(0, k)).start()
        return carry

    ahead = quarter // 2
    lax.fori_loop(0, ahead, stage_all, 0)
    stage_sum(0)
    pl.semaphore_wait(barrier, peers - 1)
    lax.fori_loop(0, ahead, send_all, 0)
    lax.fori_loop(ahead, peers - 1, stage_all, 0)
    send_halo(0)
    send_sum(0)
    lax.fori_loop(ahead, peers - 1, send_all, 0)
    stage_self(0)

    uses = [jnp.int32(peers * slots + n) for n in range(blocks)]
    for k in range(peers - 2, -1, -1):
        to = order(1, jnp.int32(k))
        for slot in range(slots - 1, -1, -1):
            b = send_sm[to * slots + slot]
            uses = [use + equal(b, n) * (k * slots + slot - use) for n, use in enumerate(uses)]
    for n in range(HALO_B):
        low, high = n, blocks - HALO_B + n
        uses[low] = uses[low] - middle_side[0] * 2 * peers * slots
        uses[high] = uses[high] - middle_side[1] * 2 * peers * slots
    places = []
    for n in range(blocks):
        place = jnp.int32(0)
        for other in range(blocks):
            if other != n:
                place = place + below(uses[other], uses[n])
        places.append(place)
        pos_sm[n] = place
    for n in range(blocks):
        which = jnp.int32(0)
        for b in range(blocks):
            which = which + equal(places[b], n) * b
        perm_sm[n] = which
    def project(layer, piece, at):
        count = piece.shape[0]
        flat = piece.reshape(count * block, width)
        keys[pl.ds(at, count)] = dot(flat, wk[layer]).astype(BF16).reshape(count, block, width)
        turned = dot(wv[layer], flat, ((0,), (1,))).astype(BF16)
        for n in range(count):
            values[at + n] = turned[:, n * block : (n + 1) * block]

    def export(at, count, n):
        part = pl.ds(at, count)
        return (
            pltpu.make_async_copy(keys.at[part], keys_out.at[part], table_sem.at[0, n]),
            pltpu.make_async_copy(values.at[part], values_out.at[part], table_sem.at[1, n]),
        )

    chunk = math.gcd(blocks, 4)
    many = math.gcd(quarter, 4)

    def hand_on(layer, at, count, n):
        if layer == layers - 1:
            for copy in export(at, count, n):
                copy.start()

    def gather(layer):
        def own_piece(i, carry):
            if layer == 0:
                piece = normed[layer, pl.ds(i * chunk, chunk)]
            else:
                piece = jnp.concatenate([normed[layer, pos_sm[i * chunk + n]] for n in range(chunk)], axis=0)
                piece = piece.reshape(chunk, block, width)
            project(layer, piece, HALO_B + i * chunk)
            hand_on(layer, HALO_B + i * chunk, chunk, 0)
            return carry

        lax.fori_loop(0, blocks // chunk, own_piece, 0)

        def halo_in(copy, side):
            copy.wait_recv()
            at = 0 if side == 0 else HALO_B + blocks
            project(layer, halo[layer, side].reshape(HALO_B, block, width), at)
            hand_on(layer, at, HALO_B, 2 + side)

        @pl.when(me > 0)
        def _():
            halo_in(halo_copy(layer, 1, me - 1), 0)

        @pl.when(me < peers - 1)
        def _():
            halo_in(halo_copy(layer, 0, me + 1), 1)

        if layer == layers - 1:
            lax.fori_loop(0, steps, early_step, 0)
            drain(0)
        for n, (inside, outside) in enumerate(((2, 0), (0, 1), (1, 3), (3, 2))):
            if n == 3:
                sum_all(layer).wait_recv()
                whole = jnp.sum(sums[layer], axis=0)
                mean = jnp.concatenate([whole[k : k + 1, :] for k in range(width // 128)], axis=1) / node_total
                mean = jnp.broadcast_to(mean, (16, width)).astype(BF16)
                virtual[...] = dot(mean, wm[layer])
                if layer == layers - 1:
                    virtual_ref[...] = virtual[...]
                    lax.fori_loop(0, blocks, settle, 0)
                    settled.start()
            part = flip(my_part, jnp.where(inner == 1, inside, outside), 2)
            start = part * quarter

            @pl.when(part == my_part)
            def _(part=part, start=start):
                far_some(layer, start, quarter - 1, part).wait_recv()

            @pl.when(part != my_part)
            def _(part=part, start=start):
                far_some(layer, start, quarter, part).wait_recv()

            def far_piece(i, carry, start=start):
                source = start + i * many
                piece = far[layer, pl.ds(source, many)].reshape(many * slots, block, width)
                project(layer, piece, near + source * slots)
                hand_on(layer, near + source * slots, many * slots, 1)
                return carry

            lax.fori_loop(0, quarter // many, far_piece, 0)

    def attend_in(layer, which, queries, at):
        count = count_sm[which]
        home = table_sm[which, 0]
        spots = []
        for j in range(listed):
            entry = table_sm[which, j]
            if 2 * j >= listed:
                entry = home + below(j, count) * (entry - home)
            spots.append(entry)
        attend(
            count,
            lambda j, pair: keys[spots[j], :, pair],
            lambda j, pair: values[spots[j], pair],
            lambda part: queries[part, at : at + block],
            context,
            at,
            listed,
            head,
            block,
        )

    def early_copies(start, count):
        at = pl.ds(start, count)
        return (
            pltpu.make_async_copy(asked.at[at], queries_out.at[at], early_sem.at[0]),
            pltpu.make_async_copy(arranged.at[at], latent_out.at[at], early_sem.at[1]),
        )

    def block_step(layer, i):
        last = layer == layers - 1
        order_at = [i * group + g for g in range(group)]
        if last:
            which = order_at
            source = [pos_sm[w] for w in which]
            for w, s in zip(which, source):
                arranged[w] = latent[s]
        else:
            which = [perm_sm[n] for n in order_at]
            source = which
        mine = jnp.concatenate([normed[layer, s] for s in source], axis=0)
        queries = dot(wq[layer], mine, ((0,), (1,))).astype(BF16)
        if last:
            for g in range(group):
                asked[which[g]] = queries[:, g * block : (g + 1) * block]
        for g in range(group):
            attend_in(layer, which[g], queries, g * block)
        current = latent if layer > 0 else x_ref
        x = jnp.concatenate([current[s] for s in source], axis=0).astype(F32)
        result = feed(x, context[...], wo[layer], wu.at[layer], wd.at[layer], gains_ref, layer)
        at = pl.ds(i * group, group)
        if last:
            early[at] = result.reshape(group, block, width)
            for copy in early_copies(i * group, group):
                copy.start()
        else:
            result = (result + virtual[0:1, :]).astype(BF16)
            latent[at] = result.reshape(group, block, width)
            wide = result.astype(F32)
            fresh = normalize(wide, gains_ref[layer + 1, 0:1, :]).astype(BF16)
            normed[layer + 1, at] = fresh.reshape(group, block, width)
            total_ref[0:1, :] = total_ref[0:1, :] + jnp.sum(wide, axis=0, keepdims=True)

    def early_step(i, carry):
        block_step(layers - 1, i)
        return carry

    def drain(layer):
        far_some(layer, 0, peers - 1, my_part).wait_send()
        sum_all(layer).wait_send()
        halo_each(lambda side, to: halo_copy(layer, side, to).wait_send())

    settled = pltpu.make_async_copy(latent, settled_out, x_sem)

    def settle(b, carry):
        latent[b] = (early[b] + virtual[0:1, :]).astype(BF16)
        return carry

    for load in loads[:3]:
        load.wait()
    gather(0)
    for load in loads[3:]:
        load.wait()
    total_ref[0:1, :] = jnp.zeros((1, width), F32)

    def sending_step(i, carry):
        block_step(0, i)

        @pl.when(i == 0)
        def _():
            send_halo(1, 1)

        @pl.when(i == steps - 1)
        def _():
            stage_sum(1)
            send_halo(1, 0)
            send_sum(1)

        held = HALO_B * middle
        begin = jnp.maximum(i * group - held, 0)
        end = (i + 1) * group - held
        def each(k, carry):
            stage(1, order(1, k))
            return carry

        def go(k, carry):
            far_out(1, order(1, k)).start()
            return carry

        lax.fori_loop(begin, end, each, 0)
        lax.fori_loop(begin, end, go, 0)
        return carry

    def rest(k, carry):
        stage(1, order(1, k))
        return carry

    def go_rest(k, carry):
        far_out(1, order(1, k)).start()
        return carry

    lax.fori_loop(0, steps, sending_step, 0)
    lax.fori_loop(blocks - HALO_B * middle, peers - 1, rest, 0)
    lax.fori_loop(blocks - HALO_B * middle, peers - 1, go_rest, 0)
    stage_self(1)

    gather(1)
    drain(1)
    for start, count, n in ((HALO_B, blocks, 0), (near, peers * slots, 1)):
        for copy in export(start, count, n):
            copy.wait()

    @pl.when(me > 0)
    def _():
        for copy in export(0, HALO_B, 2):
            copy.wait()

    @pl.when(me < peers - 1)
    def _():
        for copy in export(HALO_B + blocks, HALO_B, 3):
            copy.wait()

    for copy in early_copies(0, blocks):
        copy.wait()
    settled.wait()


def finish_kernel(layer, near, group, table_sm, count_sm, gains_ref, virtual_ref, settled_hbm, keys_hbm, values_hbm,
                  queries_hbm, latent_hbm, wo_hbm, wu_hbm, wd_hbm, out_hbm, kept_keys, kept_values, asked, current, context,
                  kept, wo, wu, wd, todo_sm, w_sem, key_sem, value_sem, row_sem, kept_sem):
    blocks, block, width = kept.shape
    listed = table_sm.shape[1]
    head = width // HEADS
    weight_loads = [
        pltpu.make_async_copy(src.at[layer], dst, w_sem.at[n])
        for n, (src, dst) in enumerate(((wo_hbm, wo), (wu_hbm, wu), (wd_hbm, wd)))
    ]
    number = jnp.int32(0)
    for b in range(blocks):
        away = jnp.int32(0)
        for j in range(listed):
            away = jnp.where((j < count_sm[b]) & (table_sm[b, j] >= near), 1, away)

        @pl.when(away > 0)
        def _(b=b, number=number):
            todo_sm[number] = b

        number = number + away

    def block_of(i, g):
        return todo_sm[jnp.minimum(i * group + g, number - 1)]

    def rows(which, g):
        return (
            pltpu.make_async_copy(queries_hbm.at[which], asked.at[g], row_sem.at[0, g]),
            pltpu.make_async_copy(latent_hbm.at[which], current.at[g], row_sem.at[1, g]),
        )

    def fetch(i, g):
        which = block_of(i, g)
        for copy in rows(which, g):
            copy.start()
        for j in range(listed):
            entry = table_sm[which, j * below(j, count_sm[which])]
            pltpu.make_async_copy(keys_hbm.at[entry], kept_keys.at[g, j], key_sem.at[g]).start()
            pltpu.make_async_copy(values_hbm.at[entry], kept_values.at[g, j], value_sem.at[g]).start()

    def fetched(i, g):
        for copy in rows(block_of(i, g), g):
            copy.wait()
        some = pl.ds(0, listed)
        pltpu.make_async_copy(keys_hbm.at[some], kept_keys.at[g], key_sem.at[g]).wait()
        pltpu.make_async_copy(values_hbm.at[some], kept_values.at[g], value_sem.at[g]).wait()

    def each_live(i, act, some=range(group)):
        for g in some:
            pl.when(i * group + g < number)(lambda g=g: act(i, g))

    together = math.gcd(group, 2)

    def late_step(i, carry):
        pl.when(i > 0)(lambda: each_live(i, fetch))
        for start in range(0, group, together):
            some = range(start, start + together)

            @pl.when(i * group + start < number)
            def _(some=some):
                each_live(i, fetched, some)
                if some[0] == 0:

                    @pl.when(i == 0)
                    def _():
                        for load in weight_loads:
                            load.start()
                        load_kept.start()

                for g in some:
                    attend(
                        count_sm[block_of(i, g)],
                        lambda j, pair, g=g: kept_keys[g, j, :, pair],
                        lambda j, pair, g=g: kept_values[g, j, pair, :],
                        lambda part, g=g: asked[g, part, :],
                        context,
                        g * block,
                        listed,
                        head,
                        block,
                    )

        @pl.when(i == 0)
        def _():
            for load in weight_loads:
                load.wait()
            load_kept.wait()

        x = current[...].reshape(group * block, width).astype(F32)
        result = feed(x, context[...], wo[...], wu, wd, gains_ref, layer) + virtual_ref[0:1, :]
        result = result.astype(BF16).reshape(group, block, width)

        def put(i, g):
            kept[block_of(i, g)] = result[g]

        each_live(i, put)
        return carry

    load_kept = pltpu.make_async_copy(settled_hbm, kept, kept_sem)

    @pl.when(number > 0)
    def _():
        each_live(0, fetch)
        lax.fori_loop(0, (number + group - 1) // group, late_step, 0)

    @pl.when(number == 0)
    def _():
        load_kept.start()
        load_kept.wait()

    give = pltpu.make_async_copy(kept, out_hbm, kept_sem)
    give.start()
    give.wait()


def body(node_features, nbr_table, nbr_count, send_block, w_query, w_key, w_value, w_out, w_up, w_down, w_virtual, gains):
    blocks, listed = nbr_table.shape
    own, width = node_features.shape
    block = own // blocks
    peers = lax.axis_size(AXIS)
    slots = send_block.shape[1]
    layers = w_query.shape[0]
    group = math.gcd(blocks, 4)
    near = 2 * HALO_B + blocks
    entries = near + peers * slots
    shapes = (peers, layers, blocks, block, width, slots, listed, group, own * peers)
    weights = (w_query, w_key, w_value, w_out, w_up, w_down, w_virtual)
    vmem, smem, hbm = (pl.BlockSpec(memory_space=s) for s in (pltpu.VMEM, pltpu.SMEM, pl.ANY))
    dma = pltpu.SemaphoreType.DMA
    shape = jax.ShapeDtypeStruct
    scratch = [pltpu.VMEM(w.shape, BF16) for w in weights]
    scratch += [
        pltpu.VMEM((blocks, block, width), BF16),
        pltpu.VMEM((layers, blocks, block, width), BF16),
        pltpu.VMEM((blocks, block, width), BF16),
        pltpu.VMEM((entries, block, width), BF16),
        pltpu.VMEM((entries, width, block), BF16),
        pltpu.VMEM((width, group * block), BF16),
        pltpu.VMEM((layers, peers, slots * block, width), BF16),
        pltpu.VMEM((layers, peers, slots * block, width), BF16),
        pltpu.VMEM((layers, 2, HALO_B * block, width), BF16),
        pltpu.VMEM((layers, 2, HALO_B * block, width), BF16),
        pltpu.VMEM((layers, width // 128, 128), F32),
        pltpu.VMEM((layers, peers, width // 128, 128), F32),
        pltpu.VMEM((8, width), F32),
        pltpu.VMEM((blocks, block, width), F32),
        pltpu.VMEM((blocks, width, block), BF16),
        pltpu.VMEM((blocks, block, width), BF16),
        pltpu.VMEM((16, width), F32),
        pltpu.SMEM(nbr_table.shape, jnp.int32),
        pltpu.SMEM(nbr_count.shape, jnp.int32),
        pltpu.SMEM((peers * slots,), jnp.int32),
        pltpu.VMEM(gains.shape, F32),
        pltpu.SMEM((blocks,), jnp.int32),
        pltpu.SMEM((blocks,), jnp.int32),
        dma,
        dma((4,)),
        dma((len(weights),)),
        dma((layers,)),
        dma((layers, 4)),
        dma((layers, 2)),
        dma((layers, 2)),
        dma((layers,)),
        dma((layers,)),
        dma((2, 4)),
        dma((2,)),
    ]
    settled, keys, values, queries, latent, virtual = pl.pallas_call(
        functools.partial(exchange_kernel, shapes),
        out_shape=(
            shape((blocks, block, width), BF16),
            shape((entries, block, width), BF16),
            shape((entries, width, block), BF16),
            shape((blocks, width, block), BF16),
            shape((blocks, block, width), BF16),
            shape((16, width), F32),
        ),
        in_specs=[hbm] * (5 + len(weights)),
        out_specs=(hbm, hbm, hbm, hbm, hbm, vmem),
        scratch_shapes=scratch,
        compiler_params=pltpu.CompilerParams(collective_id=0, has_side_effects=True, vmem_limit_bytes=VMEM_LIMIT),
        name="exchange",
    )(nbr_table, nbr_count, send_block.reshape(-1), gains, node_features.reshape(blocks, block, width), *weights)
    result = pl.pallas_call(
        functools.partial(finish_kernel, layers - 1, near, group),
        out_shape=shape((blocks, block, width), BF16),
        in_specs=[smem, smem, vmem, vmem] + [hbm] * 8,
        out_specs=hbm,
        scratch_shapes=[
            pltpu.VMEM((group, listed, block, width), BF16),
            pltpu.VMEM((group, listed, width, block), BF16),
            pltpu.VMEM((group, width, block), BF16),
            pltpu.VMEM((group, block, width), BF16),
            pltpu.VMEM((width, group * block), BF16),
            pltpu.VMEM((blocks, block, width), BF16),
            pltpu.VMEM(w_out.shape[1:], BF16),
            pltpu.VMEM(w_up.shape[1:], BF16),
            pltpu.VMEM(w_down.shape[1:], BF16),
            pltpu.SMEM((blocks,), jnp.int32),
            dma((3,)),
            dma((group,)),
            dma((group,)),
            dma((2, group)),
            dma,
        ],
        compiler_params=pltpu.CompilerParams(vmem_limit_bytes=VMEM_LIMIT),
        name="finish",
    )(nbr_table, nbr_count, gains, virtual, settled, keys, values, queries, latent, w_out, w_up, w_down)
    return result.reshape(own, width)


def solution(mesh):
    across = P(("members", "row"), None)
    in_specs = (across, P("row", None), P("row"), P("row", None)) + (P(),) * 8
    return jax.shard_map(body, mesh=mesh, in_specs=in_specs, out_specs=across, check_vma=False)
```

```python
import functools
import math

import jax
import jax.numpy as jnp
from jax import lax
from jax.experimental import pallas as pl
from jax.experimental.pallas import tpu as pltpu
from jax.sharding import PartitionSpec as P

HEADS = 4
HALO_B = 2
VMEM_LIMIT = 67_000_000
MESH = pl.DeviceIdType.MESH
BF16 = jnp.bfloat16
F32 = jnp.float32
AXIS = "row"


def normalize(values, scaling):
    centred = values - jnp.mean(values, axis=-1, keepdims=True)
    spread = jnp.mean(centred * centred, axis=-1, keepdims=True)
    return centred * lax.rsqrt(spread + 1e-05) * scaling


def dot(a, b, contract=((1,), (0,))):
    return lax.dot_general(a, b, (contract, ((), ())), preferred_element_type=F32)


def gelu(x):
    return 0.5 * x * (1.0 + jnp.tanh(math.sqrt(2 / math.pi) * (x + 0.044715 * x * x * x)))


def flip(a, b, bits):
    out = 0
    for bit in range(bits):
        weight = 1 << bit
        x = lax.rem(lax.div(a, jnp.int32(weight)), jnp.int32(2))
        y = lax.rem(lax.div(b, jnp.int32(weight)), jnp.int32(2))
        out = out + weight * lax.rem(x + y, jnp.int32(2))
    return out


def below(a, b):
    return jnp.minimum(jnp.maximum(b - a, 0), 1)


def equal(a, b):
    return 1 - jnp.minimum(jnp.maximum(a - b, b - a), 1)


def attend(count, key_of, value_of, query_of, context, at, listed, head, block):
    scale = math.log2(math.e) / math.sqrt(head)
    dead = [(1 - below(j, count)).astype(F32) * -1e30 for j in range(listed)]
    blank = jnp.zeros((head, block), BF16)
    for h in range(0, HEADS, 2):
        pair = slice(h * head, (h + 2) * head)
        upper = query_of(slice(h * head, (h + 1) * head))
        lower = query_of(slice((h + 1) * head, (h + 2) * head))
        both = jnp.concatenate(
            [jnp.concatenate([upper, blank], axis=1), jnp.concatenate([blank, lower], axis=1)], axis=0
        )
        scores = []
        for j in range(listed):
            s = dot(key_of(j, pair), both)
            scores.append(s if 2 * j < listed else s + dead[j])
        top = jnp.max(functools.reduce(jnp.maximum, scores), axis=0, keepdims=True)
        weights = [jnp.exp2((s - top) * scale) for s in scores]
        inverse = 1.0 / jnp.sum(functools.reduce(jnp.add, weights), axis=0, keepdims=True)
        probs = jnp.concatenate([w.astype(BF16) for w in weights], axis=0)
        mixed = dot(jnp.concatenate([value_of(j, pair) for j in range(listed)], axis=1), probs)
        for n in range(2):
            part = slice(n * block, (n + 1) * block)
            of_head = slice((h + n) * head, (h + n + 1) * head)
            context[of_head, at : at + block] = (mixed[n * head : (n + 1) * head, part] * inverse[:, part]).astype(BF16)


def feed(x, context, wo, wu, wd, gains_ref, layer):
    after_att = x + normalize(dot(context, wo, ((0,), (0,))), gains_ref[layer, 1:2, :])
    middle = normalize(after_att, gains_ref[layer, 2:3, :]).astype(BF16)
    hidden_size = wu.shape[-1]
    part = math.gcd(hidden_size, 512)
    down = None
    for f in range(0, hidden_size, part):
        hidden = gelu(dot(middle, wu[:, f : f + part])).astype(BF16)
        term = dot(hidden, wd[f : f + part, :])
        down = term if down is None else down + term
    return after_att + normalize(down, gains_ref[layer, 3:4, :])


def exchange_kernel(shapes, table_hbm, count_hbm, send_hbm, gains_hbm, x_hbm, wq_hbm, wk_hbm, wv_hbm, wo_hbm, wu_hbm,
                    wd_hbm, wm_hbm, settled_out, keys_out, values_out, queries_out, latent_out, virtual_ref, wq, wk, wv,
                    wo, wu, wd, wm, x_ref, normed, latent, keys, values, context, send_buf, far, halo_send, halo,
                    sum_send, sums, total_ref, early, asked, arranged, virtual, table_sm, count_sm, send_sm,
                    gains_ref, perm_sm, pos_sm, x_sem, small_sem, w_sem, far_send,
                    far_recv, halo_ssem, halo_rsem, sum_ssem, sum_rsem, table_sem, early_sem):
    peers, layers, blocks, block, width, slots, listed, group, node_total = shapes
    near = 2 * HALO_B + blocks
    bits = peers.bit_length() - 1
    half, quarter = peers // 2, peers // 4
    rows = group * block
    steps = blocks // group
    head = width // HEADS
    me = lax.axis_index(AXIS)
    inner = jnp.where((me >= quarter) & (me < half + quarter), 1, 0)

    def order(layer, k):
        outer = jnp.where(k < half, half + k, peers - 1 - k)
        lead = quarter // 2 if layer == 0 else quarter
        late = k - lead
        inside = jnp.where(
            late < 0, peers - 1 - k, jnp.where(late < half - 1, half - 1 - late, peers - 1 - lead - (late - half + 1))
        )
        return flip(me, jnp.where(inner == 1, inside, outer), bits)

    def remote(src, dst, ssem, rsem, to):
        return pltpu.make_async_remote_copy(
            src_ref=src, dst_ref=dst, send_sem=ssem, recv_sem=rsem, device_id={AXIS: to}, device_id_type=MESH
        )

    my_part = lax.div(me, jnp.int32(quarter))

    def far_out(layer, to):
        return remote(send_buf.at[layer, to], far.at[layer, me], far_send.at[layer], far_recv.at[layer, my_part], to)

    def far_some(layer, start, count, part):
        some = pl.ds(start, count)
        return remote(send_buf.at[layer, some], far.at[layer, some], far_send.at[layer], far_recv.at[layer, part], me)

    def sum_out(layer, to):
        return remote(sum_send.at[layer], sums.at[layer, me], sum_ssem.at[layer], sum_rsem.at[layer], to)

    def sum_all(layer):
        some = sums.at[layer, pl.ds(0, peers - 1)]
        return remote(some, some, sum_ssem.at[layer], sum_rsem.at[layer], me)

    def halo_copy(layer, side, to):
        return remote(
            halo_send.at[layer, side], halo.at[layer, 1 - side], halo_ssem.at[layer, side], halo_rsem.at[layer, 1 - side], to
        )

    middle_side = [jnp.where(me == half, 1, 0), jnp.where(me == half - 1, 1, 0)]
    middle = middle_side[0] + middle_side[1]

    def halo_each(act, across=None):
        for side in range(2):
            there = me > 0 if side == 0 else me < peers - 1
            if across is not None:
                there = there & (middle_side[side] == across)

            @pl.when(there)
            def _(side=side):
                act(side, me - 1 if side == 0 else me + 1)

    load_x = pltpu.make_async_copy(x_hbm, x_ref, x_sem)
    load_x.start()
    smalls = [
        pltpu.make_async_copy(src, dst, small_sem.at[n])
        for n, (src, dst) in enumerate(
            ((gains_hbm, gains_ref), (send_hbm, send_sm), (table_hbm, table_sm), (count_hbm, count_sm))
        )
    ]
    for small in smalls:
        small.start()
    barrier = pltpu.get_barrier_semaphore()

    def greet(k, carry):
        pl.semaphore_signal(barrier, inc=1, device_id={AXIS: lax.rem(me + k, peers)}, device_id_type=MESH)
        return carry

    lax.fori_loop(1, peers, greet, 0)
    loads = []
    for n, (src, dst) in enumerate(
        ((wk_hbm, wk), (wv_hbm, wv), (wm_hbm, wm), (wq_hbm, wq), (wo_hbm, wo), (wu_hbm, wu), (wd_hbm, wd))
    ):
        loads.append(pltpu.make_async_copy(src, dst, w_sem.at[n]))
    total_ref[0:1, :] = jnp.zeros((1, width), F32)
    load_x.wait()
    for small in smalls:
        small.wait()
    for load in loads:
        load.start()

    def first(i, carry):
        x = x_ref[pl.ds(i * group, group)].reshape(rows, width).astype(F32)
        total_ref[0:1, :] = total_ref[0:1, :] + jnp.sum(x, axis=0, keepdims=True)
        fresh = normalize(x, gains_ref[0, 0:1, :]).astype(BF16)
        normed[0, pl.ds(i * group, group)] = fresh.reshape(group, block, width)
        return carry

    lax.fori_loop(0, steps, first, 0)

    def stage(layer, to):
        for slot in range(slots):
            at = send_sm[to * slots + slot]
            if layer > 0:
                at = pos_sm[at]
            send_buf[layer, to, pl.ds(slot * block, block), :] = normed[layer, at]

    def stage_self(layer):
        for slot in range(slots):
            at = send_sm[me * slots + slot]
            if layer > 0:
                at = pos_sm[at]
            far[layer, me, pl.ds(slot * block, block), :] = normed[layer, at]

    def stage_halo(layer, side):
        for b in range(HALO_B):
            at = b if side == 0 else blocks - HALO_B + b
            if layer > 0:
                at = pos_sm[at]
            halo_send[layer, side, pl.ds(b * block, block), :] = normed[layer, at]

    def send_halo(layer, across=None):
        halo_each(lambda side, to: halo_copy(layer, side, to).start(), across)

    def stage_sum(layer):
        for k in range(width // 128):
            part = total_ref[0:1, k * 128 : (k + 1) * 128]
            sum_send[layer, k : k + 1, :] = part
            sums[layer, me, k : k + 1, :] = part

    def send_sum(layer):
        def one(k, carry):
            sum_out(layer, lax.rem(me + k, peers)).start()
            return carry

        lax.fori_loop(1, peers, one, 0)

    def stage_all(k, carry):
        stage(0, order(0, k))
        return carry

    def send_all(k, carry):
        far_out(0, order(0, k)).start()
        return carry

    stage_sum(0)
    halo_each(lambda side, to: stage_halo(0, side))
    lax.fori_loop(0, peers - 1, stage_all, 0)
    pl.semaphore_wait(barrier, peers - 1)
    send_halo(0)
    send_sum(0)
    lax.fori_loop(0, peers - 1, send_all, 0)
    stage_self(0)

    uses = [jnp.int32(peers * slots + n) for n in range(blocks)]
    for k in range(peers - 2, -1, -1):
        to = order(1, jnp.int32(k))
        for slot in range(slots - 1, -1, -1):
            b = send_sm[to * slots + slot]
            uses = [use + equal(b, n) * (k * slots + slot - use) for n, use in enumerate(uses)]
    for n in range(HALO_B):
        low, high = n, blocks - HALO_B + n
        uses[low] = uses[low] - middle_side[0] * 2 * peers * slots
        uses[high] = uses[high] - middle_side[1] * 2 * peers * slots
    places = []
    for n in range(blocks):
        place = jnp.int32(0)
        for other in range(blocks):
            if other != n:
                place = place + below(uses[other], uses[n])
        places.append(place)
        pos_sm[n] = place
    for n in range(blocks):
        which = jnp.int32(0)
        for b in range(blocks):
            which = which + equal(places[b], n) * b
        perm_sm[n] = which
    def project(layer, piece, at):
        count = piece.shape[0]
        flat = piece.reshape(count * block, width)
        keys[pl.ds(at, count)] = dot(flat, wk[layer]).astype(BF16).reshape(count, block, width)
        turned = dot(wv[layer], flat, ((0,), (1,))).astype(BF16)
        for n in range(count):
            values[at + n] = turned[:, n * block : (n + 1) * block]

    def export(at, count, n):
        part = pl.ds(at, count)
        return (
            pltpu.make_async_copy(keys.at[part], keys_out.at[part], table_sem.at[0, n]),
            pltpu.make_async_copy(values.at[part], values_out.at[part], table_sem.at[1, n]),
        )

    chunk = math.gcd(blocks, 4)
    many = math.gcd(quarter, 4)

    def hand_on(layer, at, count, n):
        if layer == layers - 1:
            for copy in export(at, count, n):
                copy.start()

    def gather(layer):
        def own_piece(i, carry):
            if layer == 0:
                piece = normed[layer, pl.ds(i * chunk, chunk)]
            else:
                piece = jnp.concatenate([normed[layer, pos_sm[i * chunk + n]] for n in range(chunk)], axis=0)
                piece = piece.reshape(chunk, block, width)
            project(layer, piece, HALO_B + i * chunk)
            hand_on(layer, HALO_B + i * chunk, chunk, 0)
            return carry

        lax.fori_loop(0, blocks // chunk, own_piece, 0)

        def halo_in(copy, side):
            copy.wait_recv()
            at = 0 if side == 0 else HALO_B + blocks
            project(layer, halo[layer, side].reshape(HALO_B, block, width), at)
            hand_on(layer, at, HALO_B, 2 + side)

        @pl.when(me > 0)
        def _():
            halo_in(halo_copy(layer, 1, me - 1), 0)

        @pl.when(me < peers - 1)
        def _():
            halo_in(halo_copy(layer, 0, me + 1), 1)

        if layer == layers - 1:
            lax.fori_loop(0, steps, early_step, 0)
            drain(0)
        for n, (inside, outside) in enumerate(((2, 0), (0, 1), (1, 3), (3, 2))):
            if n == 3:
                sum_all(layer).wait_recv()
                whole = jnp.sum(sums[layer], axis=0)
                mean = jnp.concatenate([whole[k : k + 1, :] for k in range(width // 128)], axis=1) / node_total
                mean = jnp.broadcast_to(mean, (16, width)).astype(BF16)
                virtual[...] = dot(mean, wm[layer])
                if layer == layers - 1:
                    virtual_ref[...] = virtual[...]
                    lax.fori_loop(0, blocks, settle, 0)
                    settled.start()
            part = flip(my_part, jnp.where(inner == 1, inside, outside), 2)
            start = part * quarter

            @pl.when(part == my_part)
            def _(part=part, start=start):
                far_some(layer, start, quarter - 1, part).wait_recv()

            @pl.when(part != my_part)
            def _(part=part, start=start):
                far_some(layer, start, quarter, part).wait_recv()

            def far_piece(i, carry, start=start):
                source = start + i * many
                piece = far[layer, pl.ds(source, many)].reshape(many * slots, block, width)
                project(layer, piece, near + source * slots)
                hand_on(layer, near + source * slots, many * slots, 1)
                return carry

            lax.fori_loop(0, quarter // many, far_piece, 0)

    def attend_in(layer, which, queries, at):
        count = count_sm[which]
        home = table_sm[which, 0]
        spots = []
        for j in range(listed):
            entry = table_sm[which, j]
            if 2 * j >= listed:
                entry = home + below(j, count) * (entry - home)
            spots.append(entry)
        attend(
            count,
            lambda j, pair: keys[spots[j], :, pair],
            lambda j, pair: values[spots[j], pair],
            lambda part: queries[part, at : at + block],
            context,
            at,
            listed,
            head,
            block,
        )

    def early_copies(start, count):
        at = pl.ds(start, count)
        return (
            pltpu.make_async_copy(asked.at[at], queries_out.at[at], early_sem.at[0]),
            pltpu.make_async_copy(arranged.at[at], latent_out.at[at], early_sem.at[1]),
        )

    def block_step(layer, i):
        last = layer == layers - 1
        order_at = [i * group + g for g in range(group)]
        if last:
            which = order_at
            source = [pos_sm[w] for w in which]
            for w, s in zip(which, source):
                arranged[w] = latent[s]
        else:
            which = [perm_sm[n] for n in order_at]
            source = which
        mine = jnp.concatenate([normed[layer, s] for s in source], axis=0)
        queries = dot(wq[layer], mine, ((0,), (1,))).astype(BF16)
        if last:
            for g in range(group):
                asked[which[g]] = queries[:, g * block : (g + 1) * block]
        for g in range(group):
            attend_in(layer, which[g], queries, g * block)
        current = latent if layer > 0 else x_ref
        x = jnp.concatenate([current[s] for s in source], axis=0).astype(F32)
        result = feed(x, context[...], wo[layer], wu.at[layer], wd.at[layer], gains_ref, layer)
        at = pl.ds(i * group, group)
        if last:
            early[at] = result.reshape(group, block, width)
            for copy in early_copies(i * group, group):
                copy.start()
        else:
            result = (result + virtual[0:1, :]).astype(BF16)
            latent[at] = result.reshape(group, block, width)
            wide = result.astype(F32)
            fresh = normalize(wide, gains_ref[layer + 1, 0:1, :]).astype(BF16)
            normed[layer + 1, at] = fresh.reshape(group, block, width)
            total_ref[0:1, :] = total_ref[0:1, :] + jnp.sum(wide, axis=0, keepdims=True)

    def early_step(i, carry):
        block_step(layers - 1, i)
        return carry

    def drain(layer):
        far_some(layer, 0, peers - 1, my_part).wait_send()
        sum_all(layer).wait_send()
        halo_each(lambda side, to: halo_copy(layer, side, to).wait_send())

    settled = pltpu.make_async_copy(latent, settled_out, x_sem)

    def settle(b, carry):
        latent[b] = (early[b] + virtual[0:1, :]).astype(BF16)
        return carry

    for load in loads[:3]:
        load.wait()
    gather(0)
    for load in loads[3:]:
        load.wait()
    total_ref[0:1, :] = jnp.zeros((1, width), F32)

    def sending_step(i, carry):
        block_step(0, i)

        @pl.when(i == 0)
        def _():
            halo_each(lambda side, to: stage_halo(1, side), 1)

        @pl.when(i == steps - 1)
        def _():
            halo_each(lambda side, to: stage_halo(1, side), 0)
            stage_sum(1)

        held = HALO_B * middle
        begin = jnp.maximum(i * group - held, 0)
        end = (i + 1) * group - held
        def each(k, carry):
            stage(1, order(1, k))
            return carry

        def go(k, carry):
            far_out(1, order(1, k)).start()
            return carry

        until = jnp.where(i == steps - 1, peers - 1, end)
        lax.fori_loop(begin, until, each, 0)

        @pl.when(i == 0)
        def _():
            send_halo(1, 1)

        @pl.when(i == steps - 1)
        def _():
            send_halo(1, 0)
            send_sum(1)

        lax.fori_loop(begin, until, go, 0)
        return carry

    lax.fori_loop(0, steps, sending_step, 0)
    stage_self(1)

    gather(1)
    drain(1)
    for start, count, n in ((HALO_B, blocks, 0), (near, peers * slots, 1)):
        for copy in export(start, count, n):
            copy.wait()

    @pl.when(me > 0)
    def _():
        for copy in export(0, HALO_B, 2):
            copy.wait()

    @pl.when(me < peers - 1)
    def _():
        for copy in export(HALO_B + blocks, HALO_B, 3):
            copy.wait()

    for copy in early_copies(0, blocks):
        copy.wait()
    settled.wait()


def finish_kernel(layer, near, group, table_sm, count_sm, gains_ref, virtual_ref, settled_hbm, keys_hbm, values_hbm,
                  queries_hbm, latent_hbm, wo_hbm, wu_hbm, wd_hbm, out_hbm, kept_keys, kept_values, asked, current, context,
                  kept, wo, wu, wd, todo_sm, w_sem, key_sem, value_sem, row_sem, kept_sem):
    blocks, block, width = kept.shape
    listed = table_sm.shape[1]
    head = width // HEADS
    weight_loads = [
        pltpu.make_async_copy(src.at[layer], dst, w_sem.at[n])
        for n, (src, dst) in enumerate(((wo_hbm, wo), (wu_hbm, wu), (wd_hbm, wd)))
    ]
    number = jnp.int32(0)
    for b in range(blocks):
        away = jnp.int32(0)
        for j in range(listed):
            away = jnp.where((j < count_sm[b]) & (table_sm[b, j] >= near), 1, away)

        @pl.when(away > 0)
        def _(b=b, number=number):
            todo_sm[number] = b

        number = number + away

    def block_of(n):
        return todo_sm[jnp.minimum(n, number - 1)]

    def rows(n):
        which = block_of(n)
        return (
            pltpu.make_async_copy(queries_hbm.at[which], asked.at[n], row_sem.at[0, n]),
            pltpu.make_async_copy(latent_hbm.at[which], current.at[n], row_sem.at[1, n]),
        )

    def fetch(n, carry):
        which = block_of(n)
        for copy in rows(n):
            copy.start()
        for j in range(listed):
            entry = table_sm[which, j * below(j, count_sm[which])]
            pltpu.make_async_copy(keys_hbm.at[entry], kept_keys.at[n, j], key_sem.at[n]).start()
            pltpu.make_async_copy(values_hbm.at[entry], kept_values.at[n, j], value_sem.at[n]).start()
        return carry

    def fetched(n):
        for copy in rows(n):
            copy.wait()
        some = pl.ds(0, listed)
        pltpu.make_async_copy(keys_hbm.at[some], kept_keys.at[n], key_sem.at[n]).wait()
        pltpu.make_async_copy(values_hbm.at[some], kept_values.at[n], value_sem.at[n]).wait()

    load_kept = pltpu.make_async_copy(settled_hbm, kept, kept_sem)
    together = context.shape[2] // block
    turns = (number + together - 1) // together

    def attend_some(i, carry):
        for g in range(together):
            pl.when(i * together + g < number)(lambda g=g: fetched(i * together + g))

        @pl.when(i == 0)
        def _():
            for load in weight_loads:
                load.start()
            load_kept.start()

        for g in range(together):
            n = i * together + g
            attend(
                count_sm[block_of(n)],
                lambda j, pair, n=n: kept_keys[n, j, :, pair],
                lambda j, pair, n=n: kept_values[n, j, pair, :],
                lambda part, n=n: asked[n, part, :],
                context.at[i],
                g * block,
                listed,
                head,
                block,
            )
        return carry

    def feed_some(i, parts):
        size = parts * together
        first = i * group
        x = current[pl.ds(first, size)].reshape(size * block, width).astype(F32)
        mixed = jnp.concatenate([context[i * (group // together) + n] for n in range(parts)], axis=1)
        result = feed(x, mixed, wo[...], wu, wd, gains_ref, layer) + virtual_ref[0:1, :]
        result = result.astype(BF16).reshape(size, block, width)
        for g in range(size):

            @pl.when(first + g < number)
            def _(g=g):
                kept[block_of(first + g)] = result[g]

    def feed_turns(i, carry):
        left = number - i * group
        if group > together:
            pl.when(left > together)(lambda: feed_some(i, group // together))
            pl.when(left <= together)(lambda: feed_some(i, 1))
        else:
            feed_some(i, 1)
        return carry

    @pl.when(number > 0)
    def _():
        lax.fori_loop(0, number, fetch, 0)
        lax.fori_loop(0, turns, attend_some, 0)
        for load in weight_loads:
            load.wait()
        load_kept.wait()
        lax.fori_loop(0, (number + group - 1) // group, feed_turns, 0)

    @pl.when(number == 0)
    def _():
        load_kept.start()
        load_kept.wait()

    give = pltpu.make_async_copy(kept, out_hbm, kept_sem)
    give.start()
    give.wait()


def body(node_features, nbr_table, nbr_count, send_block, w_query, w_key, w_value, w_out, w_up, w_down, w_virtual, gains):
    blocks, listed = nbr_table.shape
    own, width = node_features.shape
    block = own // blocks
    peers = lax.axis_size(AXIS)
    slots = send_block.shape[1]
    layers = w_query.shape[0]
    group = math.gcd(blocks, 4)
    near = 2 * HALO_B + blocks
    entries = near + peers * slots
    shapes = (peers, layers, blocks, block, width, slots, listed, group, own * peers)
    weights = (w_query, w_key, w_value, w_out, w_up, w_down, w_virtual)
    vmem, smem, hbm = (pl.BlockSpec(memory_space=s) for s in (pltpu.VMEM, pltpu.SMEM, pl.ANY))
    dma = pltpu.SemaphoreType.DMA
    shape = jax.ShapeDtypeStruct
    scratch = [pltpu.VMEM(w.shape, BF16) for w in weights]
    scratch += [
        pltpu.VMEM((blocks, block, width), BF16),
        pltpu.VMEM((layers, blocks, block, width), BF16),
        pltpu.VMEM((blocks, block, width), BF16),
        pltpu.VMEM((entries, block, width), BF16),
        pltpu.VMEM((entries, width, block), BF16),
        pltpu.VMEM((width, group * block), BF16),
        pltpu.VMEM((layers, peers, slots * block, width), BF16),
        pltpu.VMEM((layers, peers, slots * block, width), BF16),
        pltpu.VMEM((layers, 2, HALO_B * block, width), BF16),
        pltpu.VMEM((layers, 2, HALO_B * block, width), BF16),
        pltpu.VMEM((layers, width // 128, 128), F32),
        pltpu.VMEM((layers, peers, width // 128, 128), F32),
        pltpu.VMEM((8, width), F32),
        pltpu.VMEM((blocks, block, width), F32),
        pltpu.VMEM((blocks, width, block), BF16),
        pltpu.VMEM((blocks, block, width), BF16),
        pltpu.VMEM((16, width), F32),
        pltpu.SMEM(nbr_table.shape, jnp.int32),
        pltpu.SMEM(nbr_count.shape, jnp.int32),
        pltpu.SMEM((peers * slots,), jnp.int32),
        pltpu.VMEM(gains.shape, F32),
        pltpu.SMEM((blocks,), jnp.int32),
        pltpu.SMEM((blocks,), jnp.int32),
        dma,
        dma((4,)),
        dma((len(weights),)),
        dma((layers,)),
        dma((layers, 4)),
        dma((layers, 2)),
        dma((layers, 2)),
        dma((layers,)),
        dma((layers,)),
        dma((2, 4)),
        dma((2,)),
    ]
    settled, keys, values, queries, latent, virtual = pl.pallas_call(
        functools.partial(exchange_kernel, shapes),
        out_shape=(
            shape((blocks, block, width), BF16),
            shape((entries, block, width), BF16),
            shape((entries, width, block), BF16),
            shape((blocks, width, block), BF16),
            shape((blocks, block, width), BF16),
            shape((16, width), F32),
        ),
        in_specs=[hbm] * (5 + len(weights)),
        out_specs=(hbm, hbm, hbm, hbm, hbm, vmem),
        scratch_shapes=scratch,
        compiler_params=pltpu.CompilerParams(collective_id=0, has_side_effects=True, vmem_limit_bytes=VMEM_LIMIT),
        name="exchange",
    )(nbr_table, nbr_count, send_block.reshape(-1), gains, node_features.reshape(blocks, block, width), *weights)
    result = pl.pallas_call(
        functools.partial(finish_kernel, layers - 1, near, group),
        out_shape=shape((blocks, block, width), BF16),
        in_specs=[smem, smem, vmem, vmem] + [hbm] * 8,
        out_specs=hbm,
        scratch_shapes=[
            pltpu.VMEM((blocks, listed, block, width), BF16),
            pltpu.VMEM((blocks, listed, width, block), BF16),
            pltpu.VMEM((blocks, width, block), BF16),
            pltpu.VMEM((blocks, block, width), BF16),
            pltpu.VMEM((blocks // math.gcd(group, 2), width, math.gcd(group, 2) * block), BF16),
            pltpu.VMEM((blocks, block, width), BF16),
            pltpu.VMEM(w_out.shape[1:], BF16),
            pltpu.VMEM(w_up.shape[1:], BF16),
            pltpu.VMEM(w_down.shape[1:], BF16),
            pltpu.SMEM((blocks,), jnp.int32),
            dma((3,)),
            dma((blocks,)),
            dma((blocks,)),
            dma((2, blocks)),
            dma,
        ],
        compiler_params=pltpu.CompilerParams(vmem_limit_bytes=VMEM_LIMIT),
        name="finish",
    )(nbr_table, nbr_count, gains, virtual, settled, keys, values, queries, latent, w_out, w_up, w_down)
    return result.reshape(own, width)


def solution(mesh):
    across = P(("members", "row"), None)
    in_specs = (across, P("row", None), P("row"), P("row", None)) + (P(),) * 8
    return jax.shard_map(body, mesh=mesh, in_specs=in_specs, out_specs=across, check_vma=False)
```

```python
import functools
import math

import jax
import jax.numpy as jnp
from jax import lax
from jax.experimental import pallas as pl
from jax.experimental.pallas import tpu as pltpu
from jax.sharding import PartitionSpec as P

HEADS = 4
HALO_B = 2
VMEM_LIMIT = 67_000_000
MESH = pl.DeviceIdType.MESH
BF16 = jnp.bfloat16
F32 = jnp.float32
AXIS = "row"


def normalize(values, scaling):
    centred = values - jnp.mean(values, axis=-1, keepdims=True)
    spread = jnp.mean(centred * centred, axis=-1, keepdims=True)
    return centred * lax.rsqrt(spread + 1e-05) * scaling


def dot(a, b, contract=((1,), (0,))):
    return lax.dot_general(a, b, (contract, ((), ())), preferred_element_type=F32)


def gelu(x):
    return 0.5 * x * (1.0 + jnp.tanh(math.sqrt(2 / math.pi) * (x + 0.044715 * x * x * x)))


def flip(a, b, bits):
    out = 0
    for bit in range(bits):
        weight = 1 << bit
        x = lax.rem(lax.div(a, jnp.int32(weight)), jnp.int32(2))
        y = lax.rem(lax.div(b, jnp.int32(weight)), jnp.int32(2))
        out = out + weight * lax.rem(x + y, jnp.int32(2))
    return out


def below(a, b):
    return jnp.minimum(jnp.maximum(b - a, 0), 1)


def equal(a, b):
    return 1 - jnp.minimum(jnp.maximum(a - b, b - a), 1)


def attend(count, key_of, value_of, query_of, context, at, listed, head, block):
    scale = math.log2(math.e) / math.sqrt(head)
    dead = [(1 - below(j, count)).astype(F32) * -1e30 for j in range(listed)]
    blank = jnp.zeros((head, block), BF16)
    for h in range(0, HEADS, 2):
        pair = slice(h * head, (h + 2) * head)
        upper = query_of(slice(h * head, (h + 1) * head))
        lower = query_of(slice((h + 1) * head, (h + 2) * head))
        both = jnp.concatenate(
            [jnp.concatenate([upper, blank], axis=1), jnp.concatenate([blank, lower], axis=1)], axis=0
        )
        scores = []
        for j in range(listed):
            s = dot(key_of(j, pair), both)
            scores.append(s if 2 * j < listed else s + dead[j])
        top = jnp.max(functools.reduce(jnp.maximum, scores), axis=0, keepdims=True)
        weights = [jnp.exp2((s - top) * scale) for s in scores]
        inverse = 1.0 / jnp.sum(functools.reduce(jnp.add, weights), axis=0, keepdims=True)
        probs = jnp.concatenate([w.astype(BF16) for w in weights], axis=0)
        mixed = dot(jnp.concatenate([value_of(j, pair) for j in range(listed)], axis=1), probs)
        for n in range(2):
            part = slice(n * block, (n + 1) * block)
            of_head = slice((h + n) * head, (h + n + 1) * head)
            context[of_head, at : at + block] = (mixed[n * head : (n + 1) * head, part] * inverse[:, part]).astype(BF16)


def feed(x, context, wo, wu, wd, gains_ref, layer):
    after_att = x + normalize(dot(context, wo, ((0,), (0,))), gains_ref[layer, 1:2, :])
    middle = normalize(after_att, gains_ref[layer, 2:3, :]).astype(BF16)
    hidden_size = wu.shape[-1]
    part = math.gcd(hidden_size, 512)
    down = None
    for f in range(0, hidden_size, part):
        hidden = gelu(dot(middle, wu[:, f : f + part])).astype(BF16)
        term = dot(hidden, wd[f : f + part, :])
        down = term if down is None else down + term
    return after_att + normalize(down, gains_ref[layer, 3:4, :])


def exchange_kernel(shapes, table_hbm, count_hbm, send_hbm, gains_hbm, x_hbm, wq_hbm, wk_hbm, wv_hbm, wo_hbm, wu_hbm,
                    wd_hbm, wm_hbm, settled_out, keys_out, values_out, queries_out, latent_out, virtual_ref, wq, wk, wv,
                    wo, wu, wd, wm, x_ref, normed, latent, keys, values, context, send_buf, far, halo_send, halo,
                    sum_send, sums, total_ref, early, asked, arranged, virtual, table_sm, count_sm, send_sm,
                    gains_ref, perm_sm, pos_sm, x_sem, small_sem, w_sem, far_send,
                    far_recv, halo_ssem, halo_rsem, sum_ssem, sum_rsem, table_sem, early_sem):
    peers, layers, blocks, block, width, slots, listed, group, node_total = shapes
    near = 2 * HALO_B + blocks
    bits = peers.bit_length() - 1
    half, quarter = peers // 2, peers // 4
    rows = group * block
    steps = blocks // group
    head = width // HEADS
    me = lax.axis_index(AXIS)
    inner = jnp.where((me >= quarter) & (me < half + quarter), 1, 0)

    def order(layer, k):
        outer = jnp.where(k < half, half + k, peers - 1 - k)
        lead = quarter // 2 if layer == 0 else quarter
        late = k - lead
        inside = jnp.where(
            late < 0, peers - 1 - k, jnp.where(late < half - 1, half - 1 - late, peers - 1 - lead - (late - half + 1))
        )
        return flip(me, jnp.where(inner == 1, inside, outer), bits)

    def remote(src, dst, ssem, rsem, to):
        return pltpu.make_async_remote_copy(
            src_ref=src, dst_ref=dst, send_sem=ssem, recv_sem=rsem, device_id={AXIS: to}, device_id_type=MESH
        )

    my_part = lax.div(me, jnp.int32(quarter))

    def far_out(layer, to):
        return remote(send_buf.at[layer, to], far.at[layer, me], far_send.at[layer], far_recv.at[layer, my_part], to)

    def far_some(layer, start, count, part):
        some = pl.ds(start, count)
        return remote(send_buf.at[layer, some], far.at[layer, some], far_send.at[layer], far_recv.at[layer, part], me)

    def sum_out(layer, to):
        return remote(sum_send.at[layer], sums.at[layer, me], sum_ssem.at[layer], sum_rsem.at[layer], to)

    def sum_all(layer):
        some = sums.at[layer, pl.ds(0, peers - 1)]
        return remote(some, some, sum_ssem.at[layer], sum_rsem.at[layer], me)

    def halo_copy(layer, side, to):
        return remote(
            halo_send.at[layer, side], halo.at[layer, 1 - side], halo_ssem.at[layer, side], halo_rsem.at[layer, 1 - side], to
        )

    middle_side = [jnp.where(me == half, 1, 0), jnp.where(me == half - 1, 1, 0)]
    middle = middle_side[0] + middle_side[1]

    def halo_each(act, across=None):
        for side in range(2):
            there = me > 0 if side == 0 else me < peers - 1
            if across is not None:
                there = there & (middle_side[side] == across)

            @pl.when(there)
            def _(side=side):
                act(side, me - 1 if side == 0 else me + 1)

    load_x = pltpu.make_async_copy(x_hbm, x_ref, x_sem)
    load_x.start()
    smalls = [
        pltpu.make_async_copy(src, dst, small_sem.at[n])
        for n, (src, dst) in enumerate(
            ((gains_hbm, gains_ref), (send_hbm, send_sm), (table_hbm, table_sm), (count_hbm, count_sm))
        )
    ]
    for small in smalls:
        small.start()
    barrier = pltpu.get_barrier_semaphore()

    def greet(k, carry):
        pl.semaphore_signal(barrier, inc=1, device_id={AXIS: lax.rem(me + k, peers)}, device_id_type=MESH)
        return carry

    lax.fori_loop(1, peers, greet, 0)
    loads = []
    for n, (src, dst) in enumerate(
        ((wk_hbm, wk), (wv_hbm, wv), (wm_hbm, wm), (wq_hbm, wq), (wo_hbm, wo), (wu_hbm, wu), (wd_hbm, wd))
    ):
        loads.append(pltpu.make_async_copy(src, dst, w_sem.at[n]))
    total_ref[0:1, :] = jnp.zeros((1, width), F32)
    load_x.wait()
    for small in smalls:
        small.wait()
    for load in loads:
        load.start()

    def first(i, carry):
        x = x_ref[pl.ds(i * group, group)].reshape(rows, width).astype(F32)
        total_ref[0:1, :] = total_ref[0:1, :] + jnp.sum(x, axis=0, keepdims=True)
        fresh = normalize(x, gains_ref[0, 0:1, :]).astype(BF16)
        normed[0, pl.ds(i * group, group)] = fresh.reshape(group, block, width)
        return carry

    lax.fori_loop(0, steps, first, 0)

    def stage(layer, to):
        for slot in range(slots):
            at = send_sm[to * slots + slot]
            if layer > 0:
                at = pos_sm[at]
            send_buf[layer, to, pl.ds(slot * block, block), :] = normed[layer, at]

    def stage_self(layer):
        for slot in range(slots):
            at = send_sm[me * slots + slot]
            if layer > 0:
                at = pos_sm[at]
            far[layer, me, pl.ds(slot * block, block), :] = normed[layer, at]

    def stage_halo(layer, side):
        for b in range(HALO_B):
            at = b if side == 0 else blocks - HALO_B + b
            if layer > 0:
                at = pos_sm[at]
            halo_send[layer, side, pl.ds(b * block, block), :] = normed[layer, at]

    def send_halo(layer, across=None):
        halo_each(lambda side, to: halo_copy(layer, side, to).start(), across)

    def stage_sum(layer):
        for k in range(width // 128):
            part = total_ref[0:1, k * 128 : (k + 1) * 128]
            sum_send[layer, k : k + 1, :] = part
            sums[layer, me, k : k + 1, :] = part

    def send_sum(layer):
        def one(k, carry):
            sum_out(layer, lax.rem(me + k, peers)).start()
            return carry

        lax.fori_loop(1, peers, one, 0)

    def stage_all(k, carry):
        stage(0, order(0, k))
        return carry

    def send_all(k, carry):
        far_out(0, order(0, k)).start()
        return carry

    stage_sum(0)
    halo_each(lambda side, to: stage_halo(0, side))
    lax.fori_loop(0, peers - 1, stage_all, 0)
    pl.semaphore_wait(barrier, peers - 1)
    send_halo(0)
    send_sum(0)
    lax.fori_loop(0, peers - 1, send_all, 0)
    stage_self(0)

    uses = [jnp.int32(peers * slots + n) for n in range(blocks)]
    for k in range(peers - 2, -1, -1):
        to = order(1, jnp.int32(k))
        for slot in range(slots - 1, -1, -1):
            b = send_sm[to * slots + slot]
            uses = [use + equal(b, n) * (k * slots + slot - use) for n, use in enumerate(uses)]
    for n in range(HALO_B):
        low, high = n, blocks - HALO_B + n
        uses[low] = uses[low] - middle_side[0] * 2 * peers * slots
        uses[high] = uses[high] - middle_side[1] * 2 * peers * slots
    places = []
    for n in range(blocks):
        place = jnp.int32(0)
        for other in range(blocks):
            if other != n:
                place = place + below(uses[other], uses[n])
        places.append(place)
        pos_sm[n] = place
    for n in range(blocks):
        which = jnp.int32(0)
        for b in range(blocks):
            which = which + equal(places[b], n) * b
        perm_sm[n] = which
    def project(layer, piece, at):
        count = piece.shape[0]
        flat = piece.reshape(count * block, width)
        keys[pl.ds(at, count)] = dot(flat, wk[layer]).astype(BF16).reshape(count, block, width)
        turned = dot(wv[layer], flat, ((0,), (1,))).astype(BF16)
        for n in range(count):
            values[at + n] = turned[:, n * block : (n + 1) * block]

    def export(at, count, n):
        part = pl.ds(at, count)
        return (
            pltpu.make_async_copy(keys.at[part], keys_out.at[part], table_sem.at[0, n]),
            pltpu.make_async_copy(values.at[part], values_out.at[part], table_sem.at[1, n]),
        )

    chunk = math.gcd(blocks, 4)
    many = math.gcd(quarter, 4)

    def hand_on(layer, at, count, n):
        if layer == layers - 1:
            for copy in export(at, count, n):
                copy.start()

    def gather(layer):
        def own_piece(i, carry):
            if layer == 0:
                piece = normed[layer, pl.ds(i * chunk, chunk)]
            else:
                piece = jnp.concatenate([normed[layer, pos_sm[i * chunk + n]] for n in range(chunk)], axis=0)
                piece = piece.reshape(chunk, block, width)
            project(layer, piece, HALO_B + i * chunk)
            hand_on(layer, HALO_B + i * chunk, chunk, 0)
            return carry

        lax.fori_loop(0, blocks // chunk, own_piece, 0)

        def halo_in(copy, side):
            copy.wait_recv()
            at = 0 if side == 0 else HALO_B + blocks
            project(layer, halo[layer, side].reshape(HALO_B, block, width), at)
            hand_on(layer, at, HALO_B, 2 + side)

        @pl.when(me > 0)
        def _():
            halo_in(halo_copy(layer, 1, me - 1), 0)

        @pl.when(me < peers - 1)
        def _():
            halo_in(halo_copy(layer, 0, me + 1), 1)

        if layer == layers - 1:
            lax.fori_loop(0, steps, early_step, 0)
            drain(0)
        for n, (inside, outside) in enumerate(((2, 0), (0, 1), (1, 3), (3, 2))):
            if n == 3:
                sum_all(layer).wait_recv()
                whole = jnp.sum(sums[layer], axis=0)
                mean = jnp.concatenate([whole[k : k + 1, :] for k in range(width // 128)], axis=1) / node_total
                mean = jnp.broadcast_to(mean, (16, width)).astype(BF16)
                virtual[...] = dot(mean, wm[layer])
                if layer == layers - 1:
                    virtual_ref[...] = virtual[...]
                    lax.fori_loop(0, blocks, settle, 0)
                    settled.start()
            part = flip(my_part, jnp.where(inner == 1, inside, outside), 2)
            start = part * quarter

            @pl.when(part == my_part)
            def _(part=part, start=start):
                far_some(layer, start, quarter - 1, part).wait_recv()

            @pl.when(part != my_part)
            def _(part=part, start=start):
                far_some(layer, start, quarter, part).wait_recv()

            def far_piece(i, carry, start=start):
                source = start + i * many
                piece = far[layer, pl.ds(source, many)].reshape(many * slots, block, width)
                project(layer, piece, near + source * slots)
                hand_on(layer, near + source * slots, many * slots, 1)
                return carry

            lax.fori_loop(0, quarter // many, far_piece, 0)

    def attend_in(layer, which, queries, at):
        count = count_sm[which]
        home = table_sm[which, 0]
        spots = []
        for j in range(listed):
            entry = table_sm[which, j]
            if 2 * j >= listed:
                entry = home + below(j, count) * (entry - home)
            spots.append(entry)
        attend(
            count,
            lambda j, pair: keys[spots[j], :, pair],
            lambda j, pair: values[spots[j], pair],
            lambda part: queries[part, at : at + block],
            context,
            at,
            listed,
            head,
            block,
        )

    def early_copies(start, count):
        at = pl.ds(start, count)
        return (
            pltpu.make_async_copy(asked.at[at], queries_out.at[at], early_sem.at[0]),
            pltpu.make_async_copy(arranged.at[at], latent_out.at[at], early_sem.at[1]),
        )

    def block_step(layer, i):
        last = layer == layers - 1
        order_at = [i * group + g for g in range(group)]
        if last:
            which = order_at
            source = [pos_sm[w] for w in which]
            for w, s in zip(which, source):
                arranged[w] = latent[s]
        else:
            which = [perm_sm[n] for n in order_at]
            source = which
        mine = jnp.concatenate([normed[layer, s] for s in source], axis=0)
        queries = dot(wq[layer], mine, ((0,), (1,))).astype(BF16)
        if last:
            for g in range(group):
                asked[which[g]] = queries[:, g * block : (g + 1) * block]
        for g in range(group):
            attend_in(layer, which[g], queries, g * block)
        current = latent if layer > 0 else x_ref
        x = jnp.concatenate([current[s] for s in source], axis=0).astype(F32)
        result = feed(x, context[...], wo[layer], wu.at[layer], wd.at[layer], gains_ref, layer)
        at = pl.ds(i * group, group)
        if last:
            early[at] = result.reshape(group, block, width)
            for copy in early_copies(i * group, group):
                copy.start()
        else:
            result = (result + virtual[0:1, :]).astype(BF16)
            latent[at] = result.reshape(group, block, width)
            wide = result.astype(F32)
            fresh = normalize(wide, gains_ref[layer + 1, 0:1, :]).astype(BF16)
            normed[layer + 1, at] = fresh.reshape(group, block, width)
            total_ref[0:1, :] = total_ref[0:1, :] + jnp.sum(wide, axis=0, keepdims=True)

    def early_step(i, carry):
        block_step(layers - 1, i)
        return carry

    def drain(layer):
        far_some(layer, 0, peers - 1, my_part).wait_send()
        sum_all(layer).wait_send()
        halo_each(lambda side, to: halo_copy(layer, side, to).wait_send())

    settled = pltpu.make_async_copy(latent, settled_out, x_sem)

    def settle(b, carry):
        latent[b] = (early[b] + virtual[0:1, :]).astype(BF16)
        return carry

    for load in loads[:3]:
        load.wait()
    gather(0)
    for load in loads[3:]:
        load.wait()
    total_ref[0:1, :] = jnp.zeros((1, width), F32)

    def sending_step(i, carry):
        block_step(0, i)

        @pl.when(i == 0)
        def _():
            halo_each(lambda side, to: stage_halo(1, side), 1)

        @pl.when(i == steps - 1)
        def _():
            halo_each(lambda side, to: stage_halo(1, side), 0)
            stage_sum(1)

        held = HALO_B * middle
        begin = jnp.maximum(i * group - held, 0)
        end = (i + 1) * group - held
        def each(k, carry):
            stage(1, order(1, k))
            return carry

        def go(k, carry):
            far_out(1, order(1, k)).start()
            return carry

        until = jnp.where(i == steps - 1, peers - 1, end)
        lax.fori_loop(begin, until, each, 0)

        @pl.when(i == 0)
        def _():
            send_halo(1, 1)

        @pl.when(i == steps - 1)
        def _():
            send_halo(1, 0)
            send_sum(1)

        lax.fori_loop(begin, until, go, 0)
        return carry

    lax.fori_loop(0, steps, sending_step, 0)
    stage_self(1)

    gather(1)
    drain(1)
    for start, count, n in ((HALO_B, blocks, 0), (near, peers * slots, 1)):
        for copy in export(start, count, n):
            copy.wait()

    @pl.when(me > 0)
    def _():
        for copy in export(0, HALO_B, 2):
            copy.wait()

    @pl.when(me < peers - 1)
    def _():
        for copy in export(HALO_B + blocks, HALO_B, 3):
            copy.wait()

    for copy in early_copies(0, blocks):
        copy.wait()
    settled.wait()


def finish_kernel(layer, near, group, table_sm, count_sm, gains_ref, virtual_ref, settled_hbm, keys_hbm, values_hbm,
                  queries_hbm, latent_hbm, wo_hbm, wu_hbm, wd_hbm, out_hbm, kept_keys, kept_values, asked, current, context,
                  kept, wo, wu, wd, todo_sm, w_sem, key_sem, value_sem, row_sem, kept_sem):
    blocks, block, width = kept.shape
    listed = table_sm.shape[1]
    head = width // HEADS
    weight_loads = [
        pltpu.make_async_copy(src.at[layer], dst, w_sem.at[n])
        for n, (src, dst) in enumerate(((wo_hbm, wo), (wu_hbm, wu), (wd_hbm, wd)))
    ]
    number = jnp.int32(0)
    for b in range(blocks):
        away = jnp.int32(0)
        for j in range(listed):
            away = jnp.where((j < count_sm[b]) & (table_sm[b, j] >= near), 1, away)

        @pl.when(away > 0)
        def _(b=b, number=number):
            todo_sm[number] = b

        number = number + away

    def block_of(n):
        return todo_sm[jnp.minimum(n, number - 1)]

    def rows(n):
        which = block_of(n)
        return (
            pltpu.make_async_copy(queries_hbm.at[which], asked.at[n], row_sem.at[0, n]),
            pltpu.make_async_copy(latent_hbm.at[which], current.at[n], row_sem.at[1, n]),
        )

    def fetch(n, carry):
        which = block_of(n)
        for copy in rows(n):
            copy.start()
        for j in range(listed):
            entry = table_sm[which, j * below(j, count_sm[which])]
            pltpu.make_async_copy(keys_hbm.at[entry], kept_keys.at[n, j], key_sem.at[n]).start()
            pltpu.make_async_copy(values_hbm.at[entry], kept_values.at[n, j], value_sem.at[n]).start()
        return carry

    def fetched(n):
        for copy in rows(n):
            copy.wait()
        some = pl.ds(0, listed)
        pltpu.make_async_copy(keys_hbm.at[some], kept_keys.at[n], key_sem.at[n]).wait()
        pltpu.make_async_copy(values_hbm.at[some], kept_values.at[n], value_sem.at[n]).wait()

    load_kept = pltpu.make_async_copy(settled_hbm, kept, kept_sem)
    together = context.shape[2] // block
    turns = (number + together - 1) // together

    def attend_some(i, carry):
        for g in range(together):
            pl.when(i * together + g < number)(lambda g=g: fetched(i * together + g))

        lax.fori_loop((i + 1) * together, jnp.minimum((i + 2) * together, number), fetch, 0)

        @pl.when(i == 0)
        def _():
            for load in weight_loads:
                load.start()
            load_kept.start()

        for g in range(together):
            n = i * together + g
            attend(
                count_sm[block_of(n)],
                lambda j, pair, n=n: kept_keys[n, j, :, pair],
                lambda j, pair, n=n: kept_values[n, j, pair, :],
                lambda part, n=n: asked[n, part, :],
                context.at[i],
                g * block,
                listed,
                head,
                block,
            )
        return carry

    def feed_some(i, parts):
        size = parts * together
        first = i * group
        x = current[pl.ds(first, size)].reshape(size * block, width).astype(F32)
        mixed = jnp.concatenate([context[i * (group // together) + n] for n in range(parts)], axis=1)
        result = feed(x, mixed, wo[...], wu, wd, gains_ref, layer) + virtual_ref[0:1, :]
        result = result.astype(BF16).reshape(size, block, width)
        for g in range(size):

            @pl.when(first + g < number)
            def _(g=g):
                kept[block_of(first + g)] = result[g]

    def feed_turns(i, carry):
        left = number - i * group
        if group > together:
            pl.when(left > together)(lambda: feed_some(i, group // together))
            pl.when(left <= together)(lambda: feed_some(i, 1))
        else:
            feed_some(i, 1)
        return carry

    @pl.when(number > 0)
    def _():
        lax.fori_loop(0, jnp.minimum(together, number), fetch, 0)
        lax.fori_loop(0, turns, attend_some, 0)
        for load in weight_loads:
            load.wait()
        load_kept.wait()
        lax.fori_loop(0, (number + group - 1) // group, feed_turns, 0)

    @pl.when(number == 0)
    def _():
        load_kept.start()
        load_kept.wait()

    give = pltpu.make_async_copy(kept, out_hbm, kept_sem)
    give.start()
    give.wait()


def body(node_features, nbr_table, nbr_count, send_block, w_query, w_key, w_value, w_out, w_up, w_down, w_virtual, gains):
    blocks, listed = nbr_table.shape
    own, width = node_features.shape
    block = own // blocks
    peers = lax.axis_size(AXIS)
    slots = send_block.shape[1]
    layers = w_query.shape[0]
    group = math.gcd(blocks, 4)
    near = 2 * HALO_B + blocks
    entries = near + peers * slots
    shapes = (peers, layers, blocks, block, width, slots, listed, group, own * peers)
    weights = (w_query, w_key, w_value, w_out, w_up, w_down, w_virtual)
    vmem, smem, hbm = (pl.BlockSpec(memory_space=s) for s in (pltpu.VMEM, pltpu.SMEM, pl.ANY))
    dma = pltpu.SemaphoreType.DMA
    shape = jax.ShapeDtypeStruct
    scratch = [pltpu.VMEM(w.shape, BF16) for w in weights]
    scratch += [
        pltpu.VMEM((blocks, block, width), BF16),
        pltpu.VMEM((layers, blocks, block, width), BF16),
        pltpu.VMEM((blocks, block, width), BF16),
        pltpu.VMEM((entries, block, width), BF16),
        pltpu.VMEM((entries, width, block), BF16),
        pltpu.VMEM((width, group * block), BF16),
        pltpu.VMEM((layers, peers, slots * block, width), BF16),
        pltpu.VMEM((layers, peers, slots * block, width), BF16),
        pltpu.VMEM((layers, 2, HALO_B * block, width), BF16),
        pltpu.VMEM((layers, 2, HALO_B * block, width), BF16),
        pltpu.VMEM((layers, width // 128, 128), F32),
        pltpu.VMEM((layers, peers, width // 128, 128), F32),
        pltpu.VMEM((8, width), F32),
        pltpu.VMEM((blocks, block, width), F32),
        pltpu.VMEM((blocks, width, block), BF16),
        pltpu.VMEM((blocks, block, width), BF16),
        pltpu.VMEM((16, width), F32),
        pltpu.SMEM(nbr_table.shape, jnp.int32),
        pltpu.SMEM(nbr_count.shape, jnp.int32),
        pltpu.SMEM((peers * slots,), jnp.int32),
        pltpu.VMEM(gains.shape, F32),
        pltpu.SMEM((blocks,), jnp.int32),
        pltpu.SMEM((blocks,), jnp.int32),
        dma,
        dma((4,)),
        dma((len(weights),)),
        dma((layers,)),
        dma((layers, 4)),
        dma((layers, 2)),
        dma((layers, 2)),
        dma((layers,)),
        dma((layers,)),
        dma((2, 4)),
        dma((2,)),
    ]
    settled, keys, values, queries, latent, virtual = pl.pallas_call(
        functools.partial(exchange_kernel, shapes),
        out_shape=(
            shape((blocks, block, width), BF16),
            shape((entries, block, width), BF16),
            shape((entries, width, block), BF16),
            shape((blocks, width, block), BF16),
            shape((blocks, block, width), BF16),
            shape((16, width), F32),
        ),
        in_specs=[hbm] * (5 + len(weights)),
        out_specs=(hbm, hbm, hbm, hbm, hbm, vmem),
        scratch_shapes=scratch,
        compiler_params=pltpu.CompilerParams(collective_id=0, has_side_effects=True, vmem_limit_bytes=VMEM_LIMIT),
        name="exchange",
    )(nbr_table, nbr_count, send_block.reshape(-1), gains, node_features.reshape(blocks, block, width), *weights)
    result = pl.pallas_call(
        functools.partial(finish_kernel, layers - 1, near, group),
        out_shape=shape((blocks, block, width), BF16),
        in_specs=[smem, smem, vmem, vmem] + [hbm] * 8,
        out_specs=hbm,
        scratch_shapes=[
            pltpu.VMEM((blocks, listed, block, width), BF16),
            pltpu.VMEM((blocks, listed, width, block), BF16),
            pltpu.VMEM((blocks, width, block), BF16),
            pltpu.VMEM((blocks, block, width), BF16),
            pltpu.VMEM((blocks // math.gcd(group, 2), width, math.gcd(group, 2) * block), BF16),
            pltpu.VMEM((blocks, block, width), BF16),
            pltpu.VMEM(w_out.shape[1:], BF16),
            pltpu.VMEM(w_up.shape[1:], BF16),
            pltpu.VMEM(w_down.shape[1:], BF16),
            pltpu.SMEM((blocks,), jnp.int32),
            dma((3,)),
            dma((blocks,)),
            dma((blocks,)),
            dma((2, blocks)),
            dma,
        ],
        compiler_params=pltpu.CompilerParams(vmem_limit_bytes=VMEM_LIMIT),
        name="finish",
    )(nbr_table, nbr_count, gains, virtual, settled, keys, values, queries, latent, w_out, w_up, w_down)
    return result.reshape(own, width)


def solution(mesh):
    across = P(("members", "row"), None)
    in_specs = (across, P("row", None), P("row"), P("row", None)) + (P(),) * 8
    return jax.shard_map(body, mesh=mesh, in_specs=in_specs, out_specs=across, check_vma=False)
```

```python
import functools
import math

import jax
import jax.numpy as jnp
from jax import lax
from jax.experimental import pallas as pl
from jax.experimental.pallas import tpu as pltpu
from jax.sharding import PartitionSpec as P

HEADS = 4
HALO_B = 2
VMEM_LIMIT = 67_000_000
MESH = pl.DeviceIdType.MESH
BF16 = jnp.bfloat16
F32 = jnp.float32
AXIS = "row"


def normalize(values, scaling):
    centred = values - jnp.mean(values, axis=-1, keepdims=True)
    spread = jnp.mean(centred * centred, axis=-1, keepdims=True)
    return centred * lax.rsqrt(spread + 1e-05) * scaling


def dot(a, b, contract=((1,), (0,))):
    return lax.dot_general(a, b, (contract, ((), ())), preferred_element_type=F32)


def gelu(x):
    return 0.5 * x * (1.0 + jnp.tanh(math.sqrt(2 / math.pi) * (x + 0.044715 * x * x * x)))


def flip(a, b, bits):
    out = 0
    for bit in range(bits):
        weight = 1 << bit
        x = lax.rem(lax.div(a, jnp.int32(weight)), jnp.int32(2))
        y = lax.rem(lax.div(b, jnp.int32(weight)), jnp.int32(2))
        out = out + weight * lax.rem(x + y, jnp.int32(2))
    return out


def below(a, b):
    return jnp.minimum(jnp.maximum(b - a, 0), 1)


def equal(a, b):
    return 1 - jnp.minimum(jnp.maximum(a - b, b - a), 1)


def attend(count, key_of, value_of, query_of, context, at, listed, head, block):
    scale = math.log2(math.e) / math.sqrt(head)
    dead = [(1 - below(j, count)).astype(F32) * -1e30 for j in range(listed)]
    blank = jnp.zeros((head, block), BF16)
    for h in range(0, HEADS, 2):
        pair = slice(h * head, (h + 2) * head)
        upper = query_of(slice(h * head, (h + 1) * head))
        lower = query_of(slice((h + 1) * head, (h + 2) * head))
        both = jnp.concatenate(
            [jnp.concatenate([upper, blank], axis=1), jnp.concatenate([blank, lower], axis=1)], axis=0
        )
        scores = []
        for j in range(listed):
            s = dot(key_of(j, pair), both)
            scores.append(s if 2 * j < listed else s + dead[j])
        top = jnp.max(functools.reduce(jnp.maximum, scores), axis=0, keepdims=True)
        weights = [jnp.exp2((s - top) * scale) for s in scores]
        inverse = 1.0 / jnp.sum(functools.reduce(jnp.add, weights), axis=0, keepdims=True)
        probs = jnp.concatenate([w.astype(BF16) for w in weights], axis=0)
        mixed = dot(jnp.concatenate([value_of(j, pair) for j in range(listed)], axis=1), probs)
        for n in range(2):
            part = slice(n * block, (n + 1) * block)
            of_head = slice((h + n) * head, (h + n + 1) * head)
            context[of_head, at : at + block] = (mixed[n * head : (n + 1) * head, part] * inverse[:, part]).astype(BF16)


def feed(x, context, wo, wu, wd, gains_ref, layer):
    after_att = x + normalize(dot(context, wo, ((0,), (0,))), gains_ref[layer, 1:2, :])
    middle = normalize(after_att, gains_ref[layer, 2:3, :]).astype(BF16)
    hidden_size = wu.shape[-1]
    part = math.gcd(hidden_size, 512)
    down = None
    for f in range(0, hidden_size, part):
        hidden = gelu(dot(middle, wu[:, f : f + part])).astype(BF16)
        term = dot(hidden, wd[f : f + part, :])
        down = term if down is None else down + term
    return after_att + normalize(down, gains_ref[layer, 3:4, :])


class Parts:
    def __init__(self, src, dst, sem, parts):
        self.whole = pltpu.make_async_copy(src, dst, sem)
        size = dst.shape[0] // math.gcd(dst.shape[0], parts)
        slices = [pl.ds(start, size) for start in range(0, dst.shape[0], size)]
        self.pieces = [pltpu.make_async_copy(src.at[part], dst.at[part], sem) for part in slices]

    def start(self):
        for piece in self.pieces:
            piece.start()

    def wait(self):
        self.whole.wait()


def exchange_kernel(shapes, table_hbm, count_hbm, send_hbm, gains_hbm, x_hbm, wq_hbm, wk_hbm, wv_hbm, wo_hbm, wu_hbm,
                    wd_hbm, wm_hbm, settled_out, keys_out, values_out, queries_out, latent_out, virtual_ref, wq, wk, wv,
                    wo, wu, wd, wm, x_ref, normed, latent, keys, values, context, send_buf, far, halo_send, halo,
                    sum_send, sums, total_ref, early, asked, arranged, virtual, table_sm, count_sm, send_sm,
                    gains_ref, perm_sm, pos_sm, x_sem, small_sem, w_sem, far_send,
                    far_recv, halo_ssem, halo_rsem, sum_ssem, sum_rsem, table_sem, early_sem):
    peers, layers, blocks, block, width, slots, listed, group, node_total = shapes
    near = 2 * HALO_B + blocks
    bits = peers.bit_length() - 1
    half, quarter = peers // 2, peers // 4
    rows = group * block
    steps = blocks // group
    head = width // HEADS
    me = lax.axis_index(AXIS)
    inner = jnp.where((me >= quarter) & (me < half + quarter), 1, 0)

    def order(layer, k):
        outer = jnp.where(k < half, half + k, peers - 1 - k)
        lead = quarter // 2 if layer == 0 else quarter
        late = k - lead
        inside = jnp.where(
            late < 0, peers - 1 - k, jnp.where(late < half - 1, half - 1 - late, peers - 1 - lead - (late - half + 1))
        )
        return flip(me, jnp.where(inner == 1, inside, outer), bits)

    def remote(src, dst, ssem, rsem, to):
        return pltpu.make_async_remote_copy(
            src_ref=src, dst_ref=dst, send_sem=ssem, recv_sem=rsem, device_id={AXIS: to}, device_id_type=MESH
        )

    my_part = lax.div(me, jnp.int32(quarter))

    def far_out(layer, to):
        return remote(send_buf.at[layer, to], far.at[layer, me], far_send.at[layer], far_recv.at[layer, my_part], to)

    def far_some(layer, start, count, part):
        some = pl.ds(start, count)
        return remote(send_buf.at[layer, some], far.at[layer, some], far_send.at[layer], far_recv.at[layer, part], me)

    def sum_out(layer, to):
        return remote(sum_send.at[layer], sums.at[layer, me], sum_ssem.at[layer], sum_rsem.at[layer], to)

    def sum_all(layer):
        some = sums.at[layer, pl.ds(0, peers - 1)]
        return remote(some, some, sum_ssem.at[layer], sum_rsem.at[layer], me)

    def halo_copy(layer, side, to):
        return remote(
            halo_send.at[layer, side], halo.at[layer, 1 - side], halo_ssem.at[layer, side], halo_rsem.at[layer, 1 - side], to
        )

    middle_side = [jnp.where(me == half, 1, 0), jnp.where(me == half - 1, 1, 0)]
    middle = middle_side[0] + middle_side[1]

    def halo_each(act, across=None):
        for side in range(2):
            there = me > 0 if side == 0 else me < peers - 1
            if across is not None:
                there = there & (middle_side[side] == across)

            @pl.when(there)
            def _(side=side):
                act(side, me - 1 if side == 0 else me + 1)

    load_x = Parts(x_hbm, x_ref, x_sem, 8)
    load_x.start()
    smalls = [
        pltpu.make_async_copy(src, dst, small_sem.at[n])
        for n, (src, dst) in enumerate(
            ((gains_hbm, gains_ref), (send_hbm, send_sm), (table_hbm, table_sm), (count_hbm, count_sm))
        )
    ]
    for small in smalls:
        small.start()
    barrier = pltpu.get_barrier_semaphore()

    def greet(k, carry):
        pl.semaphore_signal(barrier, inc=1, device_id={AXIS: lax.rem(me + k, peers)}, device_id_type=MESH)
        return carry

    lax.fori_loop(1, peers, greet, 0)
    loads = []
    for n, (src, dst) in enumerate(
        ((wk_hbm, wk), (wv_hbm, wv), (wm_hbm, wm), (wq_hbm, wq), (wo_hbm, wo), (wu_hbm, wu), (wd_hbm, wd))
    ):
        loads.append(pltpu.make_async_copy(src, dst, w_sem.at[n]))
    total_ref[0:1, :] = jnp.zeros((1, width), F32)
    load_x.wait()
    for small in smalls:
        small.wait()
    for load in loads:
        load.start()

    def first(i, carry):
        x = x_ref[pl.ds(i * group, group)].reshape(rows, width).astype(F32)
        total_ref[0:1, :] = total_ref[0:1, :] + jnp.sum(x, axis=0, keepdims=True)
        fresh = normalize(x, gains_ref[0, 0:1, :]).astype(BF16)
        normed[0, pl.ds(i * group, group)] = fresh.reshape(group, block, width)
        return carry

    lax.fori_loop(0, steps, first, 0)

    def stage(layer, to):
        for slot in range(slots):
            at = send_sm[to * slots + slot]
            if layer > 0:
                at = pos_sm[at]
            send_buf[layer, to, pl.ds(slot * block, block), :] = normed[layer, at]

    def stage_self(layer):
        for slot in range(slots):
            at = send_sm[me * slots + slot]
            if layer > 0:
                at = pos_sm[at]
            far[layer, me, pl.ds(slot * block, block), :] = normed[layer, at]

    def stage_halo(layer, side):
        for b in range(HALO_B):
            at = b if side == 0 else blocks - HALO_B + b
            if layer > 0:
                at = pos_sm[at]
            halo_send[layer, side, pl.ds(b * block, block), :] = normed[layer, at]

    def send_halo(layer, across=None):
        halo_each(lambda side, to: halo_copy(layer, side, to).start(), across)

    def stage_sum(layer):
        for k in range(width // 128):
            part = total_ref[0:1, k * 128 : (k + 1) * 128]
            sum_send[layer, k : k + 1, :] = part
            sums[layer, me, k : k + 1, :] = part

    def send_sum(layer):
        def one(k, carry):
            sum_out(layer, lax.rem(me + k, peers)).start()
            return carry

        lax.fori_loop(1, peers, one, 0)

    def stage_all(k, carry):
        stage(0, order(0, k))
        return carry

    def send_all(k, carry):
        far_out(0, order(0, k)).start()
        return carry

    stage_sum(0)
    halo_each(lambda side, to: stage_halo(0, side))
    lax.fori_loop(0, peers - 1, stage_all, 0)
    pl.semaphore_wait(barrier, peers - 1)
    send_halo(0)
    send_sum(0)
    lax.fori_loop(0, peers - 1, send_all, 0)
    stage_self(0)

    uses = [jnp.int32(peers * slots + n) for n in range(blocks)]
    for k in range(peers - 2, -1, -1):
        to = order(1, jnp.int32(k))
        for slot in range(slots - 1, -1, -1):
            b = send_sm[to * slots + slot]
            uses = [use + equal(b, n) * (k * slots + slot - use) for n, use in enumerate(uses)]
    for n in range(HALO_B):
        low, high = n, blocks - HALO_B + n
        uses[low] = uses[low] - middle_side[0] * 2 * peers * slots
        uses[high] = uses[high] - middle_side[1] * 2 * peers * slots
    places = []
    for n in range(blocks):
        place = jnp.int32(0)
        for other in range(blocks):
            if other != n:
                place = place + below(uses[other], uses[n])
        places.append(place)
        pos_sm[n] = place
    for n in range(blocks):
        which = jnp.int32(0)
        for b in range(blocks):
            which = which + equal(places[b], n) * b
        perm_sm[n] = which
    def project(layer, piece, at):
        count = piece.shape[0]
        flat = piece.reshape(count * block, width)
        keys[pl.ds(at, count)] = dot(flat, wk[layer]).astype(BF16).reshape(count, block, width)
        turned = dot(wv[layer], flat, ((0,), (1,))).astype(BF16)
        for n in range(count):
            values[at + n] = turned[:, n * block : (n + 1) * block]

    def export(at, count, n):
        part = pl.ds(at, count)
        return (
            pltpu.make_async_copy(keys.at[part], keys_out.at[part], table_sem.at[0, n]),
            pltpu.make_async_copy(values.at[part], values_out.at[part], table_sem.at[1, n]),
        )

    chunk = math.gcd(blocks, 4)
    many = math.gcd(quarter, 4)

    def hand_on(layer, at, count, n):
        if layer == layers - 1:
            for copy in export(at, count, n):
                copy.start()

    def gather(layer):
        def own_piece(i, carry):
            if layer == 0:
                piece = normed[layer, pl.ds(i * chunk, chunk)]
            else:
                piece = jnp.concatenate([normed[layer, pos_sm[i * chunk + n]] for n in range(chunk)], axis=0)
                piece = piece.reshape(chunk, block, width)
            project(layer, piece, HALO_B + i * chunk)
            hand_on(layer, HALO_B + i * chunk, chunk, 0)
            return carry

        lax.fori_loop(0, blocks // chunk, own_piece, 0)

        def halo_in(copy, side):
            copy.wait_recv()
            at = 0 if side == 0 else HALO_B + blocks
            project(layer, halo[layer, side].reshape(HALO_B, block, width), at)
            hand_on(layer, at, HALO_B, 2 + side)

        @pl.when(me > 0)
        def _():
            halo_in(halo_copy(layer, 1, me - 1), 0)

        @pl.when(me < peers - 1)
        def _():
            halo_in(halo_copy(layer, 0, me + 1), 1)

        if layer == layers - 1:
            lax.fori_loop(0, steps, early_step, 0)
            drain(0)
        for n, (inside, outside) in enumerate(((2, 0), (0, 1), (1, 3), (3, 2))):
            if n == 3:
                sum_all(layer).wait_recv()
                whole = jnp.sum(sums[layer], axis=0)
                mean = jnp.concatenate([whole[k : k + 1, :] for k in range(width // 128)], axis=1) / node_total
                mean = jnp.broadcast_to(mean, (16, width)).astype(BF16)
                virtual[...] = dot(mean, wm[layer])
                if layer == layers - 1:
                    virtual_ref[...] = virtual[...]
                    lax.fori_loop(0, blocks, settle, 0)
                    settled.start()
            part = flip(my_part, jnp.where(inner == 1, inside, outside), 2)
            start = part * quarter

            @pl.when(part == my_part)
            def _(part=part, start=start):
                far_some(layer, start, quarter - 1, part).wait_recv()

            @pl.when(part != my_part)
            def _(part=part, start=start):
                far_some(layer, start, quarter, part).wait_recv()

            def far_piece(i, carry, start=start):
                source = start + i * many
                piece = far[layer, pl.ds(source, many)].reshape(many * slots, block, width)
                project(layer, piece, near + source * slots)
                hand_on(layer, near + source * slots, many * slots, 1)
                return carry

            lax.fori_loop(0, quarter // many, far_piece, 0)

    def attend_in(layer, which, queries, at):
        count = count_sm[which]
        home = table_sm[which, 0]
        spots = []
        for j in range(listed):
            entry = table_sm[which, j]
            if 2 * j >= listed:
                entry = home + below(j, count) * (entry - home)
            spots.append(entry)
        attend(
            count,
            lambda j, pair: keys[spots[j], :, pair],
            lambda j, pair: values[spots[j], pair],
            lambda part: queries[part, at : at + block],
            context,
            at,
            listed,
            head,
            block,
        )

    def early_copies(start, count):
        at = pl.ds(start, count)
        return (
            pltpu.make_async_copy(asked.at[at], queries_out.at[at], early_sem.at[0]),
            pltpu.make_async_copy(arranged.at[at], latent_out.at[at], early_sem.at[1]),
        )

    def block_step(layer, i):
        last = layer == layers - 1
        order_at = [i * group + g for g in range(group)]
        if last:
            which = order_at
            source = [pos_sm[w] for w in which]
            for w, s in zip(which, source):
                arranged[w] = latent[s]
        else:
            which = [perm_sm[n] for n in order_at]
            source = which
        mine = jnp.concatenate([normed[layer, s] for s in source], axis=0)
        queries = dot(wq[layer], mine, ((0,), (1,))).astype(BF16)
        if last:
            for g in range(group):
                asked[which[g]] = queries[:, g * block : (g + 1) * block]
        for g in range(group):
            attend_in(layer, which[g], queries, g * block)
        current = latent if layer > 0 else x_ref
        x = jnp.concatenate([current[s] for s in source], axis=0).astype(F32)
        result = feed(x, context[...], wo[layer], wu.at[layer], wd.at[layer], gains_ref, layer)
        at = pl.ds(i * group, group)
        if last:
            early[at] = result.reshape(group, block, width)
            for copy in early_copies(i * group, group):
                copy.start()
        else:
            result = (result + virtual[0:1, :]).astype(BF16)
            latent[at] = result.reshape(group, block, width)
            wide = result.astype(F32)
            fresh = normalize(wide, gains_ref[layer + 1, 0:1, :]).astype(BF16)
            normed[layer + 1, at] = fresh.reshape(group, block, width)
            total_ref[0:1, :] = total_ref[0:1, :] + jnp.sum(wide, axis=0, keepdims=True)

    def early_step(i, carry):
        block_step(layers - 1, i)
        return carry

    def drain(layer):
        far_some(layer, 0, peers - 1, my_part).wait_send()
        sum_all(layer).wait_send()
        halo_each(lambda side, to: halo_copy(layer, side, to).wait_send())

    settled = pltpu.make_async_copy(latent, settled_out, x_sem)

    def settle(b, carry):
        latent[b] = (early[b] + virtual[0:1, :]).astype(BF16)
        return carry

    for load in loads[:3]:
        load.wait()
    gather(0)
    for load in loads[3:]:
        load.wait()
    total_ref[0:1, :] = jnp.zeros((1, width), F32)

    def sending_step(i, carry):
        block_step(0, i)

        @pl.when(i == 0)
        def _():
            halo_each(lambda side, to: stage_halo(1, side), 1)

        @pl.when(i == steps - 1)
        def _():
            halo_each(lambda side, to: stage_halo(1, side), 0)
            stage_sum(1)

        held = HALO_B * middle
        begin = jnp.maximum(i * group - held, 0)
        end = (i + 1) * group - held
        def each(k, carry):
            stage(1, order(1, k))
            return carry

        def go(k, carry):
            far_out(1, order(1, k)).start()
            return carry

        until = jnp.where(i == steps - 1, peers - 1, end)
        lax.fori_loop(begin, until, each, 0)

        @pl.when(i == 0)
        def _():
            send_halo(1, 1)

        @pl.when(i == steps - 1)
        def _():
            send_halo(1, 0)
            send_sum(1)

        lax.fori_loop(begin, until, go, 0)
        return carry

    lax.fori_loop(0, steps, sending_step, 0)
    stage_self(1)

    gather(1)
    drain(1)
    for start, count, n in ((HALO_B, blocks, 0), (near, peers * slots, 1)):
        for copy in export(start, count, n):
            copy.wait()

    @pl.when(me > 0)
    def _():
        for copy in export(0, HALO_B, 2):
            copy.wait()

    @pl.when(me < peers - 1)
    def _():
        for copy in export(HALO_B + blocks, HALO_B, 3):
            copy.wait()

    for copy in early_copies(0, blocks):
        copy.wait()
    settled.wait()


def finish_kernel(layer, near, group, table_sm, count_sm, gains_ref, virtual_ref, settled_hbm, keys_hbm, values_hbm,
                  queries_hbm, latent_hbm, wo_hbm, wu_hbm, wd_hbm, out_hbm, kept_keys, kept_values, asked, current, context,
                  kept, wo, wu, wd, todo_sm, w_sem, key_sem, value_sem, row_sem, kept_sem):
    blocks, block, width = kept.shape
    listed = table_sm.shape[1]
    head = width // HEADS
    weight_loads = [
        Parts(src.at[layer], dst, w_sem.at[n], parts)
        for n, (src, dst, parts) in enumerate(((wo_hbm, wo, 4), (wu_hbm, wu, 16), (wd_hbm, wd, 16)))
    ]
    number = jnp.int32(0)
    for b in range(blocks):
        away = jnp.int32(0)
        for j in range(listed):
            away = jnp.where((j < count_sm[b]) & (table_sm[b, j] >= near), 1, away)

        @pl.when(away > 0)
        def _(b=b, number=number):
            todo_sm[number] = b

        number = number + away

    def block_of(n):
        return todo_sm[jnp.minimum(n, number - 1)]

    def rows(n):
        which = block_of(n)
        return (
            pltpu.make_async_copy(queries_hbm.at[which], asked.at[n], row_sem.at[0, n]),
            pltpu.make_async_copy(latent_hbm.at[which], current.at[n], row_sem.at[1, n]),
        )

    def fetch(n, carry):
        which = block_of(n)
        for copy in rows(n):
            copy.start()
        for j in range(listed):
            entry = table_sm[which, j * below(j, count_sm[which])]
            pltpu.make_async_copy(keys_hbm.at[entry], kept_keys.at[n, j], key_sem.at[n]).start()
            pltpu.make_async_copy(values_hbm.at[entry], kept_values.at[n, j], value_sem.at[n]).start()
        return carry

    def fetched(n):
        for copy in rows(n):
            copy.wait()
        some = pl.ds(0, listed)
        pltpu.make_async_copy(keys_hbm.at[some], kept_keys.at[n], key_sem.at[n]).wait()
        pltpu.make_async_copy(values_hbm.at[some], kept_values.at[n], value_sem.at[n]).wait()

    load_kept = Parts(settled_hbm, kept, kept_sem, 8)
    together = context.shape[2] // block
    turns = (number + together - 1) // together

    def attend_some(i, carry):
        for g in range(together):
            pl.when(i * together + g < number)(lambda g=g: fetched(i * together + g))

        lax.fori_loop((i + 1) * together, jnp.minimum((i + 2) * together, number), fetch, 0)

        @pl.when(i == 0)
        def _():
            for load in weight_loads:
                load.start()
            load_kept.start()

        for g in range(together):
            n = i * together + g
            attend(
                count_sm[block_of(n)],
                lambda j, pair, n=n: kept_keys[n, j, :, pair],
                lambda j, pair, n=n: kept_values[n, j, pair, :],
                lambda part, n=n: asked[n, part, :],
                context.at[i],
                g * block,
                listed,
                head,
                block,
            )
        return carry

    def feed_some(i, parts):
        size = parts * together
        first = i * group
        x = current[pl.ds(first, size)].reshape(size * block, width).astype(F32)
        mixed = jnp.concatenate([context[i * (group // together) + n] for n in range(parts)], axis=1)
        result = feed(x, mixed, wo[...], wu, wd, gains_ref, layer) + virtual_ref[0:1, :]
        result = result.astype(BF16).reshape(size, block, width)
        for g in range(size):

            @pl.when(first + g < number)
            def _(g=g):
                kept[block_of(first + g)] = result[g]

    def feed_turns(i, carry):
        left = number - i * group
        if group > together:
            pl.when(left > together)(lambda: feed_some(i, group // together))
            pl.when(left <= together)(lambda: feed_some(i, 1))
        else:
            feed_some(i, 1)
        return carry

    @pl.when(number > 0)
    def _():
        lax.fori_loop(0, jnp.minimum(together, number), fetch, 0)
        lax.fori_loop(0, turns, attend_some, 0)
        for load in weight_loads:
            load.wait()
        load_kept.wait()
        lax.fori_loop(0, (number + group - 1) // group, feed_turns, 0)

    @pl.when(number == 0)
    def _():
        load_kept.start()
        load_kept.wait()

    give = Parts(kept, out_hbm, kept_sem, 8)
    give.start()
    give.wait()


def body(node_features, nbr_table, nbr_count, send_block, w_query, w_key, w_value, w_out, w_up, w_down, w_virtual, gains):
    blocks, listed = nbr_table.shape
    own, width = node_features.shape
    block = own // blocks
    peers = lax.axis_size(AXIS)
    slots = send_block.shape[1]
    layers = w_query.shape[0]
    group = math.gcd(blocks, 4)
    near = 2 * HALO_B + blocks
    entries = near + peers * slots
    shapes = (peers, layers, blocks, block, width, slots, listed, group, own * peers)
    weights = (w_query, w_key, w_value, w_out, w_up, w_down, w_virtual)
    vmem, smem, hbm = (pl.BlockSpec(memory_space=s) for s in (pltpu.VMEM, pltpu.SMEM, pl.ANY))
    dma = pltpu.SemaphoreType.DMA
    shape = jax.ShapeDtypeStruct
    scratch = [pltpu.VMEM(w.shape, BF16) for w in weights]
    scratch += [
        pltpu.VMEM((blocks, block, width), BF16),
        pltpu.VMEM((layers, blocks, block, width), BF16),
        pltpu.VMEM((blocks, block, width), BF16),
        pltpu.VMEM((entries, block, width), BF16),
        pltpu.VMEM((entries, width, block), BF16),
        pltpu.VMEM((width, group * block), BF16),
        pltpu.VMEM((layers, peers, slots * block, width), BF16),
        pltpu.VMEM((layers, peers, slots * block, width), BF16),
        pltpu.VMEM((layers, 2, HALO_B * block, width), BF16),
        pltpu.VMEM((layers, 2, HALO_B * block, width), BF16),
        pltpu.VMEM((layers, width // 128, 128), F32),
        pltpu.VMEM((layers, peers, width // 128, 128), F32),
        pltpu.VMEM((8, width), F32),
        pltpu.VMEM((blocks, block, width), F32),
        pltpu.VMEM((blocks, width, block), BF16),
        pltpu.VMEM((blocks, block, width), BF16),
        pltpu.VMEM((16, width), F32),
        pltpu.SMEM(nbr_table.shape, jnp.int32),
        pltpu.SMEM(nbr_count.shape, jnp.int32),
        pltpu.SMEM((peers * slots,), jnp.int32),
        pltpu.VMEM(gains.shape, F32),
        pltpu.SMEM((blocks,), jnp.int32),
        pltpu.SMEM((blocks,), jnp.int32),
        dma,
        dma((4,)),
        dma((len(weights),)),
        dma((layers,)),
        dma((layers, 4)),
        dma((layers, 2)),
        dma((layers, 2)),
        dma((layers,)),
        dma((layers,)),
        dma((2, 4)),
        dma((2,)),
    ]
    settled, keys, values, queries, latent, virtual = pl.pallas_call(
        functools.partial(exchange_kernel, shapes),
        out_shape=(
            shape((blocks, block, width), BF16),
            shape((entries, block, width), BF16),
            shape((entries, width, block), BF16),
            shape((blocks, width, block), BF16),
            shape((blocks, block, width), BF16),
            shape((16, width), F32),
        ),
        in_specs=[hbm] * (5 + len(weights)),
        out_specs=(hbm, hbm, hbm, hbm, hbm, vmem),
        scratch_shapes=scratch,
        compiler_params=pltpu.CompilerParams(collective_id=0, has_side_effects=True, vmem_limit_bytes=VMEM_LIMIT),
        name="exchange",
    )(nbr_table, nbr_count, send_block.reshape(-1), gains, node_features.reshape(blocks, block, width), *weights)
    result = pl.pallas_call(
        functools.partial(finish_kernel, layers - 1, near, group),
        out_shape=shape((blocks, block, width), BF16),
        in_specs=[smem, smem, vmem, vmem] + [hbm] * 8,
        out_specs=hbm,
        scratch_shapes=[
            pltpu.VMEM((blocks, listed, block, width), BF16),
            pltpu.VMEM((blocks, listed, width, block), BF16),
            pltpu.VMEM((blocks, width, block), BF16),
            pltpu.VMEM((blocks, block, width), BF16),
            pltpu.VMEM((blocks // math.gcd(group, 2), width, math.gcd(group, 2) * block), BF16),
            pltpu.VMEM((blocks, block, width), BF16),
            pltpu.VMEM(w_out.shape[1:], BF16),
            pltpu.VMEM(w_up.shape[1:], BF16),
            pltpu.VMEM(w_down.shape[1:], BF16),
            pltpu.SMEM((blocks,), jnp.int32),
            dma((3,)),
            dma((blocks,)),
            dma((blocks,)),
            dma((2, blocks)),
            dma,
        ],
        compiler_params=pltpu.CompilerParams(vmem_limit_bytes=VMEM_LIMIT),
        name="finish",
    )(nbr_table, nbr_count, gains, virtual, settled, keys, values, queries, latent, w_out, w_up, w_down)
    return result.reshape(own, width)


def solution(mesh):
    across = P(("members", "row"), None)
    in_specs = (across, P("row", None), P("row"), P("row", None)) + (P(),) * 8
    return jax.shard_map(body, mesh=mesh, in_specs=in_specs, out_specs=across, check_vma=False)
```

```python
import functools
import math

import jax
import jax.numpy as jnp
from jax import lax
from jax.experimental import pallas as pl
from jax.experimental.pallas import tpu as pltpu
from jax.sharding import PartitionSpec as P

HEADS = 4
HALO_B = 2
VMEM_LIMIT = 67_000_000
MESH = pl.DeviceIdType.MESH
BF16 = jnp.bfloat16
F32 = jnp.float32
AXIS = "row"


def normalize(values, scaling):
    centred = values - jnp.mean(values, axis=-1, keepdims=True)
    spread = jnp.mean(centred * centred, axis=-1, keepdims=True)
    return centred * lax.rsqrt(spread + 1e-05) * scaling


def dot(a, b, contract=((1,), (0,))):
    return lax.dot_general(a, b, (contract, ((), ())), preferred_element_type=F32)


def gelu(x):
    return 0.5 * x * (1.0 + jnp.tanh(math.sqrt(2 / math.pi) * (x + 0.044715 * x * x * x)))


def flip(a, b, bits):
    out = 0
    for bit in range(bits):
        weight = 1 << bit
        x = lax.rem(lax.div(a, jnp.int32(weight)), jnp.int32(2))
        y = lax.rem(lax.div(b, jnp.int32(weight)), jnp.int32(2))
        out = out + weight * lax.rem(x + y, jnp.int32(2))
    return out


def below(a, b):
    return jnp.minimum(jnp.maximum(b - a, 0), 1)


def equal(a, b):
    return 1 - jnp.minimum(jnp.maximum(a - b, b - a), 1)


def attend(count, key_of, value_of, query_of, context, at, listed, head, block):
    scale = math.log2(math.e) / math.sqrt(head)
    dead = [(1 - below(j, count)).astype(F32) * -1e30 for j in range(listed)]
    blank = jnp.zeros((head, block), BF16)
    for h in range(0, HEADS, 2):
        pair = slice(h * head, (h + 2) * head)
        upper = query_of(slice(h * head, (h + 1) * head))
        lower = query_of(slice((h + 1) * head, (h + 2) * head))
        both = jnp.concatenate(
            [jnp.concatenate([upper, blank], axis=1), jnp.concatenate([blank, lower], axis=1)], axis=0
        )
        scores = []
        for j in range(listed):
            s = dot(key_of(j, pair), both)
            scores.append(s if 2 * j < listed else s + dead[j])
        top = jnp.max(functools.reduce(jnp.maximum, scores), axis=0, keepdims=True)
        weights = [jnp.exp2((s - top) * scale) for s in scores]
        inverse = 1.0 / jnp.sum(functools.reduce(jnp.add, weights), axis=0, keepdims=True)
        probs = jnp.concatenate([w.astype(BF16) for w in weights], axis=0)
        mixed = dot(jnp.concatenate([value_of(j, pair) for j in range(listed)], axis=1), probs)
        for n in range(2):
            part = slice(n * block, (n + 1) * block)
            of_head = slice((h + n) * head, (h + n + 1) * head)
            context[of_head, at : at + block] = (mixed[n * head : (n + 1) * head, part] * inverse[:, part]).astype(BF16)


def feed(x, context, wo, wu, wd, gains_ref, layer):
    after_att = x + normalize(dot(context, wo, ((0,), (0,))), gains_ref[layer, 1:2, :])
    middle = normalize(after_att, gains_ref[layer, 2:3, :]).astype(BF16)
    hidden_size = wu.shape[-1]
    part = math.gcd(hidden_size, 512)
    down = None
    for f in range(0, hidden_size, part):
        hidden = gelu(dot(middle, wu[:, f : f + part])).astype(BF16)
        term = dot(hidden, wd[f : f + part, :])
        down = term if down is None else down + term
    return after_att + normalize(down, gains_ref[layer, 3:4, :])


class Parts:
    def __init__(self, src, dst, sem, parts):
        self.whole = pltpu.make_async_copy(src, dst, sem)
        size = dst.shape[0] // math.gcd(dst.shape[0], parts)
        slices = [pl.ds(start, size) for start in range(0, dst.shape[0], size)]
        self.pieces = [pltpu.make_async_copy(src.at[part], dst.at[part], sem) for part in slices]

    def start(self):
        for piece in self.pieces:
            piece.start()

    def wait(self):
        self.whole.wait()


def exchange_kernel(shapes, table_hbm, count_hbm, send_hbm, gains_hbm, x_hbm, wq_hbm, wk_hbm, wv_hbm, wo_hbm, wu_hbm,
                    wd_hbm, wm_hbm, settled_out, keys_out, values_out, queries_out, latent_out, virtual_ref, wq, wk, wv,
                    wo, wu, wd, wm, x_ref, normed, latent, keys, values, context, send_buf, far, halo_send, halo,
                    sum_send, sums, total_ref, early, asked, arranged, virtual, table_sm, count_sm, send_sm,
                    gains_ref, perm_sm, pos_sm, x_sem, small_sem, w_sem, far_send,
                    far_recv, halo_ssem, halo_rsem, sum_ssem, sum_rsem, table_sem, early_sem):
    peers, layers, blocks, block, width, slots, listed, group, node_total = shapes
    near = 2 * HALO_B + blocks
    bits = peers.bit_length() - 1
    half, quarter = peers // 2, peers // 4
    rows = group * block
    steps = blocks // group
    head = width // HEADS
    me = lax.axis_index(AXIS)
    inner = jnp.where((me >= quarter) & (me < half + quarter), 1, 0)

    def order(layer, k):
        outer = jnp.where(k < half, half + k, peers - 1 - k)
        lead = quarter // 2 if layer == 0 else quarter
        late = k - lead
        inside = jnp.where(
            late < 0, peers - 1 - k, jnp.where(late < half - 1, half - 1 - late, peers - 1 - lead - (late - half + 1))
        )
        return flip(me, jnp.where(inner == 1, inside, outer), bits)

    def remote(src, dst, ssem, rsem, to):
        return pltpu.make_async_remote_copy(
            src_ref=src, dst_ref=dst, send_sem=ssem, recv_sem=rsem, device_id={AXIS: to}, device_id_type=MESH
        )

    my_part = lax.div(me, jnp.int32(quarter))

    def far_out(layer, to):
        return remote(send_buf.at[layer, to], far.at[layer, me], far_send.at[layer], far_recv.at[layer, my_part], to)

    def far_some(layer, start, count, part):
        some = pl.ds(start, count)
        return remote(send_buf.at[layer, some], far.at[layer, some], far_send.at[layer], far_recv.at[layer, part], me)

    def sum_out(layer, to):
        return remote(sum_send.at[layer], sums.at[layer, me], sum_ssem.at[layer], sum_rsem.at[layer], to)

    def sum_all(layer):
        some = sums.at[layer, pl.ds(0, peers - 1)]
        return remote(some, some, sum_ssem.at[layer], sum_rsem.at[layer], me)

    def halo_copy(layer, side, to):
        return remote(
            halo_send.at[layer, side], halo.at[layer, 1 - side], halo_ssem.at[layer, side], halo_rsem.at[layer, 1 - side], to
        )

    middle_side = [jnp.where(me == half, 1, 0), jnp.where(me == half - 1, 1, 0)]
    middle = middle_side[0] + middle_side[1]

    def halo_each(act, across=None):
        for side in range(2):
            there = me > 0 if side == 0 else me < peers - 1
            if across is not None:
                there = there & (middle_side[side] == across)

            @pl.when(there)
            def _(side=side):
                act(side, me - 1 if side == 0 else me + 1)

    load_x = Parts(x_hbm, x_ref, x_sem, 8)
    load_x.start()
    smalls = [
        pltpu.make_async_copy(src, dst, small_sem.at[n])
        for n, (src, dst) in enumerate(
            ((gains_hbm, gains_ref), (send_hbm, send_sm), (table_hbm, table_sm), (count_hbm, count_sm))
        )
    ]
    for small in smalls:
        small.start()
    barrier = pltpu.get_barrier_semaphore()

    def greet(k, carry):
        pl.semaphore_signal(barrier, inc=1, device_id={AXIS: lax.rem(me + k, peers)}, device_id_type=MESH)
        return carry

    lax.fori_loop(1, peers, greet, 0)
    loads = []
    for n, (src, dst) in enumerate(
        ((wk_hbm, wk), (wv_hbm, wv), (wm_hbm, wm), (wq_hbm, wq), (wo_hbm, wo), (wu_hbm, wu), (wd_hbm, wd))
    ):
        loads.append(pltpu.make_async_copy(src, dst, w_sem.at[n]))
    total_ref[0:1, :] = jnp.zeros((1, width), F32)
    load_x.wait()
    for small in smalls:
        small.wait()
    for load in loads:
        load.start()

    def first(i, carry):
        x = x_ref[pl.ds(i * group, group)].reshape(rows, width).astype(F32)
        total_ref[0:1, :] = total_ref[0:1, :] + jnp.sum(x, axis=0, keepdims=True)
        fresh = normalize(x, gains_ref[0, 0:1, :]).astype(BF16)
        normed[0, pl.ds(i * group, group)] = fresh.reshape(group, block, width)
        return carry

    lax.fori_loop(0, steps, first, 0)

    def stage(layer, to):
        for slot in range(slots):
            at = send_sm[to * slots + slot]
            if layer > 0:
                at = pos_sm[at]
            send_buf[layer, to, pl.ds(slot * block, block), :] = normed[layer, at]

    def stage_self(layer):
        for slot in range(slots):
            at = send_sm[me * slots + slot]
            if layer > 0:
                at = pos_sm[at]
            far[layer, me, pl.ds(slot * block, block), :] = normed[layer, at]

    def stage_halo(layer, side):
        for b in range(HALO_B):
            at = b if side == 0 else blocks - HALO_B + b
            if layer > 0:
                at = pos_sm[at]
            halo_send[layer, side, pl.ds(b * block, block), :] = normed[layer, at]

    def send_halo(layer, across=None):
        halo_each(lambda side, to: halo_copy(layer, side, to).start(), across)

    def stage_sum(layer):
        for k in range(width // 128):
            part = total_ref[0:1, k * 128 : (k + 1) * 128]
            sum_send[layer, k : k + 1, :] = part
            sums[layer, me, k : k + 1, :] = part

    def send_sum(layer):
        def one(k, carry):
            sum_out(layer, lax.rem(me + k, peers)).start()
            return carry

        lax.fori_loop(1, peers, one, 0)

    def stage_all(k, carry):
        stage(0, order(0, k))
        return carry

    def send_all(k, carry):
        far_out(0, order(0, k)).start()
        return carry

    stage_sum(0)
    halo_each(lambda side, to: stage_halo(0, side))
    lax.fori_loop(0, peers - 1, stage_all, 0)
    pl.semaphore_wait(barrier, peers - 1)
    send_halo(0)
    send_sum(0)
    lax.fori_loop(0, peers - 1, send_all, 0)
    stage_self(0)

    uses = [jnp.int32(peers * slots + n) for n in range(blocks)]
    for k in range(peers - 2, -1, -1):
        to = order(1, jnp.int32(k))
        for slot in range(slots - 1, -1, -1):
            b = send_sm[to * slots + slot]
            uses = [use + equal(b, n) * (k * slots + slot - use) for n, use in enumerate(uses)]
    for n in range(HALO_B):
        low, high = n, blocks - HALO_B + n
        uses[low] = uses[low] - middle_side[0] * 2 * peers * slots
        uses[high] = uses[high] - middle_side[1] * 2 * peers * slots
    places = []
    for n in range(blocks):
        place = jnp.int32(0)
        for other in range(blocks):
            if other != n:
                place = place + below(uses[other], uses[n])
        places.append(place)
        pos_sm[n] = place
    for n in range(blocks):
        which = jnp.int32(0)
        for b in range(blocks):
            which = which + equal(places[b], n) * b
        perm_sm[n] = which
    def project(layer, piece, at):
        count = piece.shape[0]
        flat = piece.reshape(count * block, width)
        keys[pl.ds(at, count)] = dot(flat, wk[layer]).astype(BF16).reshape(count, block, width)
        turned = dot(wv[layer], flat, ((0,), (1,))).astype(BF16)
        for n in range(count):
            values[at + n] = turned[:, n * block : (n + 1) * block]

    def export(at, count, n):
        part = pl.ds(at, count)
        return (
            pltpu.make_async_copy(keys.at[part], keys_out.at[part], table_sem.at[0, n]),
            pltpu.make_async_copy(values.at[part], values_out.at[part], table_sem.at[1, n]),
        )

    chunk = math.gcd(blocks, 4)
    many = math.gcd(quarter, 4)

    def hand_on(layer, at, count, n):
        if layer == layers - 1:
            for copy in export(at, count, n):
                copy.start()

    def gather(layer):
        def own_piece(i, carry):
            if layer == 0:
                piece = normed[layer, pl.ds(i * chunk, chunk)]
            else:
                piece = jnp.concatenate([normed[layer, pos_sm[i * chunk + n]] for n in range(chunk)], axis=0)
                piece = piece.reshape(chunk, block, width)
            project(layer, piece, HALO_B + i * chunk)
            hand_on(layer, HALO_B + i * chunk, chunk, 0)
            return carry

        lax.fori_loop(0, blocks // chunk, own_piece, 0)

        def halo_in(copy, side):
            copy.wait_recv()
            at = 0 if side == 0 else HALO_B + blocks
            project(layer, halo[layer, side].reshape(HALO_B, block, width), at)
            hand_on(layer, at, HALO_B, 2 + side)

        @pl.when(me > 0)
        def _():
            halo_in(halo_copy(layer, 1, me - 1), 0)

        @pl.when(me < peers - 1)
        def _():
            halo_in(halo_copy(layer, 0, me + 1), 1)

        if layer == layers - 1:
            lax.fori_loop(0, steps, early_step, 0)
            drain(0)
        for n, (inside, outside) in enumerate(((2, 0), (0, 1), (1, 3), (3, 2))):
            if n == 3:
                sum_all(layer).wait_recv()
                whole = jnp.sum(sums[layer], axis=0)
                mean = jnp.concatenate([whole[k : k + 1, :] for k in range(width // 128)], axis=1) / node_total
                mean = jnp.broadcast_to(mean, (16, width)).astype(BF16)
                virtual[...] = dot(mean, wm[layer])
                if layer == layers - 1:
                    virtual_ref[...] = virtual[...]
                    lax.fori_loop(0, blocks, settle, 0)
                    settled.start()
            part = flip(my_part, jnp.where(inner == 1, inside, outside), 2)
            start = part * quarter

            @pl.when(part == my_part)
            def _(part=part, start=start):
                far_some(layer, start, quarter - 1, part).wait_recv()

            @pl.when(part != my_part)
            def _(part=part, start=start):
                far_some(layer, start, quarter, part).wait_recv()

            def far_piece(i, carry, start=start):
                source = start + i * many
                piece = far[layer, pl.ds(source, many)].reshape(many * slots, block, width)
                project(layer, piece, near + source * slots)
                hand_on(layer, near + source * slots, many * slots, 1)
                return carry

            lax.fori_loop(0, quarter // many, far_piece, 0)

    def attend_in(layer, which, queries, at):
        count = count_sm[which]
        home = table_sm[which, 0]
        spots = []
        for j in range(listed):
            entry = table_sm[which, j]
            if 2 * j >= listed:
                entry = home + below(j, count) * (entry - home)
            spots.append(entry)
        attend(
            count,
            lambda j, pair: keys[spots[j], :, pair],
            lambda j, pair: values[spots[j], pair],
            lambda part: queries[part, at : at + block],
            context,
            at,
            listed,
            head,
            block,
        )

    def early_copies(start, count):
        at = pl.ds(start, count)
        return (
            pltpu.make_async_copy(asked.at[at], queries_out.at[at], early_sem.at[0]),
            pltpu.make_async_copy(arranged.at[at], latent_out.at[at], early_sem.at[1]),
        )

    def block_step(layer, i):
        last = layer == layers - 1
        order_at = [i * group + g for g in range(group)]
        if last:
            which = order_at
            source = [pos_sm[w] for w in which]
            for w, s in zip(which, source):
                arranged[w] = latent[s]
        else:
            which = [perm_sm[n] for n in order_at]
            source = which
        mine = jnp.concatenate([normed[layer, s] for s in source], axis=0)
        queries = dot(wq[layer], mine, ((0,), (1,))).astype(BF16)
        if last:
            for g in range(group):
                asked[which[g]] = queries[:, g * block : (g + 1) * block]
        for g in range(group):
            attend_in(layer, which[g], queries, g * block)
        current = latent if layer > 0 else x_ref
        x = jnp.concatenate([current[s] for s in source], axis=0).astype(F32)
        result = feed(x, context[...], wo[layer], wu.at[layer], wd.at[layer], gains_ref, layer)
        at = pl.ds(i * group, group)
        if last:
            early[at] = result.reshape(group, block, width)
            for copy in early_copies(i * group, group):
                copy.start()
        else:
            result = (result + virtual[0:1, :]).astype(BF16)
            latent[at] = result.reshape(group, block, width)
            wide = result.astype(F32)
            fresh = normalize(wide, gains_ref[layer + 1, 0:1, :]).astype(BF16)
            normed[layer + 1, at] = fresh.reshape(group, block, width)
            total_ref[0:1, :] = total_ref[0:1, :] + jnp.sum(wide, axis=0, keepdims=True)

    def early_step(i, carry):
        block_step(layers - 1, i)
        return carry

    def drain(layer):
        far_some(layer, 0, peers - 1, my_part).wait_send()
        sum_all(layer).wait_send()
        halo_each(lambda side, to: halo_copy(layer, side, to).wait_send())

    settled = pltpu.make_async_copy(latent, settled_out, x_sem)

    def settle(b, carry):
        latent[b] = (early[b] + virtual[0:1, :]).astype(BF16)
        return carry

    for load in loads[:3]:
        load.wait()
    gather(0)
    for load in loads[3:]:
        load.wait()
    total_ref[0:1, :] = jnp.zeros((1, width), F32)

    def sending_step(i, carry):
        block_step(0, i)

        @pl.when(i == 0)
        def _():
            halo_each(lambda side, to: stage_halo(1, side), 1)

        @pl.when(i == steps - 1)
        def _():
            halo_each(lambda side, to: stage_halo(1, side), 0)
            stage_sum(1)

        held = HALO_B * middle
        begin = jnp.maximum(i * group - held, 0)
        end = (i + 1) * group - held
        def each(k, carry):
            stage(1, order(1, k))
            return carry

        def go(k, carry):
            far_out(1, order(1, k)).start()
            return carry

        until = jnp.where(i == steps - 1, peers - 1, end)
        lax.fori_loop(begin, until, each, 0)

        @pl.when(i == 0)
        def _():
            send_halo(1, 1)

        @pl.when(i == steps - 1)
        def _():
            send_halo(1, 0)
            send_sum(1)

        lax.fori_loop(begin, until, go, 0)
        return carry

    lax.fori_loop(0, steps, sending_step, 0)
    stage_self(1)

    gather(1)
    drain(1)
    for start, count, n in ((HALO_B, blocks, 0), (near, peers * slots, 1)):
        for copy in export(start, count, n):
            copy.wait()

    @pl.when(me > 0)
    def _():
        for copy in export(0, HALO_B, 2):
            copy.wait()

    @pl.when(me < peers - 1)
    def _():
        for copy in export(HALO_B + blocks, HALO_B, 3):
            copy.wait()

    for copy in early_copies(0, blocks):
        copy.wait()
    settled.wait()


def finish_kernel(layer, near, group, table_sm, count_sm, gains_ref, virtual_ref, settled_hbm, keys_hbm, values_hbm,
                  queries_hbm, latent_hbm, wo_hbm, wu_hbm, wd_hbm, out_hbm, kept_keys, kept_values, asked, current, context,
                  kept, wo, wu, wd, todo_sm, w_sem, key_sem, value_sem, row_sem, kept_sem):
    blocks, block, width = kept.shape
    listed = table_sm.shape[1]
    head = width // HEADS
    weight_loads = [
        Parts(src.at[layer], dst, w_sem.at[n], parts)
        for n, (src, dst, parts) in enumerate(((wo_hbm, wo, 4), (wu_hbm, wu, 16), (wd_hbm, wd, 16)))
    ]
    number = jnp.int32(0)
    for b in range(blocks):
        away = jnp.int32(0)
        for j in range(listed):
            away = jnp.where((j < count_sm[b]) & (table_sm[b, j] >= near), 1, away)

        @pl.when(away > 0)
        def _(b=b, number=number):
            todo_sm[number] = b

        number = number + away

    def block_of(n):
        return todo_sm[jnp.minimum(n, number - 1)]

    def rows(n):
        which = block_of(n)
        return (
            pltpu.make_async_copy(queries_hbm.at[which], asked.at[n], row_sem.at[0, n]),
            pltpu.make_async_copy(latent_hbm.at[which], current.at[n], row_sem.at[1, n]),
        )

    def fetch(n, carry):
        which = block_of(n)
        for copy in rows(n):
            copy.start()
        for j in range(listed):
            entry = table_sm[which, j * below(j, count_sm[which])]
            pltpu.make_async_copy(keys_hbm.at[entry], kept_keys.at[n, j], key_sem.at[n]).start()
            pltpu.make_async_copy(values_hbm.at[entry], kept_values.at[n, j], value_sem.at[n]).start()
        return carry

    def fetched(n):
        for copy in rows(n):
            copy.wait()
        some = pl.ds(0, listed)
        pltpu.make_async_copy(keys_hbm.at[some], kept_keys.at[n], key_sem.at[n]).wait()
        pltpu.make_async_copy(values_hbm.at[some], kept_values.at[n], value_sem.at[n]).wait()

    load_kept = Parts(settled_hbm, kept, kept_sem, 8)
    together = context.shape[2] // block
    turns = (number + together - 1) // together

    def attend_some(i, carry):
        for g in range(together):
            pl.when(i * together + g < number)(lambda g=g: fetched(i * together + g))

        lax.fori_loop((i + 1) * together, jnp.minimum((i + 2) * together, number), fetch, 0)

        @pl.when(i == jnp.minimum(1, turns - 1))
        def _():
            for load in weight_loads:
                load.start()
            load_kept.start()

        for g in range(together):
            n = i * together + g
            attend(
                count_sm[block_of(n)],
                lambda j, pair, n=n: kept_keys[n, j, :, pair],
                lambda j, pair, n=n: kept_values[n, j, pair, :],
                lambda part, n=n: asked[n, part, :],
                context.at[i],
                g * block,
                listed,
                head,
                block,
            )
        return carry

    def feed_some(i, parts):
        size = parts * together
        first = i * group
        x = current[pl.ds(first, size)].reshape(size * block, width).astype(F32)
        mixed = jnp.concatenate([context[i * (group // together) + n] for n in range(parts)], axis=1)
        result = feed(x, mixed, wo[...], wu, wd, gains_ref, layer) + virtual_ref[0:1, :]
        result = result.astype(BF16).reshape(size, block, width)
        for g in range(size):

            @pl.when(first + g < number)
            def _(g=g):
                kept[block_of(first + g)] = result[g]

    def feed_turns(i, carry):
        left = number - i * group
        if group > together:
            pl.when(left > together)(lambda: feed_some(i, group // together))
            pl.when(left <= together)(lambda: feed_some(i, 1))
        else:
            feed_some(i, 1)
        return carry

    @pl.when(number > 0)
    def _():
        lax.fori_loop(0, jnp.minimum(together, number), fetch, 0)
        lax.fori_loop(0, turns, attend_some, 0)
        for load in weight_loads:
            load.wait()
        load_kept.wait()
        lax.fori_loop(0, (number + group - 1) // group, feed_turns, 0)

    @pl.when(number == 0)
    def _():
        load_kept.start()
        load_kept.wait()

    give = Parts(kept, out_hbm, kept_sem, 8)
    give.start()
    give.wait()


def body(node_features, nbr_table, nbr_count, send_block, w_query, w_key, w_value, w_out, w_up, w_down, w_virtual, gains):
    blocks, listed = nbr_table.shape
    own, width = node_features.shape
    block = own // blocks
    peers = lax.axis_size(AXIS)
    slots = send_block.shape[1]
    layers = w_query.shape[0]
    group = math.gcd(blocks, 4)
    near = 2 * HALO_B + blocks
    entries = near + peers * slots
    shapes = (peers, layers, blocks, block, width, slots, listed, group, own * peers)
    weights = (w_query, w_key, w_value, w_out, w_up, w_down, w_virtual)
    vmem, smem, hbm = (pl.BlockSpec(memory_space=s) for s in (pltpu.VMEM, pltpu.SMEM, pl.ANY))
    dma = pltpu.SemaphoreType.DMA
    shape = jax.ShapeDtypeStruct
    scratch = [pltpu.VMEM(w.shape, BF16) for w in weights]
    scratch += [
        pltpu.VMEM((blocks, block, width), BF16),
        pltpu.VMEM((layers, blocks, block, width), BF16),
        pltpu.VMEM((blocks, block, width), BF16),
        pltpu.VMEM((entries, block, width), BF16),
        pltpu.VMEM((entries, width, block), BF16),
        pltpu.VMEM((width, group * block), BF16),
        pltpu.VMEM((layers, peers, slots * block, width), BF16),
        pltpu.VMEM((layers, peers, slots * block, width), BF16),
        pltpu.VMEM((layers, 2, HALO_B * block, width), BF16),
        pltpu.VMEM((layers, 2, HALO_B * block, width), BF16),
        pltpu.VMEM((layers, width // 128, 128), F32),
        pltpu.VMEM((layers, peers, width // 128, 128), F32),
        pltpu.VMEM((8, width), F32),
        pltpu.VMEM((blocks, block, width), F32),
        pltpu.VMEM((blocks, width, block), BF16),
        pltpu.VMEM((blocks, block, width), BF16),
        pltpu.VMEM((16, width), F32),
        pltpu.SMEM(nbr_table.shape, jnp.int32),
        pltpu.SMEM(nbr_count.shape, jnp.int32),
        pltpu.SMEM((peers * slots,), jnp.int32),
        pltpu.VMEM(gains.shape, F32),
        pltpu.SMEM((blocks,), jnp.int32),
        pltpu.SMEM((blocks,), jnp.int32),
        dma,
        dma((4,)),
        dma((len(weights),)),
        dma((layers,)),
        dma((layers, 4)),
        dma((layers, 2)),
        dma((layers, 2)),
        dma((layers,)),
        dma((layers,)),
        dma((2, 4)),
        dma((2,)),
    ]
    settled, keys, values, queries, latent, virtual = pl.pallas_call(
        functools.partial(exchange_kernel, shapes),
        out_shape=(
            shape((blocks, block, width), BF16),
            shape((entries, block, width), BF16),
            shape((entries, width, block), BF16),
            shape((blocks, width, block), BF16),
            shape((blocks, block, width), BF16),
            shape((16, width), F32),
        ),
        in_specs=[hbm] * (5 + len(weights)),
        out_specs=(hbm, hbm, hbm, hbm, hbm, vmem),
        scratch_shapes=scratch,
        compiler_params=pltpu.CompilerParams(collective_id=0, has_side_effects=True, vmem_limit_bytes=VMEM_LIMIT),
        name="exchange",
    )(nbr_table, nbr_count, send_block.reshape(-1), gains, node_features.reshape(blocks, block, width), *weights)
    result = pl.pallas_call(
        functools.partial(finish_kernel, layers - 1, near, group),
        out_shape=shape((blocks, block, width), BF16),
        in_specs=[smem, smem, vmem, vmem] + [hbm] * 8,
        out_specs=hbm,
        scratch_shapes=[
            pltpu.VMEM((blocks, listed, block, width), BF16),
            pltpu.VMEM((blocks, listed, width, block), BF16),
            pltpu.VMEM((blocks, width, block), BF16),
            pltpu.VMEM((blocks, block, width), BF16),
            pltpu.VMEM((blocks // math.gcd(group, 2), width, math.gcd(group, 2) * block), BF16),
            pltpu.VMEM((blocks, block, width), BF16),
            pltpu.VMEM(w_out.shape[1:], BF16),
            pltpu.VMEM(w_up.shape[1:], BF16),
            pltpu.VMEM(w_down.shape[1:], BF16),
            pltpu.SMEM((blocks,), jnp.int32),
            dma((3,)),
            dma((blocks,)),
            dma((blocks,)),
            dma((2, blocks)),
            dma,
        ],
        compiler_params=pltpu.CompilerParams(vmem_limit_bytes=VMEM_LIMIT),
        name="finish",
    )(nbr_table, nbr_count, gains, virtual, settled, keys, values, queries, latent, w_out, w_up, w_down)
    return result.reshape(own, width)


def solution(mesh):
    across = P(("members", "row"), None)
    in_specs = (across, P("row", None), P("row"), P("row", None)) + (P(),) * 8
    return jax.shard_map(body, mesh=mesh, in_specs=in_specs, out_specs=across, check_vma=False)
```
